128 devices in a mesh: tm: 32 (over y, x, core), state: 4 (over z).
Axes of the slice: x: 4, y: 4, z: 4, core: 2. Of those that a mesh axis runs over, the one named last changes fastest.
Arguments:
- filtered_cov: float32 [128, 512, 512], P('tm', 'state'), may hold values from -4 to 5, as said below
- filtered_mean: float32 [128, 512], P('tm'), may hold values from -6 to 6
- noise_var: float32 [512], replicated, may hold values from 0.00390625 to 0.2
- trans_blocks: float32 [4, 2, 128, 128], replicated, may hold values from -1 to 2
- pattern: int32 [4, 2], replicated, may hold values from 0 to 3, as said below
Outputs:
- smooth_mean: float32 [128, 512], P('tm', 'state')
- smooth_cov: float32 [128, 512, 512], P('tm', 'state')
The draws below stay inside these ranges and needn't reach their ends.
Inputs may be any that keep to these rules, and one draw needn't show every extreme that they name: `filtered_cov`: each matrix is symmetric, and every eigenvalue is at least 0.5. `pattern`: block row r names 2 different column blocks; slot 0 names r itself.
All inputs are finite; a program needn't handle non-finite values.
Results may differ from the reference program's by a relative error of at most 0.0003.
Values sent between devices are 32-bit elements; how exact they have to be, the bound alone decides.
A program may use at most 192 MiB of HBM per device.

```python
import math
import jax
import jax.numpy as jnp
from jax import lax

NS = 512
BLK = 128
NNZ = 2
NB = 4
TIME = 128


def draw_filtered_cov(key, part):
    key_factor = jax.random.fold_in(key, 0)
    key_diag = jax.random.fold_in(key, 1)
    key_dir = jax.random.fold_in(key, 3)
    key_lift = jax.random.fold_in(key, 4)
    bound_value = math.sqrt(3.0)
    factor = jax.random.uniform(key_factor, (TIME, NS, NS), jnp.float32, -bound_value, bound_value)
    product = jnp.einsum('tik,tjk->tij', factor, factor, precision=lax.Precision.HIGHEST) / NS
    symmetric = (product + jnp.swapaxes(product, 1, 2)) * 0.5
    diagonal = jax.random.uniform(key_diag, (TIME, NS), jnp.float32, 0.5, 1.0)
    signs = jax.random.rademacher(key_dir, (TIME, NS), jnp.int32).astype(jnp.float32)
    unit_dir = signs / math.sqrt(NS)
    lift = jax.random.uniform(key_lift, (TIME,), jnp.float32, 15.0, 40.0)
    lifted = lift[:, None, None] * unit_dir[:, :, None] * unit_dir[:, None, :]
    return symmetric + lifted + jnp.eye(NS, dtype=jnp.float32)[None] * diagonal[:, None, :]


def draw_trans_blocks(key, part):
    key_off, key_diag = jax.random.split(jax.random.fold_in(key, 7))
    half_width = 0.8 / (TIME * math.sqrt(NNZ * BLK))
    off_part = jax.random.uniform(key_off, (NB, NNZ, BLK, BLK), jnp.float32, -half_width, half_width)
    diag_rates = 1.0 + (1.0 + jax.random.uniform(key_diag, (NB, BLK), jnp.float32, 0.0, 0.5)) / TIME
    slot_mask = (jnp.arange(NNZ) == 0).astype(jnp.float32)
    diag_part = jnp.eye(BLK, dtype=jnp.float32)[None, None] * diag_rates[:, None, None, :] * slot_mask[None, :, None, None]
    return off_part + diag_part


def draw_pattern(key, part):
    row_keys = jax.random.split(jax.random.fold_in(key, 11), NB)
    shuffled = jax.vmap(lambda row_key: jax.random.permutation(row_key, NB - 1))(row_keys)
    row_index = jnp.arange(NB, dtype=jnp.int32)[:, None]
    others = (row_index + 1 + shuffled[:, :NNZ - 1].astype(jnp.int32)) % NB
    return jnp.concatenate([row_index, others], axis=1).astype(jnp.int32)


def steps_of(stream_key, dims, shards, low, top_value):
    loudness = 1.0
    for position, blocks in shards:
        steps = jax.random.uniform(jax.random.fold_in(jax.random.fold_in(stream_key, 6), position), (blocks,), jnp.float32, low / len(shards), top_value / len(shards))
        loudness = loudness * jnp.repeat(jnp.exp(steps), dims[position] // blocks).reshape((-1,) + (1,) * (len(dims) - 1 - position))
    return loudness


def noise(key, shape, scale, limit, pieces=(), held_as=jnp.bfloat16):
    entries = scale * jax.random.normal(key, shape, jnp.float32)
    if pieces:
        entries = entries * steps_of(key, shape, pieces, -0.22, 0.18)
    return jnp.clip(entries, -limit, limit).astype(held_as)


def setup_inputs(seed: int = 0) -> dict:
    key_of = jax.random.split(jax.random.key(seed), 6)
    return {
        "filtered_cov": draw_filtered_cov(jax.random.fold_in(key_of[5], 71), 0),
        "filtered_mean": noise(key_of[1], (TIME, NS), 1.0, 6.0, ((0, 32),), jnp.float32),
        "noise_var": jnp.clip(jnp.exp(jax.random.uniform(key_of[2], (NS,), jnp.float32, math.log(0.00390625), math.log(0.2))), 0.00390625, 0.2),
        "trans_blocks": draw_trans_blocks(jax.random.fold_in(key_of[5], 71), 0),
        "pattern": draw_pattern(jax.random.fold_in(key_of[5], 71), 0),
    }


highest = lax.Precision.HIGHEST

def left_apply(blocks, pattern, matrix):
    block_count = blocks.shape[0]
    block_size = blocks.shape[2]
    tile_rows = matrix.reshape(block_count, block_size, matrix.shape[-1])
    picked = tile_rows[pattern]
    result = jnp.einsum('rjab,rjbk->rak', blocks, picked, precision=highest)
    return result.reshape(matrix.shape[0], matrix.shape[-1])

def right_apply(blocks, pattern, matrix):
    block_count = blocks.shape[0]
    block_size = blocks.shape[2]
    tile_cols = matrix.reshape(matrix.shape[0], block_count, block_size)
    picked = tile_cols[:, pattern]
    result = jnp.einsum('krjb,rjab->kra', picked, blocks, precision=highest)
    return result.reshape(matrix.shape[0], matrix.shape[1])

def reference(filtered_cov, filtered_mean, noise_var, trans_blocks, pattern):
    time_steps = filtered_mean.shape[0]

    def backward(state_carry, inputs):
        cov_mat, mean_vec, moment = inputs
        next_mean, next_cov = state_carry
        left_prod = left_apply(trans_blocks, pattern, cov_mat)
        predicted = right_apply(trans_blocks, pattern, left_prod) + jnp.diag(noise_var)
        factor = jnp.linalg.cholesky(predicted)
        solved = jax.scipy.linalg.cho_solve((factor, True), left_prod)
        keep_flag = (moment != time_steps - 1).astype(filtered_cov.dtype)
        gain_mat = solved.T * keep_flag
        pushed = left_apply(trans_blocks, pattern, mean_vec[:, None])[:, 0]
        offset = mean_vec - jnp.dot(gain_mat, pushed, precision=highest)
        spread = cov_mat - jnp.dot(gain_mat, left_prod, precision=highest)
        smooth_mean = jnp.dot(gain_mat, next_mean, precision=highest) + offset
        weighted = jnp.dot(gain_mat, next_cov, precision=highest)
        smooth_cov = jnp.dot(weighted, gain_mat.T, precision=highest) + spread
        return ((smooth_mean, smooth_cov), (smooth_mean, smooth_cov))
    start_state = (jnp.zeros_like(filtered_mean[0]), jnp.zeros_like(filtered_cov[0]))
    moments = jnp.arange(time_steps, dtype=jnp.int32)
    final_state, outputs = lax.scan(backward, start_state, (filtered_cov, filtered_mean, moments), reverse=True)
    return (outputs[0], outputs[1])
```

```python
from functools import partial

import jax
import jax.numpy as jnp
from jax import lax
from jax.experimental import pallas as pl
from jax.experimental.pallas import tpu as pltpu
from jax.sharding import Mesh
from jax.sharding import PartitionSpec as P

N = 512
B = 128
LROW = 512
GROW = 832
ROWS = 896
HALF = ROWS // 2
SH = ROWS // 8
MESH = pl.DeviceIdType.MESH
F32 = jnp.float32
BF16 = jnp.bfloat16
ANY = pl.BlockSpec(memory_space=pl.ANY)
VM = pl.BlockSpec(memory_space=pltpu.VMEM)
SM = pl.BlockSpec(memory_space=pltpu.SMEM)
TM = ("tm_0", "tm_1", "tm_2")


def split(x):
    high = x.astype(BF16)
    return high, (x - high.astype(F32)).astype(BF16)


def dg(a, b, cb=0):
    return lax.dot_general(a, b, (((1,), (cb,)), ((), ())), preferred_element_type=F32)


def dot_s(a, b, cb=0):
    return dg(a[0], b[0], cb) + (dg(a[0], b[1], cb) + dg(a[1], b[0], cb))


def dot3(a, b, cb=0):
    return dot_s(split(a), split(b), cb)


def packed_blocks():
    out = []
    for j in range(4):
        out.append((0, j, LROW, j, 128, 0))
    for lane, (i, j) in enumerate(((1, 1), (1, 2), (1, 3), (2, 2))):
        out.append((i, j, LROW + 128, lane, 128, 0))
    for lane, (i, j, r) in enumerate(((2, 3, 0), (2, 3, 64), (3, 3, 0), (3, 3, 64))):
        out.append((i, j, LROW + 256, lane, 64, r))
    return out


def pack_spread(ref, full):
    for i, j, row, lane, rows, r0 in packed_blocks():
        ref[row : row + rows, lane * B : lane * B + B] = full(i * B + r0, rows, j * B)


def unpack_spread(load, full_ref):
    for i, j, row, lane, rows, r0 in packed_blocks():
        block = load(row, rows, lane * B)
        full_ref[i * B + r0 : i * B + r0 + rows, j * B : j * B + B] = block
    for i in range(4):
        for j in range(i + 1, 4):
            block = full_ref[i * B : i * B + B, j * B : j * B + B]
            full_ref[j * B : j * B + B, i * B : i * B + B] = jnp.transpose(block)


def inverse128(block):
    row_id = lax.broadcasted_iota(jnp.int32, (8, B), 0)
    lane_id = lax.broadcasted_iota(jnp.int32, (8, B), 1)
    vs = tuple(block[8 * b : 8 * b + 8, :] for b in range(16))

    def body(_, vs):
        vs = list(vs)
        for i in range(0, 8, 2):
            r0 = jnp.broadcast_to(vs[0][i : i + 1, :], (8, B))
            r1 = jnp.broadcast_to(vs[0][i + 1 : i + 2, :], (8, B))
            c0 = [jnp.broadcast_to(v[:, i : i + 1], (8, B)) for v in vs]
            c1 = [jnp.broadcast_to(v[:, i + 1 : i + 2], (8, B)) for v in vs]
            a = jnp.broadcast_to(c0[0][i : i + 1, :], (8, B))
            b = jnp.broadcast_to(c0[0][i + 1 : i + 2, :], (8, B))
            d = jnp.broadcast_to(c1[0][i + 1 : i + 2, :], (8, B))
            inv = 1.0 / (a * d - b * b)
            ia, ib, idd = d * inv, -b * inv, a * inv
            is0, is1 = lane_id == i, lane_id == i + 1
            n0 = ia * r0 + ib * r1
            n1 = ib * r0 + idd * r1
            n0 = jnp.where(is0, -ia, jnp.where(is1, -ib, n0))
            n1 = jnp.where(is0, -ib, jnp.where(is1, -idd, n1))
            for k in range(16):
                base = jnp.where(is0 | is1, 0.0, vs[k])
                new = base - (c0[k] * n0 + c1[k] * n1)
                if k == 0:
                    new = jnp.where(row_id == i, n0, jnp.where(row_id == i + 1, n1, new))
                vs[k] = new
        vs = [pltpu.roll(v, B - 8, 1) for v in vs]
        return tuple(vs[1:] + vs[:1])

    vs = lax.fori_loop(0, 16, body, vs)
    return -jnp.concatenate(vs, axis=0)


def element_kernel(ids, pattern, cov, mean_a, mean_b, noise, blocks, out, left, pred, sol, upd):
    tb = lambda r, j: split(blocks[r, j])

    def rows_of(ref, block):
        return ref[pl.ds(pl.multiple_of(block * B, B), B), :]

    def lanes_of(ref, row, rows, block):
        return ref[row : row + rows, pl.ds(pl.multiple_of(block * B, B), B)]

    mean = jnp.where(ids[0] == 1, mean_a[pl.ds(ids[1], 1), :], mean_b[pl.ds(ids[1], 1), :])
    upd[0:8, :] = jnp.broadcast_to(mean, (8, N))
    pushed = []
    for r in range(4):
        t0, t1 = tb(r, 0), tb(r, 1)
        left[r * B : r * B + B, :] = dot_s(t0, split(rows_of(cov, pattern[r, 0]))) + dot_s(
            t1, split(rows_of(cov, pattern[r, 1]))
        )
        pushed.append(
            dot_s(split(lanes_of(upd, 0, 8, pattern[r, 0])), t0, 1)
            + dot_s(split(lanes_of(upd, 0, 8, pattern[r, 1])), t1, 1)
        )
    pushed = jnp.concatenate(pushed, axis=1)
    eye = lax.broadcasted_iota(jnp.int32, (B, B), 0) == lax.broadcasted_iota(jnp.int32, (B, B), 1)
    for r in range(4):
        rows = (r + 1) * B
        value = dot_s(split(lanes_of(left, 0, rows, pattern[r, 0])), tb(r, 0), 1) + dot_s(
            split(lanes_of(left, 0, rows, pattern[r, 1])), tb(r, 1), 1
        )
        pred[0:rows, r * B : r * B + B] = value
        q = jnp.where(eye, jnp.broadcast_to(noise[0:1, r * B : r * B + B], (B, B)), 0.0)
        pred[r * B : rows, r * B : r * B + B] += q
    sol[...] = left[...]
    for k in range(4):
        k0, k1 = k * B, k * B + B
        inv = split(inverse128(pred[k0:k1, k0:k1]))
        rhs = split(sol[k0:k1, :])
        ub = dot_s(inv, rhs)
        sol[k0:k1, :] = ub
        if k < 3:
            ubs = split(ub)
            tail = pred[k0:k1, k1:]
            ut = dot_s(inv, split(tail))
            uts = split(ut)
            st = split(jnp.transpose(tail))
            pred[k1:, k1:] -= dot_s(st, uts)
            sol[k1:, :] -= dot_s(st, ubs)
            pred[k0:k1, k1:] = ut
    for k in (2, 1, 0):
        k0, k1 = k * B, k * B + B
        sol[k0:k1, :] -= dot3(pred[k0:k1, k1:], sol[k1:, :])
    keep = ids[2].astype(F32)
    for i in range(4):
        for j in range(4):
            out[i * B : i * B + B, j * B : j * B + B] = (
                jnp.transpose(sol[j * B : j * B + B, i * B : i * B + B]) * keep
            )
    out[GROW : GROW + 8, :] = jnp.broadcast_to(mean, (8, N)) - keep * dot3(pushed, sol[...])
    out[GROW + 8 :, :] = jnp.zeros((ROWS - GROW - 8, N), F32)
    ls = split(left[...])
    for i in range(4):
        pred[i * B : i * B + B, :] = cov[i * B : i * B + B, :] - dot_s(
            split(out[i * B : i * B + B, :]), ls
        )
    pack_spread(out, lambda r, n, c: pred[r : r + n, c : c + B])


def scan_kernel(count, want_total, want_rest, ids, own, others, *refs):
    outs, (se, sl, sg, rh, rl, eh, el, lk) = refs[: want_total + want_rest], refs[want_total + want_rest :]
    rest_ref = outs[-1]
    me = ids[0]

    def load(k, row, rows, lane=0, lanes=N):
        slot = k if count > 2 else 0
        return jnp.where(
            k == me, own[row : row + rows, lane : lane + lanes], others[slot, row : row + rows, lane : lane + lanes]
        )

    def store(ref, slot):
        ref[0:N, :] = se[slot]
        pack_spread(ref, lambda r, n, c: sl[slot, r : r + n, c : c + B])
        ref[GROW : GROW + 8, :] = sg[slot]
        ref[GROW + 8 :, :] = jnp.zeros((ROWS - GROW - 8, N), F32)

    if want_rest:

        @pl.when(me == count - 1)
        def _():
            same = lax.broadcasted_iota(jnp.int32, (N, N), 0) == lax.broadcasted_iota(jnp.int32, (N, N), 1)
            rest_ref[0:N, :] = same.astype(F32)
            rest_ref[N:, :] = jnp.zeros((ROWS - N, N), F32)

    last = count - 1
    se[0] = load(last, 0, N)
    unpack_spread(lambda r, n, c: load(last, r, n, c, B), sl.at[0])
    sg[0] = load(last, GROW, 8)

    def step(t, _):
        k = count - 2 - t
        now = lax.rem(t, 2)
        new = 1 - now
        if want_rest:

            @pl.when(k == me)
            def _():
                store(rest_ref, now)

        for r in range(4):
            rows = slice(r * B, r * B + B)
            h, l = split(se[now, rows, :])
            rh[rows, 0:N], rl[rows, 0:N] = h, l
            h, l = split(sl[now, rows, :])
            rh[rows, N:], rl[rows, N:] = h, l
            h, l = split(load(k, r * B, B))
            eh[rows, :], el[rows, :] = h, l
        unpack_spread(lambda r, n, c: load(k, r, n, c, B), lk)
        sg[new] = dot_s(split(sg[now]), (eh[...], el[...]), 1) + load(k, GROW, 8)

        def rows_step(r, _):
            rows = pl.ds(pl.multiple_of(r * B, B), B)
            both = dot_s((eh[rows, :], el[rows, :]), (rh[...], rl[...]))
            se[new, rows, :] = both[:, :N]
            sl[new, rows, :] = dot_s(split(both[:, N:]), (eh[...], el[...]), 1) + lk[rows, :]
            return 0

        lax.fori_loop(0, 4, rows_step, 0)
        return 0

    steps = count - 1
    if want_total:
        lax.fori_loop(0, steps, step, 0)
        store(outs[0], steps % 2)
    else:
        lax.fori_loop(0, steps, step, 0)


def apply_kernel(ids, later, across, down, pair, own, out, cov, mean, w, eh, el, lk):
    unpack_spread(lambda r, n, c: later[r : r + n, c : c + B], cov)
    mean[...] = later[GROW : GROW + 8, :]

    def push(load):
        for r in range(4):
            rows = slice(r * B, r * B + B)
            h, l = split(load(r * B, B))
            eh[rows, :], el[rows, :] = h, l
            h, l = split(cov[rows, :])
            w[0, rows, :], w[1, rows, :] = h, l
        unpack_spread(lambda r, n, c: load(r, n, c, B), lk)
        mean[...] = dot_s(split(mean[...]), (eh[...], el[...]), 1) + load(GROW, 8)

        def rows_step(r, _):
            rows = pl.ds(pl.multiple_of(r * B, B), B)
            half = dot_s((eh[rows, :], el[rows, :]), (w[0], w[1]))
            cov[rows, :] = dot_s(split(half), (eh[...], el[...]), 1) + lk[rows, :]
            return 0

        lax.fori_loop(0, 4, rows_step, 0)

    push(lambda r, n, c=0, m=N: across[r : r + n, c : c + m])
    push(lambda r, n, c=0, m=N: down[r : r + n, c : c + m])
    push(lambda r, n, c=0, m=N: jnp.where(ids[0] == 0, pair[r : r + n, c : c + m], own[r : r + n, c : c + m]))
    for z in range(4):
        out[z, 0:B, :] = cov[z * B : z * B + B, :]
        out[z, B : B + 8, :] = mean[...]


def greet(peers):
    barrier = pltpu.get_barrier_semaphore()
    for peer in peers:
        pl.semaphore_signal(barrier, inc=1, device_id=peer, device_id_type=MESH)
    pl.semaphore_wait(barrier, len(peers))


def column_peers(z, c):
    return [
        {"state": lax.rem(z + dz, 4), "tm_2": c if dc == 0 else 1 - c}
        for dz in range(4)
        for dc in range(2)
        if dz or dc
    ]


def remote(src, dst, send, recv, peer):
    return pltpu.make_async_remote_copy(
        src_ref=src, dst_ref=dst, send_sem=send, recv_sem=recv, device_id=peer, device_id_type=MESH
    )


def gather_step_kernel(cov, mean, out, mean_out, send, recv, local, msend, mrecv):
    z, c = lax.axis_index("state"), lax.axis_index("tm_2")
    greet(column_peers(z, c))
    other = remote(mean, mean_out, msend, mrecv, {"tm_2": 1 - c})
    other.start()

    def copy(i):
        dz = 2 * c + i // 2
        return remote(cov.at[i], out.at[z], send.at[i], recv.at[z], {"state": dz, "tm_2": i % 2})

    def mine(i):
        return (z == 2 * c + i // 2) & (c == i % 2)

    for i in range(4):

        @pl.when(mine(i))
        def _():
            pltpu.make_async_copy(cov.at[i], out.at[z], local).start()

        @pl.when(jnp.logical_not(mine(i)))
        def _():
            copy(i).start()

    for i in range(4):

        @pl.when(mine(i))
        def _():
            pltpu.make_async_copy(cov.at[i], out.at[z], local).wait()

        @pl.when(jnp.logical_not(mine(i)))
        def _():
            copy(i).wait_send()

    source_core = z // 2
    for s in range(4):

        @pl.when(jnp.logical_not((z == s) & (c == source_core)))
        def _():
            remote(cov.at[0], out.at[s], send.at[0], recv.at[s], {"state": 0, "tm_2": 0}).wait_recv()

    other.wait()


def scatter_step_kernel(slabs, out, send, recv, local):
    z, c = lax.axis_index("state"), lax.axis_index("tm_2")
    greet(column_peers(z, c))
    core = z // 2
    slot = 2 * lax.rem(z, 2) + c

    def copy(t):
        return remote(slabs.at[t], out.at[slot], send.at[t], recv.at[slot], {"state": t, "tm_2": core})

    def mine(t):
        return (z == t) & (c == core)

    for t in range(4):

        @pl.when(mine(t))
        def _():
            pltpu.make_async_copy(slabs.at[t], out.at[slot], local).start()

        @pl.when(jnp.logical_not(mine(t)))
        def _():
            copy(t).start()

    for t in range(4):

        @pl.when(mine(t))
        def _():
            pltpu.make_async_copy(slabs.at[t], out.at[slot], local).wait()

        @pl.when(jnp.logical_not(mine(t)))
        def _():
            copy(t).wait_send()

    for i in range(4):

        @pl.when(jnp.logical_not((z == 2 * c + i // 2) & (c == i % 2)))
        def _():
            remote(slabs.at[0], out.at[i], send.at[0], recv.at[i], {"state": 0, "tm_2": 0}).wait_recv()


def swap_kernel(x, out, send, recv):
    peer = {"tm_2": 1 - lax.axis_index("tm_2")}
    greet([peer])
    copy = remote(x, out.at[0], send, recv, peer)
    copy.start()
    copy.wait()


class Copies:
    def __init__(self, out, send, recv):
        self.out, self.send, self.recv, self.used, self.sent = out, send, recv, 0, []

    def put(self, peer, slot, row, rows, src=None):
        n, self.used = self.used, self.used + 1
        place = self.out.at[slot, pl.ds(pl.multiple_of(row, 8), rows), :]
        copy = remote(place if src is None else src, place, self.send.at[n], self.recv.at[n], peer)
        copy.start()
        self.sent.append(copy)
        return n

    def arrived(self, n, slot, row, rows):
        place = self.out.at[slot, pl.ds(pl.multiple_of(row, 8), rows), :]
        remote(place, place, self.send.at[n], self.recv.at[n], {"tm_2": 0}).wait_recv()

    def finish(self):
        for copy in self.sent:
            copy.wait_send()


def gather_z_kernel(x, out, send, recv):
    z, c = lax.axis_index("state"), lax.axis_index("tm_2")
    up, down = {"state": lax.rem(z + 1, 4)}, {"state": lax.rem(z + 3, 4)}
    twin = {"tm_2": 1 - c}
    zu, zd, zo = lax.rem(z + 1, 4), lax.rem(z + 3, 4), lax.rem(z + 2, 4)
    greet([up, down, twin])
    cp = Copies(out, send, recv)
    q = HALF // 2
    mine, theirs = c * HALF, (1 - c) * HALF
    first, second = [], []
    for part in (0, 1):
        row = mine + part * q
        src = x.at[pl.ds(pl.multiple_of(row, 8), q), :]
        first.append(cp.put(up, z, row, q, src))
        row = mine + (1 - part) * q
        src = x.at[pl.ds(pl.multiple_of(row, 8), q), :]
        second.append(cp.put(down, z, row, q, src))
    tail = []
    twins = []
    for part in (0, 1):
        row = mine + part * q
        cp.arrived(first[part], zd, row, q)
        if part == 0:
            up_tail = cp.put(up, zd, row, q)
        twins.append((cp.put(twin, zd, row, q), zd, theirs + part * q))
        row = mine + (1 - part) * q
        cp.arrived(second[part], zu, row, q)
        if part == 0:
            down_tail = cp.put(down, zu, row, q)
        twins.append((cp.put(twin, zu, row, q), zu, theirs + (1 - part) * q))
    cp.arrived(up_tail, zo, mine, q)
    twins.append((cp.put(twin, zo, mine, q), zo, theirs))
    cp.arrived(down_tail, zo, mine + q, q)
    twins.append((cp.put(twin, zo, mine + q, q), zo, theirs + q))
    for n, slot, row in twins:
        cp.arrived(n, slot, row, q)
    cp.finish()


def gather_ring_kernel(axis, x, out, send, recv):
    z, c, a = lax.axis_index("state"), lax.axis_index("tm_2"), lax.axis_index(axis)
    zu, zd = lax.rem(z + 1, 4), lax.rem(z + 3, 4)
    zo = lax.rem(z + 2, 4)
    au, ad, ao = lax.rem(a + 1, 4), lax.rem(a + 3, 4), lax.rem(a + 2, 4)
    up, down = {axis: au}, {axis: ad}
    above, below, twin = {"state": zu}, {"state": zd}, {"tm_2": 1 - c}
    greet([up, down, above, below, twin])
    cp = Copies(out, send, recv)
    row = lambda quarter, core: quarter * (2 * SH) + core * SH
    h = SH // 2
    quarters = (z, zu)
    from_down, from_up = [], []
    for k, quarter in enumerate(quarters):
        r = row(quarter, c)
        src = x.at[pl.ds(pl.multiple_of(r, 8), SH), :]
        from_down.append(cp.put(up, a, r, SH, src))
        from_up.append(cp.put(down, a, r, SH, src))
    twins, zs, opp = [], [], []

    def spread(k, slot, off, rows):
        r = row(quarters[k], c) + off
        n = cp.put(above if k == 0 else below, slot, r, rows)
        zs.append((n, slot, row(zd if k == 0 else zo, c) + off, row(zd if k == 0 else zo, 1 - c) + off, rows))
        twins.append((cp.put(twin, slot, r, rows), slot, row(quarters[k], 1 - c) + off, rows))

    for k, quarter in enumerate(quarters):
        r = row(quarter, c)
        cp.arrived(from_down[k], ad, r, SH)
        opp.append((k, 0, cp.put(up, ad, r, h)))
        spread(k, ad, 0, SH)
        cp.arrived(from_up[k], au, r, SH)
        opp.append((k, h, cp.put(down, au, r + h, h)))
        spread(k, au, 0, SH)

    def take(entry):
        n, slot, r, r_twin, rows = entry
        cp.arrived(n, slot, r, rows)
        twins.append((cp.put(twin, slot, r, rows), slot, r_twin, rows))

    for k, off, n in opp:
        cp.arrived(n, ao, row(quarters[k], c) + off, h)
        spread(k, ao, off, h)
    for entry in zs:
        take(entry)
    for n, slot, r, rows in twins:
        cp.arrived(n, slot, r, rows)
    cp.finish()


def shape(*dims, dtype=F32):
    return jax.ShapeDtypeStruct(dims, dtype)


def params(limit=None, **more):
    return pltpu.CompilerParams(vmem_limit_bytes=limit, **more)


DMA = pltpu.SemaphoreType.DMA


def comm(kernel, name, collective_id, outs, scratch, *args, out_spec=ANY):
    return pl.pallas_call(
        kernel,
        name=name,
        out_shape=outs,
        in_specs=[ANY] * len(args),
        out_specs=jax.tree.map(lambda _: out_spec, outs),
        scratch_shapes=scratch,
        compiler_params=pltpu.CompilerParams(collective_id=collective_id, has_side_effects=True),
    )(*args)


BIG = 56 * 1024 * 1024
WORK = [
    pltpu.VMEM((512, 512), BF16),
    pltpu.VMEM((512, 512), BF16),
    pltpu.VMEM((512, 512), F32),
]


def scan(name, count, want_total, want_rest, ids, own, others):
    packet = shape(ROWS, N)
    return pl.pallas_call(
        partial(scan_kernel, count, want_total, want_rest),
        name=name,
        out_shape=[packet] * (want_total + want_rest),
        in_specs=[SM, VM, VM],
        out_specs=[VM] * (want_total + want_rest),
        scratch_shapes=[
            pltpu.VMEM((2, N, N), F32),
            pltpu.VMEM((2, N, N), F32),
            pltpu.VMEM((2, 8, N), F32),
            pltpu.VMEM((N, 2 * N), BF16),
            pltpu.VMEM((N, 2 * N), BF16),
        ]
        + WORK,
        compiler_params=params(BIG),
    )(ids, own, others)


def on_device(filtered_cov, filtered_mean, noise_var, trans_blocks, pattern):
    y, x, c, z = (lax.axis_index(a) for a in ("tm_0", "tm_1", "tm_2", "state"))
    cov, twin_mean = comm(
        gather_step_kernel,
        "gather_step",
        0,
        (shape(4, B, N), shape(4, N)),
        [DMA((4,)), DMA((4,)), DMA, DMA, DMA],
        filtered_cov,
        filtered_mean,
        out_spec=VM,
    )
    step = 8 * (4 * y + x) + 2 * z + c
    ids = jnp.stack([(z // 2 == c).astype(jnp.int32), lax.rem(2 * z + c, 4), (step != 127).astype(jnp.int32)])
    own = pl.pallas_call(
        element_kernel,
        name="element",
        out_shape=shape(ROWS, N),
        in_specs=[SM, SM] + [VM] * 5,
        out_specs=VM,
        scratch_shapes=[pltpu.VMEM((N, N), F32)] * 3 + [pltpu.VMEM((8, N), F32)],
        compiler_params=params(BIG),
    )(ids, pattern, cov.reshape(N, N), filtered_mean, twin_mean, noise_var.reshape(1, N), trans_blocks)
    twin = comm(swap_kernel, "swap", 1, shape(1, ROWS, N), [DMA, DMA], own)
    one = lambda v: v.reshape(1).astype(jnp.int32)
    (pair,) = scan("scan_core", 2, True, False, one(c), own, twin)
    pairs = comm(gather_z_kernel, "gather_z", 2, shape(4, ROWS, N), [DMA((12,)), DMA((12,))], pair)
    column, down = scan("scan_z", 4, True, True, one(z), pair, pairs)
    columns = comm(
        partial(gather_ring_kernel, "tm_1"), "gather_x", 3, shape(4, ROWS, N), [DMA((32,)), DMA((32,))], column
    )
    row, across = scan("scan_x", 4, True, True, one(x), column, columns)
    rows = comm(partial(gather_ring_kernel, "tm_0"), "gather_y", 4, shape(4, ROWS, N), [DMA((32,)), DMA((32,))], row)
    (later,) = scan("scan_y", 4, False, True, one(y), row, rows)
    slabs = pl.pallas_call(
        apply_kernel,
        name="apply",
        out_shape=shape(4, B + 8, N),
        in_specs=[SM] + [VM] * 5,
        out_specs=VM,
        scratch_shapes=[pltpu.VMEM((N, N), F32), pltpu.VMEM((8, N), F32), pltpu.VMEM((2, N, N), BF16)] + WORK,
        compiler_params=params(BIG),
    )(one(c), later, across, down, pair, own)
    out = comm(scatter_step_kernel, "scatter_step", 5, shape(4, B + 8, N), [DMA((4,)), DMA((4,)), DMA], slabs, out_spec=VM)
    smooth_mean = lax.dynamic_slice_in_dim(out[:, B, :], z * B, B, 1)
    return smooth_mean, out[:, :B, :]


def solution(mesh):
    torus = Mesh(
        mesh.devices.reshape(4, 4, 2, mesh.shape["state"]), ("tm_0", "tm_1", "tm_2", "state")
    )
    return jax.shard_map(
        on_device,
        mesh=torus,
        in_specs=(P(TM, "state", None), P(TM, None), P(), P(), P()),
        out_specs=(P(TM, "state"), P(TM, "state", None)),
        check_vma=False,
    )
```

```python
from functools import partial

import jax
import jax.numpy as jnp
from jax import lax
from jax.experimental import pallas as pl
from jax.experimental.pallas import tpu as pltpu
from jax.sharding import Mesh
from jax.sharding import PartitionSpec as P

N = 512
B = 128
LROW = 512
GROW = 832
ROWS = 896
HALF = ROWS // 2
SH = ROWS // 8
MESH = pl.DeviceIdType.MESH
F32 = jnp.float32
BF16 = jnp.bfloat16
ANY = pl.BlockSpec(memory_space=pl.ANY)
VM = pl.BlockSpec(memory_space=pltpu.VMEM)
SM = pl.BlockSpec(memory_space=pltpu.SMEM)
TM = ("tm_0", "tm_1", "tm_2")


def split(x):
    high = x.astype(BF16)
    return high, (x - high.astype(F32)).astype(BF16)


def dg(a, b, cb=0):
    return lax.dot_general(a, b, (((1,), (cb,)), ((), ())), preferred_element_type=F32)


def dot_s(a, b, cb=0):
    return dg(a[0], b[0], cb) + (dg(a[0], b[1], cb) + dg(a[1], b[0], cb))


def dot3(a, b, cb=0):
    return dot_s(split(a), split(b), cb)


def dot6(a, b, cb=0, ca=1):
    return lax.dot_general(
        a, b, (((ca,), (cb,)), ((), ())), precision=lax.Precision.HIGHEST, preferred_element_type=F32
    )


def packed_blocks():
    out = []
    for j in range(4):
        out.append((0, j, LROW, j, 128, 0))
    for lane, (i, j) in enumerate(((1, 1), (1, 2), (1, 3), (2, 2))):
        out.append((i, j, LROW + 128, lane, 128, 0))
    for lane, (i, j, r) in enumerate(((2, 3, 0), (2, 3, 64), (3, 3, 0), (3, 3, 64))):
        out.append((i, j, LROW + 256, lane, 64, r))
    return out


def pack_spread(ref, full):
    for i, j, row, lane, rows, r0 in packed_blocks():
        ref[row : row + rows, lane * B : lane * B + B] = full(i * B + r0, rows, j * B)


def unpack_spread(load, full_ref):
    for i, j, row, lane, rows, r0 in packed_blocks():
        block = load(row, rows, lane * B)
        full_ref[i * B + r0 : i * B + r0 + rows, j * B : j * B + B] = block
    for i in range(4):
        for j in range(i + 1, 4):
            block = full_ref[i * B : i * B + B, j * B : j * B + B]
            full_ref[j * B : j * B + B, i * B : i * B + B] = jnp.transpose(block)


def small_mul(a, b):
    return [
        [sum((a[i][t] * b[t][j] for t in range(1, len(b))), a[i][0] * b[0][j]) for j in range(len(b[0]))]
        for i in range(len(a))
    ]


def small_inverse(m):
    n = len(m)
    if n == 2:
        a, b, d = m[0][0], m[0][1], m[1][1]
        inv = 1.0 / (a * d - b * b)
        return [[d * inv, -b * inv], [-b * inv, a * inv]]
    h = n // 2
    upper = [row[h:] for row in m[:h]]
    lower = [[upper[j][i] for j in range(h)] for i in range(h)]
    first = small_inverse([row[:h] for row in m[:h]])
    q = small_mul(lower, first)
    qb = small_mul(q, upper)
    schur = [[m[h + min(i, j)][h + max(i, j)] - qb[min(i, j)][max(i, j)] for j in range(h)] for i in range(h)]
    second = small_inverse(schur)
    sq = small_mul(second, q)
    qsq = small_mul([[q[j][i] for j in range(h)] for i in range(h)], sq)
    out = [[None] * n for _ in range(n)]
    for i in range(h):
        for j in range(h):
            out[i][j] = first[i][j] + qsq[i][j]
            out[h + i][h + j] = second[i][j]
            out[h + i][j] = out[j][h + i] = -sq[i][j]
    return out


PANEL = 64


def inverse128(block):
    groups = PANEL // 8
    row_id = lax.broadcasted_iota(jnp.int32, (8, B), 0)
    lane_id = lax.broadcasted_iota(jnp.int32, (8, B), 1)
    lanes = lax.broadcasted_iota(jnp.int32, (B, B), 1)

    def body(_, x):
        top = x[:PANEL, :]
        vs = [x[8 * k : 8 * k + 8, :] for k in range(groups)]
        for q in range(groups):
            at = 8 * q
            cols = [[jnp.broadcast_to(v[:, at + s : at + s + 1], (8, B)) for v in vs] for s in range(8)]
            rows = [jnp.broadcast_to(vs[q][s : s + 1, :], (8, B)) for s in range(8)]
            m = [[None] * 8 for _ in range(8)]
            for s in range(8):
                for t in range(s, 8):
                    m[s][t] = m[t][s] = jnp.broadcast_to(cols[s][q][t : t + 1, :], (8, B))
            inv = small_inverse(m)
            new_rows = [n[0] for n in small_mul(inv, [[r] for r in rows])]
            for s in range(8):
                for t in range(8):
                    new_rows[s] = jnp.where(lane_id == at + t, -inv[s][t], new_rows[s])
            inside = (lane_id >= at) & (lane_id < at + 8)
            for k in range(groups):
                if k == q:
                    new = new_rows[0]
                    for s in range(1, 8):
                        new = jnp.where(row_id == s, new_rows[s], new)
                else:
                    new = jnp.where(inside, 0.0, vs[k])
                    new -= sum((cols[s][k] * new_rows[s] for s in range(1, 8)), cols[0][k] * new_rows[0])
                vs[k] = new
        done = jnp.concatenate(vs, axis=0)
        rest = jnp.where(lanes < PANEL, 0.0, x) - dot6(top, done, 0, 0)
        return pltpu.roll(jnp.concatenate([rest[PANEL:, :], done], axis=0), B - PANEL, 1)

    return -lax.fori_loop(0, B // PANEL, body, block)


def element_kernel(ids, pattern, cov, mean_a, mean_b, noise, blocks, out, left, pred, sol, upd):
    tb = lambda r, j: blocks[r, j]

    def rows_of(ref, block):
        return ref[pl.ds(pl.multiple_of(block * B, B), B), :]

    def lanes_of(ref, row, rows, block):
        return ref[row : row + rows, pl.ds(pl.multiple_of(block * B, B), B)]

    mean = jnp.where(ids[0] == 1, mean_a[pl.ds(ids[1], 1), :], mean_b[pl.ds(ids[1], 1), :])
    upd[0:8, :] = jnp.broadcast_to(mean, (8, N))
    pushed = []
    for r in range(4):
        t0, t1 = tb(r, 0), tb(r, 1)
        left[r * B : r * B + B, :] = dot6(t0, rows_of(cov, pattern[r, 0])) + dot6(
            t1, rows_of(cov, pattern[r, 1])
        )
        pushed.append(
            dot6(lanes_of(upd, 0, 8, pattern[r, 0]), t0, 1)
            + dot6(lanes_of(upd, 0, 8, pattern[r, 1]), t1, 1)
        )
    pushed = jnp.concatenate(pushed, axis=1)
    eye = lax.broadcasted_iota(jnp.int32, (B, B), 0) == lax.broadcasted_iota(jnp.int32, (B, B), 1)
    for r in range(4):
        rows = (r + 1) * B
        value = dot6(lanes_of(left, 0, rows, pattern[r, 0]), tb(r, 0), 1) + dot6(
            lanes_of(left, 0, rows, pattern[r, 1]), tb(r, 1), 1
        )
        pred[0:rows, r * B : r * B + B] = value
        q = jnp.where(eye, jnp.broadcast_to(noise[0:1, r * B : r * B + B], (B, B)), 0.0)
        pred[r * B : rows, r * B : r * B + B] += q
    sol[...] = left[...]
    for k in range(4):
        k0, k1 = k * B, k * B + B
        inv = inverse128(pred[k0:k1, k0:k1])
        ub = dot6(inv, sol[k0:k1, :])
        sol[k0:k1, :] = ub
        if k < 3:
            tail = pred[k0:k1, k1:]
            ut = dot6(inv, tail)
            st = jnp.transpose(tail)
            pred[k1:, k1:] -= dot6(st, ut)
            sol[k1:, :] -= dot6(st, ub)
            pred[k0:k1, k1:] = ut
    for k in (2, 1, 0):
        k0, k1 = k * B, k * B + B
        sol[k0:k1, :] -= dot6(pred[k0:k1, k1:], sol[k1:, :])
    keep = ids[2].astype(F32)
    for i in range(4):
        for j in range(4):
            out[i * B : i * B + B, j * B : j * B + B] = (
                jnp.transpose(sol[j * B : j * B + B, i * B : i * B + B]) * keep
            )
    out[GROW : GROW + 8, :] = jnp.broadcast_to(mean, (8, N)) - keep * dot6(pushed, sol[...])
    out[GROW + 8 :, :] = jnp.zeros((ROWS - GROW - 8, N), F32)
    pred[...] = cov[...] - dot6(out[0:N, :], left[...])
    pack_spread(out, lambda r, n, c: pred[r : r + n, c : c + B])


def scan_kernel(count, want_total, want_rest, ids, own, others, *refs):
    outs, (se, sl, sg, rh, rl, eh, el, lk) = refs[: want_total + want_rest], refs[want_total + want_rest :]
    rest_ref = outs[-1]
    me = ids[0]

    def load(k, row, rows, lane=0, lanes=N):
        slot = k if count > 2 else 0
        return jnp.where(
            k == me, own[row : row + rows, lane : lane + lanes], others[slot, row : row + rows, lane : lane + lanes]
        )

    def store(ref, slot):
        ref[0:N, :] = se[slot]
        pack_spread(ref, lambda r, n, c: sl[slot, r : r + n, c : c + B])
        ref[GROW : GROW + 8, :] = sg[slot]
        ref[GROW + 8 :, :] = jnp.zeros((ROWS - GROW - 8, N), F32)

    if want_rest:

        @pl.when(me == count - 1)
        def _():
            same = lax.broadcasted_iota(jnp.int32, (N, N), 0) == lax.broadcasted_iota(jnp.int32, (N, N), 1)
            rest_ref[0:N, :] = same.astype(F32)
            rest_ref[N:, :] = jnp.zeros((ROWS - N, N), F32)

    last = count - 1
    se[0] = load(last, 0, N)
    unpack_spread(lambda r, n, c: load(last, r, n, c, B), sl.at[0])
    sg[0] = load(last, GROW, 8)

    def step(t, _):
        k = count - 2 - t
        now = lax.rem(t, 2)
        new = 1 - now
        if want_rest:

            @pl.when(k == me)
            def _():
                store(rest_ref, now)

        for r in range(4):
            rows = slice(r * B, r * B + B)
            h, l = split(se[now, rows, :])
            rh[rows, 0:N], rl[rows, 0:N] = h, l
            h, l = split(sl[now, rows, :])
            rh[rows, N:], rl[rows, N:] = h, l
            h, l = split(load(k, r * B, B))
            eh[rows, :], el[rows, :] = h, l
        unpack_spread(lambda r, n, c: load(k, r, n, c, B), lk)
        sg[new] = dot_s(split(sg[now]), (eh[...], el[...]), 1) + load(k, GROW, 8)

        e = (eh[...], el[...])
        se[new] = dot_s(e, (rh[:, :N], rl[:, :N]))
        half = split(dot_s(e, (rh[:, N:], rl[:, N:])))
        sl[new] = dot_s(half, e, 1) + lk[...]
        return 0

    steps = count - 1
    if want_total:
        lax.fori_loop(0, steps, step, 0)
        store(outs[0], steps % 2)
    else:
        lax.fori_loop(0, steps, step, 0)


def apply_kernel(ids, later, across, down, pair, own, out, cov, mean, w, eh, el, lk):
    unpack_spread(lambda r, n, c: later[r : r + n, c : c + B], cov)
    mean[...] = later[GROW : GROW + 8, :]

    def push(load):
        for r in range(4):
            rows = slice(r * B, r * B + B)
            h, l = split(load(r * B, B))
            eh[rows, :], el[rows, :] = h, l
            h, l = split(cov[rows, :])
            w[0, rows, :], w[1, rows, :] = h, l
        unpack_spread(lambda r, n, c: load(r, n, c, B), lk)
        mean[...] = dot_s(split(mean[...]), (eh[...], el[...]), 1) + load(GROW, 8)

        e = (eh[...], el[...])
        cov[...] = dot_s(split(dot_s(e, (w[0], w[1]))), e, 1) + lk[...]

    push(lambda r, n, c=0, m=N: across[r : r + n, c : c + m])
    push(lambda r, n, c=0, m=N: down[r : r + n, c : c + m])
    push(lambda r, n, c=0, m=N: jnp.where(ids[0] == 0, pair[r : r + n, c : c + m], own[r : r + n, c : c + m]))
    for z in range(4):
        out[z, 0:B, :] = cov[z * B : z * B + B, :]
        out[z, B : B + 8, :] = mean[...]


def greet(peers):
    barrier = pltpu.get_barrier_semaphore()
    for peer in peers:
        pl.semaphore_signal(barrier, inc=1, device_id=peer, device_id_type=MESH)
    pl.semaphore_wait(barrier, len(peers))


def column_peers(z, c):
    return [
        {"state": lax.rem(z + dz, 4), "tm_2": c if dc == 0 else 1 - c}
        for dz in range(4)
        for dc in range(2)
        if dz or dc
    ]


def remote(src, dst, send, recv, peer):
    return pltpu.make_async_remote_copy(
        src_ref=src, dst_ref=dst, send_sem=send, recv_sem=recv, device_id=peer, device_id_type=MESH
    )


def gather_step_kernel(cov, mean, out, mean_out, send, recv, local, msend, mrecv):
    z, c = lax.axis_index("state"), lax.axis_index("tm_2")
    greet(column_peers(z, c))
    other = remote(mean, mean_out, msend, mrecv, {"tm_2": 1 - c})
    other.start()

    def copy(i):
        dz = 2 * c + i // 2
        return remote(cov.at[i], out.at[z], send.at[i], recv.at[z], {"state": dz, "tm_2": i % 2})

    def mine(i):
        return (z == 2 * c + i // 2) & (c == i % 2)

    for i in range(4):

        @pl.when(mine(i))
        def _():
            pltpu.make_async_copy(cov.at[i], out.at[z], local).start()

        @pl.when(jnp.logical_not(mine(i)))
        def _():
            copy(i).start()

    for i in range(4):

        @pl.when(mine(i))
        def _():
            pltpu.make_async_copy(cov.at[i], out.at[z], local).wait()

        @pl.when(jnp.logical_not(mine(i)))
        def _():
            copy(i).wait_send()

    source_core = z // 2
    for s in range(4):

        @pl.when(jnp.logical_not((z == s) & (c == source_core)))
        def _():
            remote(cov.at[0], out.at[s], send.at[0], recv.at[s], {"state": 0, "tm_2": 0}).wait_recv()

    other.wait()


def scatter_step_kernel(slabs, out, send, recv, local):
    z, c = lax.axis_index("state"), lax.axis_index("tm_2")
    greet(column_peers(z, c))
    core = z // 2
    slot = 2 * lax.rem(z, 2) + c

    def copy(t):
        return remote(slabs.at[t], out.at[slot], send.at[t], recv.at[slot], {"state": t, "tm_2": core})

    def mine(t):
        return (z == t) & (c == core)

    for t in range(4):

        @pl.when(mine(t))
        def _():
            pltpu.make_async_copy(slabs.at[t], out.at[slot], local).start()

        @pl.when(jnp.logical_not(mine(t)))
        def _():
            copy(t).start()

    for t in range(4):

        @pl.when(mine(t))
        def _():
            pltpu.make_async_copy(slabs.at[t], out.at[slot], local).wait()

        @pl.when(jnp.logical_not(mine(t)))
        def _():
            copy(t).wait_send()

    for i in range(4):

        @pl.when(jnp.logical_not((z == 2 * c + i // 2) & (c == i % 2)))
        def _():
            remote(slabs.at[0], out.at[i], send.at[0], recv.at[i], {"state": 0, "tm_2": 0}).wait_recv()


def swap_kernel(x, out, send, recv):
    peer = {"tm_2": 1 - lax.axis_index("tm_2")}
    greet([peer])
    copy = remote(x, out.at[0], send, recv, peer)
    copy.start()
    copy.wait()


class Copies:
    def __init__(self, out, send, recv):
        self.out, self.send, self.recv, self.used, self.sent = out, send, recv, 0, []

    def put(self, peer, slot, row, rows, src=None):
        n, self.used = self.used, self.used + 1
        place = self.out.at[slot, pl.ds(pl.multiple_of(row, 8), rows), :]
        copy = remote(place if src is None else src, place, self.send.at[n], self.recv.at[n], peer)
        copy.start()
        self.sent.append(copy)
        return n

    def arrived(self, n, slot, row, rows):
        place = self.out.at[slot, pl.ds(pl.multiple_of(row, 8), rows), :]
        remote(place, place, self.send.at[n], self.recv.at[n], {"tm_2": 0}).wait_recv()

    def finish(self):
        for copy in self.sent:
            copy.wait_send()


def gather_z_kernel(x, out, send, recv):
    z, c = lax.axis_index("state"), lax.axis_index("tm_2")
    up, down = {"state": lax.rem(z + 1, 4)}, {"state": lax.rem(z + 3, 4)}
    twin = {"tm_2": 1 - c}
    zu, zd, zo = lax.rem(z + 1, 4), lax.rem(z + 3, 4), lax.rem(z + 2, 4)
    greet([up, down, twin])
    cp = Copies(out, send, recv)
    parts, q = 4, HALF // 4
    mine, theirs = c * HALF, (1 - c) * HALF
    ups, downs, tails, twins = [], [], [], []

    def source(row):
        return x.at[pl.ds(pl.multiple_of(row, 8), q), :]

    for j in range(parts):
        row = mine + j * q
        ups.append((cp.put(up, z, row, q, source(row)), j))
        row = mine + (parts - 1 - j) * q
        downs.append((cp.put(down, z, row, q, source(row)), parts - 1 - j))

    def hand(slot, j):
        twins.append((cp.put(twin, slot, mine + j * q, q), slot, theirs + j * q))

    for (nu, ju), (nd, jd) in zip(ups, downs):
        cp.arrived(nu, zd, mine + ju * q, q)
        if ju < parts // 2:
            tails.append((cp.put(up, zd, mine + ju * q, q), ju))
        hand(zd, ju)
        cp.arrived(nd, zu, mine + jd * q, q)
        if jd >= parts // 2:
            tails.append((cp.put(down, zu, mine + jd * q, q), jd))
        hand(zu, jd)
    for n, j in tails:
        cp.arrived(n, zo, mine + j * q, q)
        hand(zo, j)
    for n, slot, row in twins:
        cp.arrived(n, slot, row, q)
    cp.finish()


PIECES = ((0, 56), (56, 56))


def gather_ring_kernel(axis, x, out, send, recv):
    z, c, a = lax.axis_index("state"), lax.axis_index("tm_2"), lax.axis_index(axis)
    zu, zd, zo = lax.rem(z + 1, 4), lax.rem(z + 3, 4), lax.rem(z + 2, 4)
    au, ad, ao = lax.rem(a + 1, 4), lax.rem(a + 3, 4), lax.rem(a + 2, 4)
    up, down = {axis: au}, {axis: ad}
    above, below, twin = {"state": zu}, {"state": zd}, {"tm_2": 1 - c}
    greet([up, down, above, below, twin])
    cp = Copies(out, send, recv)
    row = lambda quarter, core: quarter * (2 * SH) + core * SH
    quarters = (z, zu)
    coming = (zd, zo)
    pieces = len(PIECES)
    order_up = list(range(pieces))
    order_down = order_up[::-1]
    ups, downs, twins, zs, tails = [], [], [], [], []
    for ju, jd in zip(order_up, order_down):
        for k in (0, 1):
            for into, peer, j in ((ups, up, ju), (downs, down, jd)):
                off, rows = PIECES[j]
                r = row(quarters[k], c) + off
                into.append((cp.put(peer, a, r, rows, x.at[pl.ds(pl.multiple_of(r, 8), rows), :]), k, j))

    def spread(k, slot, j):
        off, rows = PIECES[j]
        r = row(quarters[k], c) + off
        zs.append((cp.put(below if k else above, slot, r, rows), slot, k, j))
        twins.append((cp.put(twin, slot, r, rows), slot, row(quarters[k], 1 - c) + off, rows))

    def take(count):
        while len(zs) > count:
            n, slot, k, j = zs.pop(0)
            off, rows = PIECES[j]
            r = row(coming[k], c) + off
            cp.arrived(n, slot, r, rows)
            twins.append((cp.put(twin, slot, r, rows), slot, row(coming[k], 1 - c) + off, rows))

    for (nu, k, ju), (nd, _, jd) in zip(ups, downs):
        off, rows = PIECES[ju]
        cp.arrived(nu, ad, row(quarters[k], c) + off, rows)
        if ju < pieces // 2:
            tails.append((cp.put(up, ad, row(quarters[k], c) + off, rows), k, ju))
        spread(k, ad, ju)
        off, rows = PIECES[jd]
        cp.arrived(nd, au, row(quarters[k], c) + off, rows)
        if jd >= pieces // 2:
            tails.append((cp.put(down, au, row(quarters[k], c) + off, rows), k, jd))
        spread(k, au, jd)
    for n, k, j in tails:
        off, rows = PIECES[j]
        cp.arrived(n, ao, row(quarters[k], c) + off, rows)
        spread(k, ao, j)
    take(0)
    for n, slot, r, rows in twins:
        cp.arrived(n, slot, r, rows)
    cp.finish()


def shape(*dims, dtype=F32):
    return jax.ShapeDtypeStruct(dims, dtype)


def params(limit=None, **more):
    return pltpu.CompilerParams(vmem_limit_bytes=limit, **more)


DMA = pltpu.SemaphoreType.DMA


def comm(kernel, name, collective_id, outs, scratch, *args, out_spec=ANY):
    return pl.pallas_call(
        kernel,
        name=name,
        out_shape=outs,
        in_specs=[ANY] * len(args),
        out_specs=jax.tree.map(lambda _: out_spec, outs),
        scratch_shapes=scratch,
        compiler_params=pltpu.CompilerParams(collective_id=collective_id, has_side_effects=True),
    )(*args)


BIG = 56 * 1024 * 1024
WORK = [
    pltpu.VMEM((512, 512), BF16),
    pltpu.VMEM((512, 512), BF16),
    pltpu.VMEM((512, 512), F32),
]


def scan(name, count, want_total, want_rest, ids, own, others):
    packet = shape(ROWS, N)
    return pl.pallas_call(
        partial(scan_kernel, count, want_total, want_rest),
        name=name,
        out_shape=[packet] * (want_total + want_rest),
        in_specs=[SM, VM, VM],
        out_specs=[VM] * (want_total + want_rest),
        scratch_shapes=[
            pltpu.VMEM((2, N, N), F32),
            pltpu.VMEM((2, N, N), F32),
            pltpu.VMEM((2, 8, N), F32),
            pltpu.VMEM((N, 2 * N), BF16),
            pltpu.VMEM((N, 2 * N), BF16),
        ]
        + WORK,
        compiler_params=params(BIG),
    )(ids, own, others)


def on_device(filtered_cov, filtered_mean, noise_var, trans_blocks, pattern):
    y, x, c, z = (lax.axis_index(a) for a in ("tm_0", "tm_1", "tm_2", "state"))
    cov, twin_mean = comm(
        gather_step_kernel,
        "gather_step",
        0,
        (shape(4, B, N), shape(4, N)),
        [DMA((4,)), DMA((4,)), DMA, DMA, DMA],
        filtered_cov,
        filtered_mean,
        out_spec=VM,
    )
    step = 8 * (4 * y + x) + 2 * z + c
    ids = jnp.stack([(z // 2 == c).astype(jnp.int32), lax.rem(2 * z + c, 4), (step != 127).astype(jnp.int32)])
    own = pl.pallas_call(
        element_kernel,
        name="element",
        out_shape=shape(ROWS, N),
        in_specs=[SM, SM] + [VM] * 5,
        out_specs=VM,
        scratch_shapes=[pltpu.VMEM((N, N), F32)] * 3 + [pltpu.VMEM((8, N), F32)],
        compiler_params=params(BIG),
    )(ids, pattern, cov.reshape(N, N), filtered_mean, twin_mean, noise_var.reshape(1, N), trans_blocks)
    twin = comm(swap_kernel, "swap", 1, shape(1, ROWS, N), [DMA, DMA], own)
    one = lambda v: v.reshape(1).astype(jnp.int32)
    (pair,) = scan("scan_core", 2, True, False, one(c), own, twin)
    pairs = comm(gather_z_kernel, "gather_z", 2, shape(4, ROWS, N), [DMA((24,)), DMA((24,))], pair)
    column, down = scan("scan_z", 4, True, True, one(z), pair, pairs)
    columns = comm(
        partial(gather_ring_kernel, "tm_1"), "gather_x", 3, shape(4, ROWS, N), [DMA((48,)), DMA((48,))], column
    )
    row, across = scan("scan_x", 4, True, True, one(x), column, columns)
    rows = comm(partial(gather_ring_kernel, "tm_0"), "gather_y", 4, shape(4, ROWS, N), [DMA((48,)), DMA((48,))], row)
    (later,) = scan("scan_y", 4, False, True, one(y), row, rows)
    slabs = pl.pallas_call(
        apply_kernel,
        name="apply",
        out_shape=shape(4, B + 8, N),
        in_specs=[SM] + [VM] * 5,
        out_specs=VM,
        scratch_shapes=[pltpu.VMEM((N, N), F32), pltpu.VMEM((8, N), F32), pltpu.VMEM((2, N, N), BF16)] + WORK,
        compiler_params=params(BIG),
    )(one(c), later, across, down, pair, own)
    out = comm(scatter_step_kernel, "scatter_step", 5, shape(4, B + 8, N), [DMA((4,)), DMA((4,)), DMA], slabs, out_spec=VM)
    smooth_mean = lax.dynamic_slice_in_dim(out[:, B, :], z * B, B, 1)
    return smooth_mean, out[:, :B, :]


def solution(mesh):
    torus = Mesh(
        mesh.devices.reshape(4, 4, 2, mesh.shape["state"]), ("tm_0", "tm_1", "tm_2", "state")
    )
    return jax.shard_map(
        on_device,
        mesh=torus,
        in_specs=(P(TM, "state", None), P(TM, None), P(), P(), P()),
        out_specs=(P(TM, "state"), P(TM, "state", None)),
        check_vma=False,
    )
```

```python
from functools import partial

import jax
import jax.numpy as jnp
from jax import lax
from jax.experimental import pallas as pl
from jax.experimental.pallas import tpu as pltpu
from jax.sharding import Mesh
from jax.sharding import PartitionSpec as P

N = 512
B = 128
LROW = 512
GROW = 832
ROWS = 896
HALF = 424
PARTS = ((0, 112), (112, 104), (216, 104), (320, 104))
SH = ROWS // 8
MESH = pl.DeviceIdType.MESH
F32 = jnp.float32
BF16 = jnp.bfloat16
ANY = pl.BlockSpec(memory_space=pl.ANY)
VM = pl.BlockSpec(memory_space=pltpu.VMEM)
SM = pl.BlockSpec(memory_space=pltpu.SMEM)
TM = ("tm_0", "tm_1", "tm_2")


def split(x):
    high = x.astype(BF16)
    return high, (x - high.astype(F32)).astype(BF16)


def dg(a, b, cb=0):
    return lax.dot_general(a, b, (((1,), (cb,)), ((), ())), preferred_element_type=F32)


def dot_s(a, b, cb=0):
    return dg(a[0], b[0], cb) + (dg(a[0], b[1], cb) + dg(a[1], b[0], cb))


def dot3(a, b, cb=0):
    return dot_s(split(a), split(b), cb)


def dot6(a, b, cb=0, ca=1):
    return lax.dot_general(
        a, b, (((ca,), (cb,)), ((), ())), precision=lax.Precision.HIGHEST, preferred_element_type=F32
    )


def packed_blocks():
    out = []
    for j in range(4):
        out.append((0, j, LROW, j, 128, 0))
    for lane, (i, j) in enumerate(((1, 1), (1, 2), (1, 3), (2, 2))):
        out.append((i, j, LROW + 128, lane, 128, 0))
    for lane, (i, j, r) in enumerate(((2, 3, 0), (2, 3, 64), (3, 3, 0), (3, 3, 64))):
        out.append((i, j, LROW + 256, lane, 64, r))
    return out


def pack_spread(ref, full):
    for i, j, row, lane, rows, r0 in packed_blocks():
        ref[row : row + rows, lane * B : lane * B + B] = full(i * B + r0, rows, j * B)


def unpack_spread(load, full_ref):
    for i, j, row, lane, rows, r0 in packed_blocks():
        block = load(row, rows, lane * B)
        full_ref[i * B + r0 : i * B + r0 + rows, j * B : j * B + B] = block
    for i in range(4):
        for j in range(i + 1, 4):
            block = full_ref[i * B : i * B + B, j * B : j * B + B]
            full_ref[j * B : j * B + B, i * B : i * B + B] = jnp.transpose(block)


def small_mul(a, b):
    return [
        [sum((a[i][t] * b[t][j] for t in range(1, len(b))), a[i][0] * b[0][j]) for j in range(len(b[0]))]
        for i in range(len(a))
    ]


def small_inverse(m):
    n = len(m)
    if n == 2:
        a, b, d = m[0][0], m[0][1], m[1][1]
        inv = 1.0 / (a * d - b * b)
        return [[d * inv, -b * inv], [-b * inv, a * inv]]
    h = n // 2
    upper = [row[h:] for row in m[:h]]
    lower = [[upper[j][i] for j in range(h)] for i in range(h)]
    first = small_inverse([row[:h] for row in m[:h]])
    q = small_mul(lower, first)
    qb = small_mul(q, upper)
    schur = [[m[h + min(i, j)][h + max(i, j)] - qb[min(i, j)][max(i, j)] for j in range(h)] for i in range(h)]
    second = small_inverse(schur)
    sq = small_mul(second, q)
    qsq = small_mul([[q[j][i] for j in range(h)] for i in range(h)], sq)
    out = [[None] * n for _ in range(n)]
    for i in range(h):
        for j in range(h):
            out[i][j] = first[i][j] + qsq[i][j]
            out[h + i][h + j] = second[i][j]
            out[h + i][j] = out[j][h + i] = -sq[i][j]
    return out


PANEL = 64


def inverse128(block):
    groups = PANEL // 8
    row_id = lax.broadcasted_iota(jnp.int32, (8, B), 0)
    lane_id = lax.broadcasted_iota(jnp.int32, (8, B), 1)
    lanes = lax.broadcasted_iota(jnp.int32, (B, B), 1)

    def body(_, x):
        top = x[:PANEL, :]
        vs = [x[8 * k : 8 * k + 8, :] for k in range(groups)]
        for q in range(groups):
            at = 8 * q
            cols = [[jnp.broadcast_to(v[:, at + s : at + s + 1], (8, B)) for v in vs] for s in range(8)]
            rows = [jnp.broadcast_to(vs[q][s : s + 1, :], (8, B)) for s in range(8)]
            m = [[None] * 8 for _ in range(8)]
            for s in range(8):
                for t in range(s, 8):
                    m[s][t] = m[t][s] = jnp.broadcast_to(cols[s][q][t : t + 1, :], (8, B))
            inv = small_inverse(m)
            new_rows = [n[0] for n in small_mul(inv, [[r] for r in rows])]
            for s in range(8):
                for t in range(8):
                    new_rows[s] = jnp.where(lane_id == at + t, -inv[s][t], new_rows[s])
            inside = (lane_id >= at) & (lane_id < at + 8)
            for k in range(groups):
                if k == q:
                    new = new_rows[0]
                    for s in range(1, 8):
                        new = jnp.where(row_id == s, new_rows[s], new)
                else:
                    new = jnp.where(inside, 0.0, vs[k])
                    new -= sum((cols[s][k] * new_rows[s] for s in range(1, 8)), cols[0][k] * new_rows[0])
                vs[k] = new
        done = jnp.concatenate(vs, axis=0)
        rest = jnp.where(lanes < PANEL, 0.0, x) - dot6(top, done, 0, 0)
        return pltpu.roll(jnp.concatenate([rest[PANEL:, :], done], axis=0), B - PANEL, 1)

    return -lax.fori_loop(0, B // PANEL, body, block)


def element_kernel(pattern, cov_in, mean_a, mean_b, noise, blocks, out, left, pred, sol, upd, cov, inv_ref):
    y, x, c, z = (lax.axis_index(a) for a in ("tm_0", "tm_1", "tm_2", "state"))
    for i in range(4):
        for t in range(3):
            lanes = slice((i + t) % 4 * B, (i + t) % 4 * B + B)
            cov[i * B : i * B + B, lanes] = cov_in[i, :, lanes]
        j = (i + 3) % 4
        cov[i * B : i * B + B, j * B : j * B + B] = jnp.transpose(cov_in[j, :, i * B : i * B + B])
    tb = lambda r, j: blocks[r, j]

    def rows_of(ref, block):
        return ref[pl.ds(pl.multiple_of(block * B, B), B), :]

    def lanes_of(ref, row, rows, block):
        return ref[row : row + rows, pl.ds(pl.multiple_of(block * B, B), B)]

    place = lax.rem(2 * z + c, 4)
    mean = jnp.where(z // 2 == c, mean_a[pl.ds(place, 1), :], mean_b[pl.ds(place, 1), :])
    upd[0:8, :] = jnp.broadcast_to(mean, (8, N))
    pushed = []
    for r in range(4):
        t0, t1 = tb(r, 0), tb(r, 1)
        left[r * B : r * B + B, :] = dot6(t0, rows_of(cov, pattern[r, 0])) + dot6(
            t1, rows_of(cov, pattern[r, 1])
        )
        pushed.append(
            dot6(lanes_of(upd, 0, 8, pattern[r, 0]), t0, 1)
            + dot6(lanes_of(upd, 0, 8, pattern[r, 1]), t1, 1)
        )
    pushed = jnp.concatenate(pushed, axis=1)
    eye = lax.broadcasted_iota(jnp.int32, (B, B), 0) == lax.broadcasted_iota(jnp.int32, (B, B), 1)
    for r in range(4):
        rows = (r + 1) * B
        value = dot6(lanes_of(left, 0, rows, pattern[r, 0]), tb(r, 0), 1) + dot6(
            lanes_of(left, 0, rows, pattern[r, 1]), tb(r, 1), 1
        )
        pred[0:rows, r * B : r * B + B] = value
        q = jnp.where(eye, jnp.broadcast_to(noise[0:1, r * B : r * B + B], (B, B)), 0.0)
        pred[r * B : rows, r * B : r * B + B] += q
    sol[...] = left[...]

    def eliminate(k, _):
        at = pl.ds(pl.multiple_of(k * B, B), B)
        inv_ref[...] = inverse128(pred[at, at])
        for kk in range(4):

            @pl.when(k == kk)
            def _():
                k0, k1 = kk * B, kk * B + B
                inv = inv_ref[...]
                ub = dot6(inv, sol[k0:k1, :])
                sol[k0:k1, :] = ub
                if kk < 3:
                    tail = pred[k0:k1, k1:]
                    ut = dot6(inv, tail)
                    st = jnp.transpose(tail)
                    pred[k1:, k1:] -= dot6(st, ut)
                    sol[k1:, :] -= dot6(st, ub)
                    pred[k0:k1, k1:] = ut

        return 0

    lax.fori_loop(0, 4, eliminate, 0)
    for k in (2, 1, 0):
        k0, k1 = k * B, k * B + B
        sol[k0:k1, :] -= dot6(pred[k0:k1, k1:], sol[k1:, :])
    keep = (8 * (4 * y + x) + 2 * z + c != 127).astype(F32)
    for i in range(4):
        for j in range(4):
            out[i * B : i * B + B, j * B : j * B + B] = (
                jnp.transpose(sol[j * B : j * B + B, i * B : i * B + B]) * keep
            )
    out[GROW : GROW + 8, :] = jnp.broadcast_to(mean, (8, N)) - keep * dot6(pushed, sol[...])
    out[GROW + 8 :, :] = jnp.zeros((ROWS - GROW - 8, N), F32)
    pred[...] = cov[...] - dot6(out[0:N, :], left[...])
    pack_spread(out, lambda r, n, c: pred[r : r + n, c : c + B])


def scan_kernel(axis, count, want_total, want_rest, own, others, *refs):
    outs, (se, sl, sg, rh, rl, eh, el, lk) = refs[: want_total + want_rest], refs[want_total + want_rest :]
    rest_ref = outs[-1]
    me = lax.axis_index(axis)

    def load(k, row, rows, lane=0, lanes=N):
        slot = k if count > 2 else 0
        return jnp.where(
            k == me, own[row : row + rows, lane : lane + lanes], others[slot, row : row + rows, lane : lane + lanes]
        )

    def store(ref, slot):
        ref[0:N, :] = se[slot]
        pack_spread(ref, lambda r, n, c: sl[slot, r : r + n, c : c + B])
        ref[GROW : GROW + 8, :] = sg[slot]
        ref[GROW + 8 :, :] = jnp.zeros((ROWS - GROW - 8, N), F32)

    if want_rest:

        @pl.when(me == count - 1)
        def _():
            same = lax.broadcasted_iota(jnp.int32, (N, N), 0) == lax.broadcasted_iota(jnp.int32, (N, N), 1)
            rest_ref[0:N, :] = same.astype(F32)
            rest_ref[N:, :] = jnp.zeros((ROWS - N, N), F32)

    last = count - 1
    se[0] = load(last, 0, N)
    unpack_spread(lambda r, n, c: load(last, r, n, c, B), sl.at[0])
    sg[0] = load(last, GROW, 8)

    def step(t, _):
        k = count - 2 - t
        now = lax.rem(t, 2)
        new = 1 - now
        if want_rest:

            @pl.when(k == me)
            def _():
                store(rest_ref, now)

        for r in range(4):
            rows = slice(r * B, r * B + B)
            h, l = split(se[now, rows, :])
            rh[rows, 0:N], rl[rows, 0:N] = h, l
            h, l = split(sl[now, rows, :])
            rh[rows, N:], rl[rows, N:] = h, l
            h, l = split(load(k, r * B, B))
            eh[rows, :], el[rows, :] = h, l
        unpack_spread(lambda r, n, c: load(k, r, n, c, B), lk)
        sg[new] = dot_s(split(sg[now]), (eh[...], el[...]), 1) + load(k, GROW, 8)

        e = (eh[...], el[...])
        se[new] = dot_s(e, (rh[:, :N], rl[:, :N]))
        half = split(dot_s(e, (rh[:, N:], rl[:, N:])))
        sl[new] = dot_s(half, e, 1) + lk[...]
        return 0

    steps = count - 1
    if want_total:
        lax.fori_loop(0, steps, step, 0)
        store(outs[0], steps % 2)
    else:
        lax.fori_loop(0, steps, step, 0)


def apply_kernel(later, across, down, pair, own, out, mean_out, cov, mean, add, w, eh, el, lk):
    unpack_spread(lambda r, n, c: later[r : r + n, c : c + B], cov)
    mean[...] = later[GROW : GROW + 8, :]

    def take(load):
        for r in range(4):
            rows = slice(r * B, r * B + B)
            h, l = split(load(r * B, B))
            eh[rows, :], el[rows, :] = h, l
        unpack_spread(lambda r, n, c: load(r, n, c, B), lk)
        add[...] = load(GROW, 8)

    loads = (
        lambda r, n, c=0, m=N: across[r : r + n, c : c + m],
        lambda r, n, c=0, m=N: down[r : r + n, c : c + m],
        lambda r, n, c=0, m=N: jnp.where(
            lax.axis_index("tm_2") == 0, pair[r : r + n, c : c + m], own[r : r + n, c : c + m]
        ),
    )

    def push(t, _):
        for k in range(3):
            pl.when(t == k)(partial(take, loads[k]))
        for r in range(4):
            rows = slice(r * B, r * B + B)
            h, l = split(cov[rows, :])
            w[0, rows, :], w[1, rows, :] = h, l
        e = (eh[...], el[...])
        mean[...] = dot_s(split(mean[...]), e, 1) + add[...]
        cov[...] = dot_s(split(dot_s(e, (w[0], w[1]))), e, 1) + lk[...]
        return 0

    lax.fori_loop(0, 3, push, 0)
    for z in range(4):
        out[z] = cov[z * B : z * B + B, :]
    mean_out[...] = mean[...]


def greet(peers):
    barrier = pltpu.get_barrier_semaphore()
    for peer in peers:
        pl.semaphore_signal(barrier, inc=1, device_id=peer, device_id_type=MESH)
    pl.semaphore_wait(barrier, len(peers))


def column_peers(z, c):
    return [
        {"state": lax.rem(z + dz, 4), "tm_2": c if dc == 0 else 1 - c}
        for dz in range(4)
        for dc in range(2)
        if dz or dc
    ]


def remote(src, dst, send, recv, peer):
    return pltpu.make_async_remote_copy(
        src_ref=src, dst_ref=dst, send_sem=send, recv_sem=recv, device_id=peer, device_id_type=MESH
    )


def lanes_of_block(ref, j):
    return ref.at[:, pl.ds(pl.multiple_of(lax.rem(j, 4) * B, B), B)]


def gather_step_kernel(cov, mean, out, mean_out, relay, send, recv, relay_send, relay_recv, local, msend, mrecv):
    z, c = lax.axis_index("state"), lax.axis_index("tm_2")
    greet(column_peers(z, c))
    other = remote(mean, mean_out, msend, mrecv, {"tm_2": 1 - c})
    other.start()

    def start(src, dst, row, ssem, rsem, peer):
        for t in range(3):
            remote(lanes_of_block(src, row + t), lanes_of_block(dst, row + t), ssem, rsem, peer).start()

    def whole(ref, ssem, rsem):
        part = ref.at[:, 0 : 3 * B]
        return remote(part, part, ssem, rsem, {"state": 0, "tm_2": 0})

    def target(i):
        dz, e = 2 * c + i // 2, i % 2
        mine = (z == dz) & (c == e)
        far = lax.rem(dz + 4 - z, 4) == 2
        return dz, e, mine, far

    for i in range(4):
        dz, e, mine, far = target(i)

        @pl.when(far)
        def _():
            start(cov.at[i], relay.at[e], z, send.at[i], relay_recv.at[e], {"state": lax.rem(z + (3 if e else 1), 4)})

    for i in range(4):
        dz, e, mine, far = target(i)

        @pl.when(mine)
        def _():
            pltpu.make_async_copy(cov.at[i], out.at[z], local).start()

        @pl.when(jnp.logical_not(mine | far))
        def _():
            start(cov.at[i], out.at[z], z, send.at[i], recv.at[z], {"state": dz, "tm_2": e})

    duties = []
    for e in range(2):
        source, dz = lax.rem(z + (1 if e else 3), 4), lax.rem(z + (3 if e else 1), 4)
        duty = source // 2 != c
        duties.append(duty)

        @pl.when(duty)
        def _():
            whole(relay.at[e], send.at[0], relay_recv.at[e]).wait_recv()
            start(relay.at[e], out.at[source], source, relay_send.at[e], recv.at[source], {"state": dz, "tm_2": e})

    for i in range(4):
        dz, e, mine, far = target(i)

        @pl.when(mine)
        def _():
            pltpu.make_async_copy(cov.at[i], out.at[z], local).wait()

        @pl.when(jnp.logical_not(mine))
        def _():
            whole(cov.at[i], send.at[i], recv.at[0]).wait_send()

    for e in range(2):

        @pl.when(duties[e])
        def _():
            whole(relay.at[e], relay_send.at[e], recv.at[0]).wait_send()

    source_core = z // 2
    for s in range(4):

        @pl.when(jnp.logical_not((z == s) & (c == source_core)))
        def _():
            whole(out.at[s], send.at[0], recv.at[s]).wait_recv()

    other.wait()


def scatter_step_kernel(slabs, mean, out, mean_out, relay, send, recv, relay_send, relay_recv, local, msend, mrecv):
    z, c = lax.axis_index("state"), lax.axis_index("tm_2")
    greet(column_peers(z, c))
    core = z // 2
    slot = 2 * lax.rem(z, 2) + c
    opposite = lax.rem(z + 2, 4)
    onward = lax.rem(z + 1 + 2 * c, 4)
    far = remote(slabs.at[opposite], relay, relay_send.at[0], relay_recv, {"state": onward})
    far.start()

    def copy(t):
        return remote(slabs.at[t], out.at[slot], send.at[t], recv.at[slot], {"state": t, "tm_2": core})

    def mean_copy(t):
        return remote(mean, mean_out.at[slot], msend.at[t], mrecv.at[slot], {"state": t, "tm_2": core})

    def mine(t):
        return (z == t) & (c == core)

    def copies(t):
        return pltpu.make_async_copy(slabs.at[t], out.at[slot], local.at[0]), pltpu.make_async_copy(
            mean, mean_out.at[slot], local.at[1]
        )

    for t in range(4):

        @pl.when(mine(t))
        def _():
            for copy_here in copies(t):
                copy_here.start()

        @pl.when(jnp.logical_not(mine(t)))
        def _():
            mean_copy(t).start()

        @pl.when(jnp.logical_not(mine(t)) & (t != opposite))
        def _():
            copy(t).start()

    source = lax.rem(z + 3 + 2 * c, 4)
    far.wait_recv()
    on = remote(
        relay,
        out.at[2 * lax.rem(source, 2) + c],
        relay_send.at[1],
        recv.at[2 * lax.rem(source, 2) + c],
        {"state": onward, "tm_2": source // 2},
    )
    on.start()
    for t in range(4):

        @pl.when(mine(t))
        def _():
            for copy_here in copies(t):
                copy_here.wait()

        @pl.when(jnp.logical_not(mine(t)))
        def _():
            mean_copy(t).wait_send()

        @pl.when(jnp.logical_not(mine(t)) & (t != opposite))
        def _():
            copy(t).wait_send()

    far.wait_send()
    on.wait_send()
    for i in range(4):

        @pl.when(jnp.logical_not((z == 2 * c + i // 2) & (c == i % 2)))
        def _():
            remote(slabs.at[0], out.at[i], send.at[0], recv.at[i], {"state": 0, "tm_2": 0}).wait_recv()
            remote(mean, mean_out.at[i], msend.at[0], mrecv.at[i], {"state": 0, "tm_2": 0}).wait_recv()


def swap_kernel(x, out, send, recv):
    peer = {"tm_2": 1 - lax.axis_index("tm_2")}
    greet([peer])
    copy = remote(x, out.at[0], send, recv, peer)
    copy.start()
    copy.wait()


class Copies:
    def __init__(self, out, send, recv):
        self.out, self.send, self.recv, self.used, self.sent = out, send, recv, 0, []

    def put(self, peer, slot, row, rows, src=None):
        n, self.used = self.used, self.used + 1
        place = self.out.at[slot, pl.ds(pl.multiple_of(row, 8), rows), :]
        copy = remote(place if src is None else src, place, self.send.at[n], self.recv.at[n], peer)
        copy.start()
        self.sent.append(copy)
        return n

    def arrived(self, n, slot, row, rows):
        place = self.out.at[slot, pl.ds(pl.multiple_of(row, 8), rows), :]
        remote(place, place, self.send.at[n], self.recv.at[n], {"tm_2": 0}).wait_recv()

    def finish(self):
        for copy in self.sent:
            copy.wait_send()


def gather_z_kernel(x, out, send, recv):
    z, c = lax.axis_index("state"), lax.axis_index("tm_2")
    up, down = {"state": lax.rem(z + 1, 4)}, {"state": lax.rem(z + 3, 4)}
    twin = {"tm_2": 1 - c}
    zu, zd, zo = lax.rem(z + 1, 4), lax.rem(z + 3, 4), lax.rem(z + 2, 4)
    greet([up, down, twin])
    cp = Copies(out, send, recv)
    mine, theirs = c * HALF, (1 - c) * HALF
    ups, downs, tails, twins = [], [], [], []

    def source(row, rows):
        return x.at[pl.ds(pl.multiple_of(row, 8), rows), :]

    for up_part, down_part in zip(PARTS, PARTS[::-1]):
        off, rows = up_part
        ups.append((cp.put(up, z, mine + off, rows, source(mine + off, rows)), up_part))
        off, rows = down_part
        downs.append((cp.put(down, z, mine + off, rows, source(mine + off, rows)), down_part))

    def hand(slot, part):
        off, rows = part
        twins.append((cp.put(twin, slot, mine + off, rows), slot, theirs + off, rows))

    for j, ((nu, up_part), (nd, down_part)) in enumerate(zip(ups, downs)):
        off, rows = up_part
        cp.arrived(nu, zd, mine + off, rows)
        if j < len(PARTS) // 2:
            tails.append((cp.put(up, zd, mine + off, rows), up_part))
        hand(zd, up_part)
        off, rows = down_part
        cp.arrived(nd, zu, mine + off, rows)
        if j < len(PARTS) // 2:
            tails.append((cp.put(down, zu, mine + off, rows), down_part))
        hand(zu, down_part)
    for n, part in tails:
        cp.arrived(n, zo, mine + part[0], part[1])
        hand(zo, part)
    for n, slot, row, rows in twins:
        cp.arrived(n, slot, row, rows)
    cp.finish()


PIECES = ((0, 32), (32, 24), (56, 32), (88, 24))


def gather_ring_kernel(axis, x, out, send, recv):
    z, c, a = lax.axis_index("state"), lax.axis_index("tm_2"), lax.axis_index(axis)
    zu, zd, zo = lax.rem(z + 1, 4), lax.rem(z + 3, 4), lax.rem(z + 2, 4)
    au, ad, ao = lax.rem(a + 1, 4), lax.rem(a + 3, 4), lax.rem(a + 2, 4)
    up, down = {axis: au}, {axis: ad}
    above, below, twin = {"state": zu}, {"state": zd}, {"tm_2": 1 - c}
    greet([up, down, above, below, twin])
    cp = Copies(out, send, recv)
    row = lambda quarter, core: quarter * (2 * SH) + core * SH
    quarters = (z, zu)
    coming = (zd, zo)
    pieces = len(PIECES)
    order_up = list(range(pieces))
    order_down = order_up[::-1]
    ups, downs, twins, zs, tails = [], [], [], [], []
    for ju, jd in zip(order_up, order_down):
        for k in (0, 1):
            for into, peer, j in ((ups, up, ju), (downs, down, jd)):
                off, rows = PIECES[j]
                r = row(quarters[k], c) + off
                into.append((cp.put(peer, a, r, rows, x.at[pl.ds(pl.multiple_of(r, 8), rows), :]), k, j))

    def spread(k, slot, j):
        off, rows = PIECES[j]
        r = row(quarters[k], c) + off
        zs.append((cp.put(below if k else above, slot, r, rows), slot, k, j))
        twins.append((cp.put(twin, slot, r, rows), slot, row(quarters[k], 1 - c) + off, rows))

    def take(count):
        while len(zs) > count:
            n, slot, k, j = zs.pop(0)
            off, rows = PIECES[j]
            r = row(coming[k], c) + off
            cp.arrived(n, slot, r, rows)
            twins.append((cp.put(twin, slot, r, rows), slot, row(coming[k], 1 - c) + off, rows))

    for (nu, k, ju), (nd, _, jd) in zip(ups, downs):
        off, rows = PIECES[ju]
        cp.arrived(nu, ad, row(quarters[k], c) + off, rows)
        if ju < pieces // 2:
            tails.append((cp.put(up, ad, row(quarters[k], c) + off, rows), k, ju))
        spread(k, ad, ju)
        off, rows = PIECES[jd]
        cp.arrived(nd, au, row(quarters[k], c) + off, rows)
        if jd >= pieces // 2:
            tails.append((cp.put(down, au, row(quarters[k], c) + off, rows), k, jd))
        spread(k, au, jd)
    for n, k, j in tails:
        off, rows = PIECES[j]
        cp.arrived(n, ao, row(quarters[k], c) + off, rows)
        spread(k, ao, j)
        take(len(zs) - 2)
    take(0)
    for n, slot, r, rows in twins:
        cp.arrived(n, slot, r, rows)
    cp.finish()


def shape(*dims, dtype=F32):
    return jax.ShapeDtypeStruct(dims, dtype)


def params(limit=None, **more):
    return pltpu.CompilerParams(vmem_limit_bytes=limit, **more)


DMA = pltpu.SemaphoreType.DMA


def comm(kernel, name, collective_id, outs, scratch, *args, out_spec=ANY):
    return pl.pallas_call(
        kernel,
        name=name,
        out_shape=outs,
        in_specs=[ANY] * len(args),
        out_specs=jax.tree.map(lambda _: out_spec, outs),
        scratch_shapes=scratch,
        compiler_params=pltpu.CompilerParams(
            collective_id=collective_id, has_side_effects=True, vmem_limit_bytes=4 * 1024 * 1024
        ),
    )(*args)


BIG = 32 * 1024 * 1024
WORK = [
    pltpu.VMEM((512, 512), BF16),
    pltpu.VMEM((512, 512), BF16),
    pltpu.VMEM((512, 512), F32),
]


def scan(name, axis, count, want_total, want_rest, own, others):
    packet = shape(ROWS, N)
    return pl.pallas_call(
        partial(scan_kernel, axis, count, want_total, want_rest),
        name=name,
        out_shape=[packet] * (want_total + want_rest),
        in_specs=[VM, VM],
        out_specs=[VM] * (want_total + want_rest),
        scratch_shapes=[
            pltpu.VMEM((2, N, N), F32),
            pltpu.VMEM((2, N, N), F32),
            pltpu.VMEM((2, 8, N), F32),
            pltpu.VMEM((N, 2 * N), BF16),
            pltpu.VMEM((N, 2 * N), BF16),
        ]
        + WORK,
        compiler_params=params(BIG),
    )(own, others)


def on_device(filtered_cov, filtered_mean, noise_var, trans_blocks, pattern):
    z = lax.axis_index("state")
    cov, twin_mean = comm(
        gather_step_kernel,
        "gather_step",
        0,
        (shape(4, B, N), shape(4, N)),
        [pltpu.VMEM((2, B, N), F32), DMA((4,)), DMA((4,)), DMA((2,)), DMA((2,)), DMA, DMA, DMA],
        filtered_cov,
        filtered_mean,
        out_spec=VM,
    )
    own = pl.pallas_call(
        element_kernel,
        name="element",
        out_shape=shape(ROWS, N),
        in_specs=[SM] + [VM] * 5,
        out_specs=VM,
        scratch_shapes=[pltpu.VMEM((N, N), F32)] * 3 + [pltpu.VMEM((8, N), F32), pltpu.VMEM((N, N), F32), pltpu.VMEM((B, B), F32)],
        compiler_params=params(BIG),
    )(pattern, cov, filtered_mean, twin_mean, noise_var.reshape(1, N), trans_blocks)
    twin = comm(swap_kernel, "swap", 1, shape(1, ROWS, N), [DMA, DMA], own)
    (pair,) = scan("scan_core", "tm_2", 2, True, False, own, twin)
    pairs = comm(gather_z_kernel, "gather_z", 2, shape(4, ROWS, N), [DMA((24,)), DMA((24,))], pair)
    column, down = scan("scan_z", "state", 4, True, True, pair, pairs)
    columns = comm(
        partial(gather_ring_kernel, "tm_1"), "gather_x", 3, shape(4, ROWS, N), [DMA((96,)), DMA((96,))], column
    )
    row, across = scan("scan_x", "tm_1", 4, True, True, column, columns)
    rows = comm(partial(gather_ring_kernel, "tm_0"), "gather_y", 4, shape(4, ROWS, N), [DMA((96,)), DMA((96,))], row)
    (later,) = scan("scan_y", "tm_0", 4, False, True, row, rows)
    slabs, mean = pl.pallas_call(
        apply_kernel,
        name="apply",
        out_shape=(shape(4, B, N), shape(8, N)),
        in_specs=[VM] * 5,
        out_specs=(VM, VM),
        scratch_shapes=[pltpu.VMEM((N, N), F32), pltpu.VMEM((8, N), F32), pltpu.VMEM((8, N), F32), pltpu.VMEM((2, N, N), BF16)]
        + WORK,
        compiler_params=params(BIG),
    )(later, across, down, pair, own)
    smooth_cov, means = comm(
        scatter_step_kernel,
        "scatter_step",
        5,
        (shape(4, B, N), shape(4, 8, N)),
        [pltpu.VMEM((B, N), F32), DMA((4,)), DMA((4,)), DMA((2,)), DMA, DMA((2,)), DMA((4,)), DMA((4,))],
        slabs,
        mean,
        out_spec=VM,
    )
    return lax.dynamic_slice_in_dim(means[:, 0, :], z * B, B, 1), smooth_cov


def solution(mesh):
    torus = Mesh(
        mesh.devices.reshape(4, 4, 2, mesh.shape["state"]), ("tm_0", "tm_1", "tm_2", "state")
    )
    return jax.shard_map(
        on_device,
        mesh=torus,
        in_specs=(P(TM, "state", None), P(TM, None), P(), P(), P()),
        out_specs=(P(TM, "state"), P(TM, "state", None)),
        check_vma=False,
    )
```

```python
from functools import partial

import jax
import jax.numpy as jnp
from jax import lax
from jax.experimental import pallas as pl
from jax.experimental.pallas import tpu as pltpu
from jax.sharding import Mesh
from jax.sharding import PartitionSpec as P

N = 512
B = 128
LROW = 512
GROW = 832
ROWS = 896
MESH = pl.DeviceIdType.MESH
F32 = jnp.float32
BF16 = jnp.bfloat16
ANY = pl.BlockSpec(memory_space=pl.ANY)
VM = pl.BlockSpec(memory_space=pltpu.VMEM)
SM = pl.BlockSpec(memory_space=pltpu.SMEM)
TM = ("tm_0", "tm_1", "tm_2")


def split(x):
    high = x.astype(BF16)
    return high, (x - high.astype(F32)).astype(BF16)


def dg(a, b, cb=0):
    return lax.dot_general(a, b, (((1,), (cb,)), ((), ())), preferred_element_type=F32)


def dot_s(a, b, cb=0):
    return dg(a[0], b[0], cb) + (dg(a[0], b[1], cb) + dg(a[1], b[0], cb))


def dot3(a, b, cb=0):
    return dot_s(split(a), split(b), cb)


def dot6(a, b, cb=0, ca=1):
    return lax.dot_general(
        a, b, (((ca,), (cb,)), ((), ())), precision=lax.Precision.HIGHEST, preferred_element_type=F32
    )


def packed_blocks():
    out = []
    for j in range(4):
        out.append((0, j, LROW, j, 128, 0))
    for lane, (i, j) in enumerate(((1, 1), (1, 2), (1, 3), (2, 2))):
        out.append((i, j, LROW + 128, lane, 128, 0))
    for lane, (i, j, r) in enumerate(((2, 3, 0), (2, 3, 64), (3, 3, 0), (3, 3, 64))):
        out.append((i, j, LROW + 256, lane, 64, r))
    return out


def pack_spread(ref, full):
    for i, j, row, lane, rows, r0 in packed_blocks():
        ref[row : row + rows, lane * B : lane * B + B] = full(i * B + r0, rows, j * B)


def unpack_spread(load, full_ref):
    for i, j, row, lane, rows, r0 in packed_blocks():
        block = load(row, rows, lane * B)
        full_ref[i * B + r0 : i * B + r0 + rows, j * B : j * B + B] = block
    for i in range(4):
        for j in range(i + 1, 4):
            block = full_ref[i * B : i * B + B, j * B : j * B + B]
            full_ref[j * B : j * B + B, i * B : i * B + B] = jnp.transpose(block)


def small_mul(a, b):
    return [
        [sum((a[i][t] * b[t][j] for t in range(1, len(b))), a[i][0] * b[0][j]) for j in range(len(b[0]))]
        for i in range(len(a))
    ]


def small_inverse(m):
    n = len(m)
    if n == 2:
        a, b, d = m[0][0], m[0][1], m[1][1]
        inv = 1.0 / (a * d - b * b)
        return [[d * inv, -b * inv], [-b * inv, a * inv]]
    h = n // 2
    upper = [row[h:] for row in m[:h]]
    lower = [[upper[j][i] for j in range(h)] for i in range(h)]
    first = small_inverse([row[:h] for row in m[:h]])
    q = small_mul(lower, first)
    qb = small_mul(q, upper)
    schur = [[m[h + min(i, j)][h + max(i, j)] - qb[min(i, j)][max(i, j)] for j in range(h)] for i in range(h)]
    second = small_inverse(schur)
    sq = small_mul(second, q)
    qsq = small_mul([[q[j][i] for j in range(h)] for i in range(h)], sq)
    out = [[None] * n for _ in range(n)]
    for i in range(h):
        for j in range(h):
            out[i][j] = first[i][j] + qsq[i][j]
            out[h + i][h + j] = second[i][j]
            out[h + i][j] = out[j][h + i] = -sq[i][j]
    return out


PANEL = 64


def inverse128(block):
    groups = PANEL // 8
    row_id = lax.broadcasted_iota(jnp.int32, (8, B), 0)
    lane_id = lax.broadcasted_iota(jnp.int32, (8, B), 1)
    lanes = lax.broadcasted_iota(jnp.int32, (B, B), 1)

    def body(_, x):
        top = x[:PANEL, :]
        vs = [x[8 * k : 8 * k + 8, :] for k in range(groups)]
        for q in range(groups):
            at = 8 * q
            cols = [[jnp.broadcast_to(v[:, at + s : at + s + 1], (8, B)) for v in vs] for s in range(8)]
            rows = [jnp.broadcast_to(vs[q][s : s + 1, :], (8, B)) for s in range(8)]
            m = [[None] * 8 for _ in range(8)]
            for s in range(8):
                for t in range(s, 8):
                    m[s][t] = m[t][s] = jnp.broadcast_to(cols[s][q][t : t + 1, :], (8, B))
            inv = small_inverse(m)
            new_rows = [n[0] for n in small_mul(inv, [[r] for r in rows])]
            for s in range(8):
                for t in range(8):
                    new_rows[s] = jnp.where(lane_id == at + t, -inv[s][t], new_rows[s])
            inside = (lane_id >= at) & (lane_id < at + 8)
            for k in range(groups):
                if k == q:
                    new = new_rows[0]
                    for s in range(1, 8):
                        new = jnp.where(row_id == s, new_rows[s], new)
                else:
                    new = jnp.where(inside, 0.0, vs[k])
                    new -= sum((cols[s][k] * new_rows[s] for s in range(1, 8)), cols[0][k] * new_rows[0])
                vs[k] = new
        done = jnp.concatenate(vs, axis=0)
        rest = jnp.where(lanes < PANEL, 0.0, x) - dot6(top, done, 0, 0)
        return pltpu.roll(jnp.concatenate([rest[PANEL:, :], done], axis=0), B - PANEL, 1)

    return -lax.fori_loop(0, B // PANEL, body, block)


def element_kernel(pattern, cov_in, mean_a, mean_b, noise, blocks, out, left, pred, sol, upd, cov, inv_ref):
    y, x, c, z = (lax.axis_index(a) for a in ("tm_0", "tm_1", "tm_2", "state"))
    for i in range(4):
        for t in range(3):
            lanes = slice((i + t) % 4 * B, (i + t) % 4 * B + B)
            cov[i * B : i * B + B, lanes] = cov_in[i, :, lanes]
        j = (i + 3) % 4
        cov[i * B : i * B + B, j * B : j * B + B] = jnp.transpose(cov_in[j, :, i * B : i * B + B])
    tb = lambda r, j: blocks[r, j]

    def rows_of(ref, block):
        return ref[pl.ds(pl.multiple_of(block * B, B), B), :]

    def lanes_of(ref, row, rows, block):
        return ref[row : row + rows, pl.ds(pl.multiple_of(block * B, B), B)]

    place = lax.rem(2 * z + c, 4)
    mean = jnp.where(z // 2 == c, mean_a[pl.ds(place, 1), :], mean_b[pl.ds(place, 1), :])
    upd[0:8, :] = jnp.broadcast_to(mean, (8, N))
    pushed = []
    for r in range(4):
        t0, t1 = tb(r, 0), tb(r, 1)
        left[r * B : r * B + B, :] = dot6(t0, rows_of(cov, pattern[r, 0])) + dot6(
            t1, rows_of(cov, pattern[r, 1])
        )
        pushed.append(
            dot6(lanes_of(upd, 0, 8, pattern[r, 0]), t0, 1)
            + dot6(lanes_of(upd, 0, 8, pattern[r, 1]), t1, 1)
        )
    pushed = jnp.concatenate(pushed, axis=1)
    eye = lax.broadcasted_iota(jnp.int32, (B, B), 0) == lax.broadcasted_iota(jnp.int32, (B, B), 1)
    for r in range(4):
        rows = (r + 1) * B
        value = dot6(lanes_of(left, 0, rows, pattern[r, 0]), tb(r, 0), 1) + dot6(
            lanes_of(left, 0, rows, pattern[r, 1]), tb(r, 1), 1
        )
        pred[0:rows, r * B : r * B + B] = value
        q = jnp.where(eye, jnp.broadcast_to(noise[0:1, r * B : r * B + B], (B, B)), 0.0)
        pred[r * B : rows, r * B : r * B + B] += q
    sol[...] = left[...]

    def eliminate(k, _):
        at = pl.ds(pl.multiple_of(k * B, B), B)
        inv_ref[...] = inverse128(pred[at, at])
        for kk in range(4):

            @pl.when(k == kk)
            def _():
                k0, k1 = kk * B, kk * B + B
                inv = inv_ref[...]
                ub = dot6(inv, sol[k0:k1, :])
                sol[k0:k1, :] = ub
                if kk < 3:
                    tail = pred[k0:k1, k1:]
                    ut = dot6(inv, tail)
                    st = jnp.transpose(tail)
                    pred[k1:, k1:] -= dot6(st, ut)
                    sol[k1:, :] -= dot6(st, ub)
                    pred[k0:k1, k1:] = ut

        return 0

    lax.fori_loop(0, 4, eliminate, 0)
    for k in (2, 1, 0):
        k0, k1 = k * B, k * B + B
        sol[k0:k1, :] -= dot6(pred[k0:k1, k1:], sol[k1:, :])
    keep = (8 * (4 * y + x) + 2 * z + c != 127).astype(F32)
    for i in range(4):
        for j in range(4):
            out[i * B : i * B + B, j * B : j * B + B] = (
                jnp.transpose(sol[j * B : j * B + B, i * B : i * B + B]) * keep
            )
    out[GROW : GROW + 8, :] = jnp.broadcast_to(mean, (8, N)) - keep * dot6(pushed, sol[...])
    out[GROW + 8 :, :] = jnp.zeros((ROWS - GROW - 8, N), F32)
    pred[...] = cov[...] - dot6(out[0:N, :], left[...])
    pack_spread(out, lambda r, n, c: pred[r : r + n, c : c + B])


def suffixes(count, me, own, other, total, rest, work, ready=lambda part: None, done=lambda part: None):
    se, sl, sg, rh, rl, eh, el, lk = work

    def load(k, row, rows, lane=0, lanes=N):
        return jnp.where(k == me, own[row : row + rows, lane : lane + lanes], other(k, row, rows, lane, lanes))

    last, steps = count - 1, count - 1

    def split_into(high, low, value):
        for r in range(4):
            rows = slice(r * B, r * B + B)
            high[rows, :], low[rows, :] = split(value(rows))

    if rest is not None:

        @pl.when(me == last)
        def _():
            same = lax.broadcasted_iota(jnp.int32, (N, N), 0) == lax.broadcasted_iota(jnp.int32, (N, N), 1)
            rest[0:N, :] = same.astype(F32)
            rest[N:, :] = jnp.zeros((ROWS - N, N), F32)

    def gains(t, _):
        k = last - 1 - t
        now = lax.rem(t, 2)
        if rest is not None:

            @pl.when(k == me)
            def _():
                rest[0:N, :] = se[now]

        split_into(eh.at[k], el.at[k], lambda rows: load(k, rows.start, B))
        split_into(rh, rl, lambda rows: se[now, rows, :])
        se[1 - now] = dot_s((eh[k], el[k]), (rh[...], rl[...]))
        return 0

    ready(0)
    if total is not None:
        se[0] = load(last, 0, N)
        lax.fori_loop(0, steps, gains, 0)
        total[0:N, :] = se[steps % 2]
        done(0)
    else:

        def just_split(t, _):
            k = last - 1 - t
            split_into(eh.at[k], el.at[k], lambda rows: load(k, rows.start, B))
            return 0

        lax.fori_loop(0, steps, just_split, 0)
    ready(1)
    unpack_spread(lambda r, n, c: load(last, r, n, c, B), sl.at[0])
    sg[0] = load(last, GROW, 8)

    def keep(ref, slot):
        pack_spread(ref, lambda r, n, c: sl[slot, r : r + n, c : c + B])
        ref[GROW : GROW + 8, :] = sg[slot]
        ref[GROW + 8 :, :] = jnp.zeros((ROWS - GROW - 8, N), F32)

    def spreads(t, _):
        k = last - 1 - t
        now = lax.rem(t, 2)
        if rest is not None:

            @pl.when(k == me)
            def _():
                keep(rest, now)

        split_into(rh, rl, lambda rows: sl[now, rows, :])
        unpack_spread(lambda r, n, c: load(k, r, n, c, B), lk)
        e = (eh[k], el[k])
        sg[1 - now] = dot_s(split(sg[now]), e, 1) + load(k, GROW, 8)
        half = split(dot_s(e, (rh[...], rl[...])))
        sl[1 - now] = dot_s(half, e, 1) + lk[...]
        return 0

    lax.fori_loop(0, steps, spreads, 0)
    if total is not None:
        keep(total, steps % 2)
        done(1)


def scan_kernel(own, others, rest, *work):
    suffixes(
        4,
        lax.axis_index("tm_0"),
        own,
        lambda k, row, rows, lane, lanes: others[k, row : row + rows, lane : lane + lanes],
        None,
        rest,
        work,
    )


def apply_kernel(later, across, down, pair, own, out, mean_out, cov, mean, add, w, eh, el, lk):
    unpack_spread(lambda r, n, c: later[r : r + n, c : c + B], cov)
    mean[...] = later[GROW : GROW + 8, :]

    def take(load):
        for r in range(4):
            rows = slice(r * B, r * B + B)
            h, l = split(load(r * B, B))
            eh[rows, :], el[rows, :] = h, l
        unpack_spread(lambda r, n, c: load(r, n, c, B), lk)
        add[...] = load(GROW, 8)

    loads = (
        lambda r, n, c=0, m=N: across[r : r + n, c : c + m],
        lambda r, n, c=0, m=N: down[r : r + n, c : c + m],
        lambda r, n, c=0, m=N: jnp.where(
            lax.axis_index("tm_2") == 0, pair[r : r + n, c : c + m], own[r : r + n, c : c + m]
        ),
    )

    def push(t, _):
        for k in range(3):
            pl.when(t == k)(partial(take, loads[k]))
        for r in range(4):
            rows = slice(r * B, r * B + B)
            h, l = split(cov[rows, :])
            w[0, rows, :], w[1, rows, :] = h, l
        e = (eh[...], el[...])
        mean[...] = dot_s(split(mean[...]), e, 1) + add[...]
        cov[...] = dot_s(split(dot_s(e, (w[0], w[1]))), e, 1) + lk[...]
        return 0

    lax.fori_loop(0, 3, push, 0)
    for z in range(4):
        out[z] = cov[z * B : z * B + B, :]
    mean_out[...] = mean[...]


def greet(peers):
    barrier = pltpu.get_barrier_semaphore()
    for peer in peers:
        pl.semaphore_signal(barrier, inc=1, device_id=peer, device_id_type=MESH)
    pl.semaphore_wait(barrier, len(peers))


def column_peers(z, c):
    return [
        {"state": lax.rem(z + dz, 4), "tm_2": c if dc == 0 else 1 - c}
        for dz in range(4)
        for dc in range(2)
        if dz or dc
    ]


def remote(src, dst, send, recv, peer):
    return pltpu.make_async_remote_copy(
        src_ref=src, dst_ref=dst, send_sem=send, recv_sem=recv, device_id=peer, device_id_type=MESH
    )


def lanes_of_block(ref, j):
    return ref.at[:, pl.ds(pl.multiple_of(lax.rem(j, 4) * B, B), B)]


def gather_step_kernel(cov, mean, out, mean_out, relay, send, recv, relay_send, relay_recv, local, msend, mrecv):
    z, c = lax.axis_index("state"), lax.axis_index("tm_2")
    greet(column_peers(z, c))
    other = remote(mean, mean_out, msend, mrecv, {"tm_2": 1 - c})
    other.start()

    def start(src, dst, row, ssem, rsem, peer):
        for t in range(3):
            remote(lanes_of_block(src, row + t), lanes_of_block(dst, row + t), ssem, rsem, peer).start()

    def whole(ref, ssem, rsem):
        part = ref.at[:, 0 : 3 * B]
        return remote(part, part, ssem, rsem, {"state": 0, "tm_2": 0})

    def target(i):
        dz, e = 2 * c + i // 2, i % 2
        mine = (z == dz) & (c == e)
        far = lax.rem(dz + 4 - z, 4) == 2
        return dz, e, mine, far

    for i in range(4):
        dz, e, mine, far = target(i)

        @pl.when(far)
        def _():
            start(cov.at[i], relay.at[e], z, send.at[i], relay_recv.at[e], {"state": lax.rem(z + (3 if e else 1), 4)})

    for i in range(4):
        dz, e, mine, far = target(i)

        @pl.when(mine)
        def _():
            pltpu.make_async_copy(cov.at[i], out.at[z], local).start()

        @pl.when(jnp.logical_not(mine | far))
        def _():
            start(cov.at[i], out.at[z], z, send.at[i], recv.at[z], {"state": dz, "tm_2": e})

    duties = []
    for e in range(2):
        source, dz = lax.rem(z + (1 if e else 3), 4), lax.rem(z + (3 if e else 1), 4)
        duty = source // 2 != c
        duties.append(duty)

        @pl.when(duty)
        def _():
            whole(relay.at[e], send.at[0], relay_recv.at[e]).wait_recv()
            start(relay.at[e], out.at[source], source, relay_send.at[e], recv.at[source], {"state": dz, "tm_2": e})

    for i in range(4):
        dz, e, mine, far = target(i)

        @pl.when(mine)
        def _():
            pltpu.make_async_copy(cov.at[i], out.at[z], local).wait()

        @pl.when(jnp.logical_not(mine))
        def _():
            whole(cov.at[i], send.at[i], recv.at[0]).wait_send()

    for e in range(2):

        @pl.when(duties[e])
        def _():
            whole(relay.at[e], relay_send.at[e], recv.at[0]).wait_send()

    source_core = z // 2
    for s in range(4):

        @pl.when(jnp.logical_not((z == s) & (c == source_core)))
        def _():
            whole(out.at[s], send.at[0], recv.at[s]).wait_recv()

    other.wait()


def scatter_step_kernel(slabs, mean, out, mean_out, relay, send, recv, relay_send, relay_recv, local, msend, mrecv):
    z, c = lax.axis_index("state"), lax.axis_index("tm_2")
    greet(column_peers(z, c))
    core = z // 2
    slot = 2 * lax.rem(z, 2) + c
    opposite = lax.rem(z + 2, 4)
    onward = lax.rem(z + 1 + 2 * c, 4)
    far = remote(slabs.at[opposite], relay, relay_send.at[0], relay_recv, {"state": onward})
    far.start()

    def copy(t):
        return remote(slabs.at[t], out.at[slot], send.at[t], recv.at[slot], {"state": t, "tm_2": core})

    def mean_copy(t):
        return remote(mean, mean_out.at[slot], msend.at[t], mrecv.at[slot], {"state": t, "tm_2": core})

    def mine(t):
        return (z == t) & (c == core)

    def copies(t):
        return pltpu.make_async_copy(slabs.at[t], out.at[slot], local.at[0]), pltpu.make_async_copy(
            mean, mean_out.at[slot], local.at[1]
        )

    for t in range(4):

        @pl.when(mine(t))
        def _():
            for copy_here in copies(t):
                copy_here.start()

        @pl.when(jnp.logical_not(mine(t)))
        def _():
            mean_copy(t).start()

        @pl.when(jnp.logical_not(mine(t)) & (t != opposite))
        def _():
            copy(t).start()

    source = lax.rem(z + 3 + 2 * c, 4)
    far.wait_recv()
    on = remote(
        relay,
        out.at[2 * lax.rem(source, 2) + c],
        relay_send.at[1],
        recv.at[2 * lax.rem(source, 2) + c],
        {"state": onward, "tm_2": source // 2},
    )
    on.start()
    for t in range(4):

        @pl.when(mine(t))
        def _():
            for copy_here in copies(t):
                copy_here.wait()

        @pl.when(jnp.logical_not(mine(t)))
        def _():
            mean_copy(t).wait_send()

        @pl.when(jnp.logical_not(mine(t)) & (t != opposite))
        def _():
            copy(t).wait_send()

    far.wait_send()
    on.wait_send()
    for i in range(4):

        @pl.when(jnp.logical_not((z == 2 * c + i // 2) & (c == i % 2)))
        def _():
            remote(slabs.at[0], out.at[i], send.at[0], recv.at[i], {"state": 0, "tm_2": 0}).wait_recv()
            remote(mean, mean_out.at[i], msend.at[0], mrecv.at[i], {"state": 0, "tm_2": 0}).wait_recv()


class Copies:
    def __init__(self, out, send, recv):
        self.out, self.send, self.recv, self.used, self.sent = out, send, recv, 0, []

    def put(self, peer, slot, row, rows, src=None):
        n, self.used = self.used, self.used + 1
        place = self.out.at[slot, pl.ds(pl.multiple_of(row, 8), rows), :]
        copy = remote(place if src is None else src, place, self.send.at[n], self.recv.at[n], peer)
        copy.start()
        self.sent.append(copy)
        return n

    def arrived(self, n, slot, row, rows):
        place = self.out.at[slot, pl.ds(pl.multiple_of(row, 8), rows), :]
        remote(place, place, self.send.at[n], self.recv.at[n], {"tm_2": 0}).wait_recv()

    def finish(self):
        for copy in self.sent:
            copy.wait_send()


Z_PIECES = (((0, 64), (64, 64), (128, 64), (192, 64)), ((0, 48), (48, 40), (88, 40), (128, 40)))
Z_HALF = (256, 168)


def pair_kernel(own, total, out, twin_buf, *refs):
    work, (swap_send, swap_recv, send, recv) = refs[:8], refs[8:]
    z, c = lax.axis_index("state"), lax.axis_index("tm_2")
    zu, zd, zo = lax.rem(z + 1, 4), lax.rem(z + 3, 4), lax.rem(z + 2, 4)
    up, down, twin = {"state": zu}, {"state": zd}, {"tm_2": 1 - c}
    greet([up, down, twin])
    swaps = []
    for part, rows in ((0, pl.ds(0, N)), (1, pl.ds(N, ROWS - N))):
        swaps.append(remote(own.at[rows], twin_buf.at[rows], swap_send.at[part], swap_recv.at[part], twin))
        swaps[part].start()
    cp = Copies(out, send, recv)
    ups, downs, tails, twins = [], [], [], []

    def rows_of(part, core, piece):
        return (N if part else 0) + core * Z_HALF[part] + piece[0], piece[1]

    def first_hop(part):
        pieces = Z_PIECES[part]
        for j, (a, b) in enumerate(zip(pieces, pieces[::-1])):
            for into, peer, piece in ((ups, up, a), (downs, down, b)):
                row, rows = rows_of(part, c, piece)
                n = cp.put(peer, z, row, rows, total.at[pl.ds(pl.multiple_of(row, 8), rows), :])
                into.append((n, part, piece, j < len(pieces) // 2))

    suffixes(
        2,
        c,
        own,
        lambda k, row, rows, lane, lanes: twin_buf[row : row + rows, lane : lane + lanes],
        total,
        None,
        work,
        lambda part: swaps[part].wait(),
        first_hop,
    )

    def hand(slot, part, piece):
        row, rows = rows_of(part, c, piece)
        twins.append((cp.put(twin, slot, row, rows), slot, rows_of(part, 1 - c, piece)))

    for pair in zip(ups, downs):
        for (n, part, piece, further), slot, peer in zip(pair, (zd, zu), (up, down)):
            row, rows = rows_of(part, c, piece)
            cp.arrived(n, slot, row, rows)
            if further:
                tails.append((cp.put(peer, slot, row, rows), part, piece))
            hand(slot, part, piece)
    for n, part, piece in tails:
        row, rows = rows_of(part, c, piece)
        cp.arrived(n, zo, row, rows)
        hand(zo, part, piece)
    for n, slot, (row, rows) in twins:
        cp.arrived(n, slot, row, rows)
    cp.finish()


R_PIECES = (((0, 32), (32, 32)), ((0, 24), (24, 24)))
R_EIGHTH = (64, 48)


def ring_kernel(mine, axis, own, others, rest, out, total, *refs):
    work, (send, recv) = refs[:8], refs[8:]
    z, c, a = lax.axis_index("state"), lax.axis_index("tm_2"), lax.axis_index(axis)
    zu, zd, zo = lax.rem(z + 1, 4), lax.rem(z + 3, 4), lax.rem(z + 2, 4)
    au, ad, ao = lax.rem(a + 1, 4), lax.rem(a + 3, 4), lax.rem(a + 2, 4)
    up, down = {axis: au}, {axis: ad}
    above, below, twin = {"state": zu}, {"state": zd}, {"tm_2": 1 - c}
    peers = [up, down, above, below, twin]
    barrier = pltpu.get_barrier_semaphore()
    for peer in peers:
        pl.semaphore_signal(barrier, inc=1, device_id=peer, device_id_type=MESH)
    cp = Copies(out, send, recv)
    quarters = (z, zu)
    coming = (zd, zo)
    ups, downs, twins, zs, tails = [], [], [], [], []

    def rows_of(part, quarter, core, piece):
        return (N if part else 0) + (2 * quarter + core) * R_EIGHTH[part] + piece[0], piece[1]

    def first_hop(part):
        if part == 0:
            pl.semaphore_wait(barrier, len(peers))
        pieces = R_PIECES[part]
        for j, pair in enumerate(zip(pieces, pieces[::-1])):
            for k in (0, 1):
                for into, peer, piece in zip((ups, downs), (up, down), pair):
                    row, rows = rows_of(part, quarters[k], c, piece)
                    n = cp.put(peer, a, row, rows, total.at[pl.ds(pl.multiple_of(row, 8), rows), :])
                    into.append((n, part, k, piece, j < len(pieces) // 2))

    suffixes(
        4,
        lax.axis_index(mine),
        own,
        lambda k, row, rows, lane, lanes: others[k, row : row + rows, lane : lane + lanes],
        total,
        rest,
        work,
        done=first_hop,
    )

    def spread(slot, part, k, piece):
        row, rows = rows_of(part, quarters[k], c, piece)
        zs.append((cp.put(below if k else above, slot, row, rows), slot, part, k, piece))
        twins.append((cp.put(twin, slot, row, rows), slot, rows_of(part, quarters[k], 1 - c, piece)))

    def take(count):
        while len(zs) > count:
            n, slot, part, k, piece = zs.pop(0)
            row, rows = rows_of(part, coming[k], c, piece)
            cp.arrived(n, slot, row, rows)
            twins.append((cp.put(twin, slot, row, rows), slot, rows_of(part, coming[k], 1 - c, piece)))

    for pair in zip(ups, downs):
        for (n, part, k, piece, further), slot, peer in zip(pair, (ad, au), (up, down)):
            row, rows = rows_of(part, quarters[k], c, piece)
            cp.arrived(n, slot, row, rows)
            if further:
                tails.append((cp.put(peer, slot, row, rows), part, k, piece))
            spread(slot, part, k, piece)
    for n, part, k, piece in tails:
        row, rows = rows_of(part, quarters[k], c, piece)
        cp.arrived(n, ao, row, rows)
        spread(ao, part, k, piece)
        take(len(zs) - 2)
    take(0)
    for n, slot, (row, rows) in twins:
        cp.arrived(n, slot, row, rows)
    cp.finish()


def shape(*dims, dtype=F32):
    return jax.ShapeDtypeStruct(dims, dtype)


def params(limit=None, **more):
    return pltpu.CompilerParams(vmem_limit_bytes=limit, **more)


DMA = pltpu.SemaphoreType.DMA


def comm(kernel, name, collective_id, outs, scratch, *args, out_spec=ANY):
    return pl.pallas_call(
        kernel,
        name=name,
        out_shape=outs,
        in_specs=[ANY] * len(args),
        out_specs=jax.tree.map(lambda _: out_spec, outs),
        scratch_shapes=scratch,
        compiler_params=pltpu.CompilerParams(
            collective_id=collective_id, has_side_effects=True, vmem_limit_bytes=4 * 1024 * 1024
        ),
    )(*args)


BIG = 32 * 1024 * 1024
WORK = [
    pltpu.VMEM((512, 512), BF16),
    pltpu.VMEM((512, 512), BF16),
    pltpu.VMEM((512, 512), F32),
]


def suffix_work(count):
    return [
        pltpu.VMEM((2, N, N), F32),
        pltpu.VMEM((2, N, N), F32),
        pltpu.VMEM((2, 8, N), F32),
        pltpu.VMEM((N, N), BF16),
        pltpu.VMEM((N, N), BF16),
        pltpu.VMEM((count - 1, N, N), BF16),
        pltpu.VMEM((count - 1, N, N), BF16),
        pltpu.VMEM((N, N), F32),
    ]


def ring(name, collective_id, mine, axis, own, others):
    packet = shape(ROWS, N)
    return pl.pallas_call(
        partial(ring_kernel, mine, axis),
        name=name,
        out_shape=(packet, shape(4, ROWS, N), packet),
        in_specs=[VM, VM],
        out_specs=(VM, VM, VM),
        scratch_shapes=suffix_work(4) + [DMA((96,)), DMA((96,))],
        compiler_params=params(RING_LIMIT, collective_id=collective_id, has_side_effects=True),
    )(own, others)


RING_LIMIT = 24 * 1024 * 1024


def on_device(filtered_cov, filtered_mean, noise_var, trans_blocks, pattern):
    z = lax.axis_index("state")
    cov, twin_mean = comm(
        gather_step_kernel,
        "gather_step",
        0,
        (shape(4, B, N), shape(4, N)),
        [pltpu.VMEM((2, B, N), F32), DMA((4,)), DMA((4,)), DMA((2,)), DMA((2,)), DMA, DMA, DMA],
        filtered_cov,
        filtered_mean,
        out_spec=VM,
    )
    own = pl.pallas_call(
        element_kernel,
        name="element",
        out_shape=shape(ROWS, N),
        in_specs=[SM] + [VM] * 5,
        out_specs=VM,
        scratch_shapes=[pltpu.VMEM((N, N), F32)] * 3 + [pltpu.VMEM((8, N), F32), pltpu.VMEM((N, N), F32), pltpu.VMEM((B, B), F32)],
        compiler_params=params(BIG),
    )(pattern, cov, filtered_mean, twin_mean, noise_var.reshape(1, N), trans_blocks)
    packet, packets = shape(ROWS, N), shape(4, ROWS, N)
    pair, pairs = pl.pallas_call(
        pair_kernel,
        name="pair",
        out_shape=(packet, packets),
        in_specs=[VM],
        out_specs=(VM, VM),
        scratch_shapes=[pltpu.VMEM((ROWS, N), F32)] + suffix_work(2) + [DMA((2,)), DMA((2,)), DMA((48,)), DMA((48,))],
        compiler_params=params(RING_LIMIT, collective_id=2, has_side_effects=True),
    )(own)
    down, columns, column = ring("ring_x", 3, "state", "tm_1", pair, pairs)
    across, rows, row = ring("ring_y", 4, "tm_1", "tm_0", column, columns)
    later = pl.pallas_call(
        scan_kernel,
        name="scan_y",
        out_shape=packet,
        in_specs=[VM, VM],
        out_specs=VM,
        scratch_shapes=suffix_work(4),
        compiler_params=params(BIG),
    )(row, rows)
    slabs, mean = pl.pallas_call(
        apply_kernel,
        name="apply",
        out_shape=(shape(4, B, N), shape(8, N)),
        in_specs=[VM] * 5,
        out_specs=(VM, VM),
        scratch_shapes=[pltpu.VMEM((N, N), F32), pltpu.VMEM((8, N), F32), pltpu.VMEM((8, N), F32), pltpu.VMEM((2, N, N), BF16)]
        + WORK,
        compiler_params=params(BIG),
    )(later, across, down, pair, own)
    smooth_cov, means = comm(
        scatter_step_kernel,
        "scatter_step",
        5,
        (shape(4, B, N), shape(4, 8, N)),
        [pltpu.VMEM((B, N), F32), DMA((4,)), DMA((4,)), DMA((2,)), DMA, DMA((2,)), DMA((4,)), DMA((4,))],
        slabs,
        mean,
        out_spec=VM,
    )
    return lax.dynamic_slice_in_dim(means[:, 0, :], z * B, B, 1), smooth_cov


def solution(mesh):
    torus = Mesh(
        mesh.devices.reshape(4, 4, 2, mesh.shape["state"]), ("tm_0", "tm_1", "tm_2", "state")
    )
    return jax.shard_map(
        on_device,
        mesh=torus,
        in_specs=(P(TM, "state", None), P(TM, None), P(), P(), P()),
        out_specs=(P(TM, "state"), P(TM, "state", None)),
        check_vma=False,
    )
```

```python
from functools import partial

import jax
import jax.numpy as jnp
from jax import lax
from jax.experimental import pallas as pl
from jax.experimental.pallas import tpu as pltpu
from jax.sharding import Mesh
from jax.sharding import PartitionSpec as P

N = 512
B = 128
LROW = 512
GROW = 832
ROWS = 896
MESH = pl.DeviceIdType.MESH
F32 = jnp.float32
BF16 = jnp.bfloat16
ANY = pl.BlockSpec(memory_space=pl.ANY)
VM = pl.BlockSpec(memory_space=pltpu.VMEM)
SM = pl.BlockSpec(memory_space=pltpu.SMEM)
TM = ("tm_0", "tm_1", "tm_2")


def split(x):
    high = x.astype(BF16)
    return high, (x - high.astype(F32)).astype(BF16)


def dg(a, b, cb=0):
    return lax.dot_general(a, b, (((1,), (cb,)), ((), ())), preferred_element_type=F32)


def dot_s(a, b, cb=0):
    return dg(a[0], b[0], cb) + (dg(a[0], b[1], cb) + dg(a[1], b[0], cb))


def dot3(a, b, cb=0):
    return dot_s(split(a), split(b), cb)


def dot6(a, b, cb=0, ca=1):
    return lax.dot_general(
        a, b, (((ca,), (cb,)), ((), ())), precision=lax.Precision.HIGHEST, preferred_element_type=F32
    )


def packed_blocks():
    out = []
    for j in range(4):
        out.append((0, j, LROW, j, 128, 0))
    for lane, (i, j) in enumerate(((1, 1), (1, 2), (1, 3), (2, 2))):
        out.append((i, j, LROW + 128, lane, 128, 0))
    for lane, (i, j, r) in enumerate(((2, 3, 0), (2, 3, 64), (3, 3, 0), (3, 3, 64))):
        out.append((i, j, LROW + 256, lane, 64, r))
    return out


def pack_spread(ref, full):
    for i, j, row, lane, rows, r0 in packed_blocks():
        ref[row : row + rows, lane * B : lane * B + B] = full(i * B + r0, rows, j * B)


def unpack_spread(load, full_ref):
    for i, j, row, lane, rows, r0 in packed_blocks():
        block = load(row, rows, lane * B)
        full_ref[i * B + r0 : i * B + r0 + rows, j * B : j * B + B] = block
    for i in range(4):
        for j in range(i + 1, 4):
            block = full_ref[i * B : i * B + B, j * B : j * B + B]
            full_ref[j * B : j * B + B, i * B : i * B + B] = jnp.transpose(block)


def small_mul(a, b):
    return [
        [sum((a[i][t] * b[t][j] for t in range(1, len(b))), a[i][0] * b[0][j]) for j in range(len(b[0]))]
        for i in range(len(a))
    ]


def small_inverse(m):
    n = len(m)
    if n == 2:
        a, b, d = m[0][0], m[0][1], m[1][1]
        inv = 1.0 / (a * d - b * b)
        return [[d * inv, -b * inv], [-b * inv, a * inv]]
    h = n // 2
    upper = [row[h:] for row in m[:h]]
    lower = [[upper[j][i] for j in range(h)] for i in range(h)]
    first = small_inverse([row[:h] for row in m[:h]])
    q = small_mul(lower, first)
    qb = small_mul(q, upper)
    schur = [[m[h + min(i, j)][h + max(i, j)] - qb[min(i, j)][max(i, j)] for j in range(h)] for i in range(h)]
    second = small_inverse(schur)
    sq = small_mul(second, q)
    qsq = small_mul([[q[j][i] for j in range(h)] for i in range(h)], sq)
    out = [[None] * n for _ in range(n)]
    for i in range(h):
        for j in range(h):
            out[i][j] = first[i][j] + qsq[i][j]
            out[h + i][h + j] = second[i][j]
            out[h + i][j] = out[j][h + i] = -sq[i][j]
    return out


PANEL = 64


def inverse128(block):
    groups = PANEL // 8
    row_id = lax.broadcasted_iota(jnp.int32, (8, B), 0)
    lane_id = lax.broadcasted_iota(jnp.int32, (8, B), 1)
    lanes = lax.broadcasted_iota(jnp.int32, (B, B), 1)

    def body(_, x):
        top = x[:PANEL, :]
        vs = [x[8 * k : 8 * k + 8, :] for k in range(groups)]
        for q in range(groups):
            at = 8 * q
            cols = [[jnp.broadcast_to(v[:, at + s : at + s + 1], (8, B)) for v in vs] for s in range(8)]
            rows = [jnp.broadcast_to(vs[q][s : s + 1, :], (8, B)) for s in range(8)]
            m = [[None] * 8 for _ in range(8)]
            for s in range(8):
                for t in range(s, 8):
                    m[s][t] = m[t][s] = jnp.broadcast_to(cols[s][q][t : t + 1, :], (8, B))
            inv = small_inverse(m)
            new_rows = [n[0] for n in small_mul(inv, [[r] for r in rows])]
            for s in range(8):
                for t in range(8):
                    new_rows[s] = jnp.where(lane_id == at + t, -inv[s][t], new_rows[s])
            inside = (lane_id >= at) & (lane_id < at + 8)
            for k in range(groups):
                if k == q:
                    new = new_rows[0]
                    for s in range(1, 8):
                        new = jnp.where(row_id == s, new_rows[s], new)
                else:
                    new = jnp.where(inside, 0.0, vs[k])
                    new -= sum((cols[s][k] * new_rows[s] for s in range(1, 8)), cols[0][k] * new_rows[0])
                vs[k] = new
        done = jnp.concatenate(vs, axis=0)
        rest = jnp.where(lanes < PANEL, 0.0, x) - dot6(top, done, 0, 0)
        return pltpu.roll(jnp.concatenate([rest[PANEL:, :], done], axis=0), B - PANEL, 1)

    return -lax.fori_loop(0, B // PANEL, body, block)


def element_kernel(pattern, cov_in, mean_a, mean_b, noise, blocks, out, left, pred, sol, upd, cov, inv_ref):
    y, x, c, z = (lax.axis_index(a) for a in ("tm_0", "tm_1", "tm_2", "state"))
    for i in range(4):
        for t in range(3):
            lanes = slice((i + t) % 4 * B, (i + t) % 4 * B + B)
            cov[i * B : i * B + B, lanes] = cov_in[i, :, lanes]
        j = (i + 3) % 4
        cov[i * B : i * B + B, j * B : j * B + B] = jnp.transpose(cov_in[j, :, i * B : i * B + B])
    tb = lambda r, j: blocks[r, j]

    def rows_of(ref, block):
        return ref[pl.ds(pl.multiple_of(block * B, B), B), :]

    def lanes_of(ref, row, rows, block):
        return ref[row : row + rows, pl.ds(pl.multiple_of(block * B, B), B)]

    place = lax.rem(2 * z + c, 4)
    mean = jnp.where(z // 2 == c, mean_a[pl.ds(place, 1), :], mean_b[pl.ds(place, 1), :])
    upd[0:8, :] = jnp.broadcast_to(mean, (8, N))
    pushed = []
    for r in range(4):
        t0, t1 = tb(r, 0), tb(r, 1)
        left[r * B : r * B + B, :] = dot6(t0, rows_of(cov, pattern[r, 0])) + dot6(
            t1, rows_of(cov, pattern[r, 1])
        )
        pushed.append(
            dot6(lanes_of(upd, 0, 8, pattern[r, 0]), t0, 1)
            + dot6(lanes_of(upd, 0, 8, pattern[r, 1]), t1, 1)
        )
    pushed = jnp.concatenate(pushed, axis=1)
    eye = lax.broadcasted_iota(jnp.int32, (B, B), 0) == lax.broadcasted_iota(jnp.int32, (B, B), 1)
    for r in range(4):
        rows = (r + 1) * B
        value = dot6(lanes_of(left, 0, rows, pattern[r, 0]), tb(r, 0), 1) + dot6(
            lanes_of(left, 0, rows, pattern[r, 1]), tb(r, 1), 1
        )
        pred[0:rows, r * B : r * B + B] = value
        q = jnp.where(eye, jnp.broadcast_to(noise[0:1, r * B : r * B + B], (B, B)), 0.0)
        pred[r * B : rows, r * B : r * B + B] += q
    sol[...] = left[...]

    def eliminate(k, _):
        at = pl.ds(pl.multiple_of(k * B, B), B)
        inv_ref[...] = inverse128(pred[at, at])
        for kk in range(4):

            @pl.when(k == kk)
            def _():
                k0, k1 = kk * B, kk * B + B
                inv = inv_ref[...]
                ub = dot6(inv, sol[k0:k1, :])
                sol[k0:k1, :] = ub
                if kk < 3:
                    tail = pred[k0:k1, k1:]
                    ut = dot6(inv, tail)
                    st = jnp.transpose(tail)
                    pred[k1:, k1:] -= dot6(st, ut)
                    sol[k1:, :] -= dot6(st, ub)
                    pred[k0:k1, k1:] = ut

        return 0

    lax.fori_loop(0, 4, eliminate, 0)
    for k in (2, 1, 0):
        k0, k1 = k * B, k * B + B
        sol[k0:k1, :] -= dot6(pred[k0:k1, k1:], sol[k1:, :])
    keep = (8 * (4 * y + x) + 2 * z + c != 127).astype(F32)
    for i in range(4):
        for j in range(4):
            out[i * B : i * B + B, j * B : j * B + B] = (
                jnp.transpose(sol[j * B : j * B + B, i * B : i * B + B]) * keep
            )
    out[GROW : GROW + 8, :] = jnp.broadcast_to(mean, (8, N)) - keep * dot6(pushed, sol[...])
    out[GROW + 8 :, :] = jnp.zeros((ROWS - GROW - 8, N), F32)
    pred[...] = cov[...] - dot6(out[0:N, :], left[...])
    pack_spread(out, lambda r, n, c: pred[r : r + n, c : c + B])


def split_into(high, low, value):
    for r in range(4):
        rows = slice(r * B, r * B + B)
        high[rows, :], low[rows, :] = split(value(rows))


def chosen(me, own, other):
    def load(k, row, rows, lane=0, lanes=N):
        return jnp.where(k == me, own[row : row + rows, lane : lane + lanes], other(k, row, rows, lane, lanes))

    return load


def split_gains(count, load, work):
    eh, el = work[5:7]

    def body(k, _):
        split_into(eh.at[k], el.at[k], lambda rows: load(k, rows.start, B))
        return 0

    lax.fori_loop(0, count - 1, body, 0)


def gains(count, me, load, total, rest, work):
    se, _, _, rh, rl, eh, el, _ = work
    last = count - 1
    if rest is not None:

        @pl.when(me == last)
        def _():
            same = lax.broadcasted_iota(jnp.int32, (N, N), 0) == lax.broadcasted_iota(jnp.int32, (N, N), 1)
            rest[0:N, :] = same.astype(F32)

    def step(t, _):
        k = last - 1 - t
        now = lax.rem(t, 2)
        if rest is not None:

            @pl.when(k == me)
            def _():
                rest[0:N, :] = se[now]

        split_into(eh.at[k], el.at[k], lambda rows: load(k, rows.start, B))
        split_into(rh, rl, lambda rows: se[now, rows, :])
        se[1 - now] = dot_s((eh[k], el[k]), (rh[...], rl[...]))
        return 0

    se[0] = load(last, 0, N)
    lax.fori_loop(0, last, step, 0)
    total[0:N, :] = se[last % 2]


def spreads(count, me, load, total, rest, work):
    _, sl, sg, rh, rl, eh, el, lk = work
    last = count - 1
    if rest is not None:

        @pl.when(me == last)
        def _():
            rest[N:, :] = jnp.zeros((ROWS - N, N), F32)

    unpack_spread(lambda r, n, c: load(last, r, n, c, B), sl.at[0])
    sg[0] = load(last, GROW, 8)

    def keep(ref, slot):
        pack_spread(ref, lambda r, n, c: sl[slot, r : r + n, c : c + B])
        ref[GROW : GROW + 8, :] = sg[slot]
        ref[GROW + 8 :, :] = jnp.zeros((ROWS - GROW - 8, N), F32)

    def step(t, _):
        k = last - 1 - t
        now = lax.rem(t, 2)
        if rest is not None:

            @pl.when(k == me)
            def _():
                keep(rest, now)

        split_into(rh, rl, lambda rows: sl[now, rows, :])
        unpack_spread(lambda r, n, c: load(k, r, n, c, B), lk)
        e = (eh[k], el[k])
        sg[1 - now] = dot_s(split(sg[now]), e, 1) + load(k, GROW, 8)
        half = split(dot_s(e, (rh[...], rl[...])))
        sl[1 - now] = dot_s(half, e, 1) + lk[...]
        return 0

    lax.fori_loop(0, last, step, 0)
    if total is not None:
        keep(total, last % 2)


def from_slots(others):
    return lambda k, row, rows, lane, lanes: others[k, row : row + rows, lane : lane + lanes]


def scan_kernel(own, others, rest, *work):
    me = lax.axis_index("tm_0")
    load = chosen(me, own, from_slots(others))
    split_gains(4, load, work)
    spreads(4, me, load, None, rest, work)


def apply_kernel(later, across, down, pair, own, out, mean_out, cov, mean, add, w, eh, el, lk):
    unpack_spread(lambda r, n, c: later[r : r + n, c : c + B], cov)
    mean[...] = later[GROW : GROW + 8, :]

    def take(load):
        for r in range(4):
            rows = slice(r * B, r * B + B)
            h, l = split(load(r * B, B))
            eh[rows, :], el[rows, :] = h, l
        unpack_spread(lambda r, n, c: load(r, n, c, B), lk)
        add[...] = load(GROW, 8)

    loads = (
        lambda r, n, c=0, m=N: across[r : r + n, c : c + m],
        lambda r, n, c=0, m=N: down[r : r + n, c : c + m],
        lambda r, n, c=0, m=N: jnp.where(
            lax.axis_index("tm_2") == 0, pair[r : r + n, c : c + m], own[r : r + n, c : c + m]
        ),
    )

    def push(t, _):
        for k in range(3):
            pl.when(t == k)(partial(take, loads[k]))
        for r in range(4):
            rows = slice(r * B, r * B + B)
            h, l = split(cov[rows, :])
            w[0, rows, :], w[1, rows, :] = h, l
        e = (eh[...], el[...])
        mean[...] = dot_s(split(mean[...]), e, 1) + add[...]
        cov[...] = dot_s(split(dot_s(e, (w[0], w[1]))), e, 1) + lk[...]
        return 0

    lax.fori_loop(0, 3, push, 0)
    for z in range(4):
        out[z] = cov[z * B : z * B + B, :]
    mean_out[...] = mean[...]


def greet(peers):
    barrier = pltpu.get_barrier_semaphore()
    for peer in peers:
        pl.semaphore_signal(barrier, inc=1, device_id=peer, device_id_type=MESH)
    pl.semaphore_wait(barrier, len(peers))


def column_peers(z, c):
    return [
        {"state": lax.rem(z + dz, 4), "tm_2": c if dc == 0 else 1 - c}
        for dz in range(4)
        for dc in range(2)
        if dz or dc
    ]


def remote(src, dst, send, recv, peer):
    return pltpu.make_async_remote_copy(
        src_ref=src, dst_ref=dst, send_sem=send, recv_sem=recv, device_id=peer, device_id_type=MESH
    )


def lanes_of_block(ref, j):
    return ref.at[:, pl.ds(pl.multiple_of(lax.rem(j, 4) * B, B), B)]


def gather_step_kernel(
    cov,
    mean,
    noise,
    blocks,
    out,
    mean_out,
    mean_here,
    noise_here,
    blocks_here,
    relay,
    send,
    recv,
    relay_send,
    relay_recv,
    local,
    msend,
    mrecv,
    small,
):
    z, c = lax.axis_index("state"), lax.axis_index("tm_2")
    greet(column_peers(z, c))
    other = remote(mean, mean_out, msend, mrecv, {"tm_2": 1 - c})
    other.start()
    here = [
        pltpu.make_async_copy(src, dst, small.at[n])
        for n, (src, dst) in enumerate(((mean, mean_here), (noise, noise_here), (blocks, blocks_here)))
    ]
    for copy_here in here:
        copy_here.start()

    def start(src, dst, row, ssem, rsem, peer):
        for t in range(3):
            remote(lanes_of_block(src, row + t), lanes_of_block(dst, row + t), ssem, rsem, peer).start()

    def whole(ref, ssem, rsem):
        part = ref.at[:, 0 : 3 * B]
        return remote(part, part, ssem, rsem, {"state": 0, "tm_2": 0})

    def target(i):
        dz, e = 2 * c + i // 2, i % 2
        mine = (z == dz) & (c == e)
        far = lax.rem(dz + 4 - z, 4) == 2
        return dz, e, mine, far

    for i in range(4):
        dz, e, mine, far = target(i)

        @pl.when(far)
        def _():
            start(cov.at[i], relay.at[e], z, send.at[i], relay_recv.at[e], {"state": lax.rem(z + (3 if e else 1), 4)})

    for i in range(4):
        dz, e, mine, far = target(i)

        @pl.when(mine)
        def _():
            pltpu.make_async_copy(cov.at[i], out.at[z], local).start()

        @pl.when(jnp.logical_not(mine | far))
        def _():
            start(cov.at[i], out.at[z], z, send.at[i], recv.at[z], {"state": dz, "tm_2": e})

    duties = []
    for e in range(2):
        source, dz = lax.rem(z + (1 if e else 3), 4), lax.rem(z + (3 if e else 1), 4)
        duty = source // 2 != c
        duties.append(duty)

        @pl.when(duty)
        def _():
            whole(relay.at[e], send.at[0], relay_recv.at[e]).wait_recv()
            start(relay.at[e], out.at[source], source, relay_send.at[e], recv.at[source], {"state": dz, "tm_2": e})

    for i in range(4):
        dz, e, mine, far = target(i)

        @pl.when(mine)
        def _():
            pltpu.make_async_copy(cov.at[i], out.at[z], local).wait()

        @pl.when(jnp.logical_not(mine))
        def _():
            whole(cov.at[i], send.at[i], recv.at[0]).wait_send()

    for e in range(2):

        @pl.when(duties[e])
        def _():
            whole(relay.at[e], relay_send.at[e], recv.at[0]).wait_send()

    source_core = z // 2
    for s in range(4):

        @pl.when(jnp.logical_not((z == s) & (c == source_core)))
        def _():
            whole(out.at[s], send.at[0], recv.at[s]).wait_recv()

    other.wait()
    for copy_here in here:
        copy_here.wait()


def scatter_step_kernel(slabs, mean, out, mean_out, relay, send, recv, relay_send, relay_recv, local, msend, mrecv):
    z, c = lax.axis_index("state"), lax.axis_index("tm_2")
    greet(column_peers(z, c))
    core = z // 2
    slot = 2 * lax.rem(z, 2) + c
    opposite = lax.rem(z + 2, 4)
    onward = lax.rem(z + 1 + 2 * c, 4)
    far = remote(slabs.at[opposite], relay, relay_send.at[0], relay_recv, {"state": onward})
    far.start()

    def copy(t):
        return remote(slabs.at[t], out.at[slot], send.at[t], recv.at[slot], {"state": t, "tm_2": core})

    def mean_copy(t):
        return remote(mean, mean_out.at[slot], msend.at[t], mrecv.at[slot], {"state": t, "tm_2": core})

    def mine(t):
        return (z == t) & (c == core)

    def copies(t):
        return pltpu.make_async_copy(slabs.at[t], out.at[slot], local.at[0]), pltpu.make_async_copy(
            mean, mean_out.at[slot], local.at[1]
        )

    for t in range(4):

        @pl.when(mine(t))
        def _():
            for copy_here in copies(t):
                copy_here.start()

        @pl.when(jnp.logical_not(mine(t)))
        def _():
            mean_copy(t).start()

        @pl.when(jnp.logical_not(mine(t)) & (t != opposite))
        def _():
            copy(t).start()

    source = lax.rem(z + 3 + 2 * c, 4)
    far.wait_recv()
    on = remote(
        relay,
        out.at[2 * lax.rem(source, 2) + c],
        relay_send.at[1],
        recv.at[2 * lax.rem(source, 2) + c],
        {"state": onward, "tm_2": source // 2},
    )
    on.start()
    for t in range(4):

        @pl.when(mine(t))
        def _():
            for copy_here in copies(t):
                copy_here.wait()

        @pl.when(jnp.logical_not(mine(t)))
        def _():
            mean_copy(t).wait_send()

        @pl.when(jnp.logical_not(mine(t)) & (t != opposite))
        def _():
            copy(t).wait_send()

    far.wait_send()
    on.wait_send()
    for i in range(4):

        @pl.when(jnp.logical_not((z == 2 * c + i // 2) & (c == i % 2)))
        def _():
            remote(slabs.at[0], out.at[i], send.at[0], recv.at[i], {"state": 0, "tm_2": 0}).wait_recv()
            remote(mean, mean_out.at[i], msend.at[0], mrecv.at[i], {"state": 0, "tm_2": 0}).wait_recv()


class Copies:
    def __init__(self, out, send, recv):
        self.out, self.send, self.recv, self.used, self.sent = out, send, recv, 0, []

    def put(self, peer, slot, row, rows, src=None):
        n, self.used = self.used, self.used + 1
        place = self.out.at[slot, pl.ds(pl.multiple_of(row, 8), rows), :]
        copy = remote(place if src is None else src, place, self.send.at[n], self.recv.at[n], peer)
        copy.start()
        self.sent.append(copy)
        return n

    def arrived(self, n, slot, row, rows):
        place = self.out.at[slot, pl.ds(pl.multiple_of(row, 8), rows), :]
        remote(place, place, self.send.at[n], self.recv.at[n], {"tm_2": 0}).wait_recv()

    def finish(self):
        for copy in self.sent:
            copy.wait_send()


Z_PIECES = (((0, 64), (64, 64), (128, 64), (192, 64)), ((0, 48), (48, 40), (88, 40), (128, 40)))
Z_HALF = (256, 168)


def pair_kernel(own, total, out, twin_buf, *refs):
    work, (swap_send, swap_recv, send, recv) = refs[:8], refs[8:]
    z, c = lax.axis_index("state"), lax.axis_index("tm_2")
    zu, zd, zo = lax.rem(z + 1, 4), lax.rem(z + 3, 4), lax.rem(z + 2, 4)
    up, down, twin = {"state": zu}, {"state": zd}, {"tm_2": 1 - c}
    greet([up, down, twin])
    swaps = []
    for part, rows in ((0, pl.ds(0, N)), (1, pl.ds(N, ROWS - N))):
        swaps.append(remote(own.at[rows], twin_buf.at[rows], swap_send.at[part], swap_recv.at[part], twin))
        swaps[part].start()
    cp = Copies(out, send, recv)
    ups, downs, tails, twins = [], [], [], []

    def rows_of(part, core, piece):
        return (N if part else 0) + core * Z_HALF[part] + piece[0], piece[1]

    def first_hop(part):
        pieces = Z_PIECES[part]
        for j, (a, b) in enumerate(zip(pieces, pieces[::-1])):
            for into, peer, piece in ((ups, up, a), (downs, down, b)):
                row, rows = rows_of(part, c, piece)
                n = cp.put(peer, z, row, rows, total.at[pl.ds(pl.multiple_of(row, 8), rows), :])
                into.append((n, part, piece, j < len(pieces) // 2))

    load = chosen(c, own, lambda k, row, rows, lane, lanes: twin_buf[row : row + rows, lane : lane + lanes])
    swaps[0].wait()
    gains(2, c, load, total, None, work)
    first_hop(0)
    swaps[1].wait()
    spreads(2, c, load, total, None, work)
    first_hop(1)

    def hand(slot, part, piece):
        row, rows = rows_of(part, c, piece)
        twins.append((cp.put(twin, slot, row, rows), slot, rows_of(part, 1 - c, piece)))

    for pair in zip(ups, downs):
        for (n, part, piece, further), slot, peer in zip(pair, (zd, zu), (up, down)):
            row, rows = rows_of(part, c, piece)
            cp.arrived(n, slot, row, rows)
            if further:
                tails.append((cp.put(peer, slot, row, rows), part, piece))
            hand(slot, part, piece)
    for n, part, piece in tails:
        row, rows = rows_of(part, c, piece)
        cp.arrived(n, zo, row, rows)
        hand(zo, part, piece)
    for n, slot, (row, rows) in twins:
        cp.arrived(n, slot, row, rows)
    cp.finish()


QUARTER = (128, 96)
PIECES = 4


def ring_kernel(mine, axis, own, others, rest, out, total, *refs):
    z, c, a = lax.axis_index("state"), lax.axis_index("tm_2"), lax.axis_index(axis)
    work, (send, recv, twin_send, twin_recv) = refs[:8], refs[8:]
    me = lax.axis_index(mine)
    zu, zd, zo = lax.rem(z + 1, 4), lax.rem(z + 3, 4), lax.rem(z + 2, 4)
    au, ad, ao = lax.rem(a + 1, 4), lax.rem(a + 3, 4), lax.rem(a + 2, 4)
    up, down = {axis: au}, {axis: ad}
    above, below, twin = {"state": zu}, {"state": zd}, {"tm_2": 1 - c}
    peers = [up, down, above, below, twin]
    barrier = pltpu.get_barrier_semaphore()
    for peer in peers:
        pl.semaphore_signal(barrier, inc=1, device_id=peer, device_id_type=MESH)
    quarters = (z, zu)
    coming = (zd, zo)
    load = chosen(me, own, from_slots(others))

    def run(part):
        base, size = N if part else 0, QUARTER[part] // PIECES
        span = pl.ds(base, 4 * QUARTER[part])
        if part:
            split_gains(4, load, work)
            spreads(4, me, load, total, rest, work)
        else:
            gains(4, me, load, total, rest, work)
        pl.semaphore_wait(barrier, len(peers))
        cp = Copies(out, send, recv)

        def hand(src, dst, sem):
            copy = remote(src, dst, twin_send.at[sem], twin_recv.at[sem], twin)
            copy.start()

        def row_of(quarter, j):
            return pl.multiple_of(base + quarter * QUARTER[part] + j * size, 8)

        ups, downs, zs, tails = [], [], [], []
        for j in range(PIECES):
            for k in (0, 1):
                for into, peer, jj in ((ups, up, j), (downs, down, PIECES - 1 - j)):
                    row = row_of(quarters[k], jj)
                    n = cp.put(peer, a, row, size, total.at[pl.ds(row, size), :])
                    into.append((n, k, jj, j < PIECES // 2))
        hand(total.at[span], total.at[span], 0)
        hand(rest.at[span], rest.at[span], 1)

        def pass_on(slot, row):
            place = out.at[slot, pl.ds(row, size), :]
            hand(place, place, 2)

        def spread(slot, k, j):
            row = row_of(quarters[k], j)
            zs.append((cp.put(below if k else above, slot, row, size), slot, k, j))
            pass_on(slot, row)

        def take(count):
            while len(zs) > count:
                n, slot, k, j = zs.pop(0)
                row = row_of(coming[k], j)
                cp.arrived(n, slot, row, size)
                pass_on(slot, row)

        for pair in zip(ups, downs):
            for (n, k, j, further), slot, peer in zip(pair, (ad, au), (up, down)):
                row = row_of(quarters[k], j)
                cp.arrived(n, slot, row, size)
                if further:
                    tails.append((cp.put(peer, slot, row, size), k, j))
                spread(slot, k, j)
        for n, k, j in tails:
            cp.arrived(n, ao, row_of(quarters[k], j), size)
            spread(ao, k, j)
            take(len(zs) - 2)
        take(0)
        cp.finish()
        other = pl.ds(0 if part else N, 4 * QUARTER[1 - part])
        for sem, ref in enumerate((total, rest)):
            remote(ref.at[span], ref.at[span], twin_send.at[sem], twin_recv.at[sem], twin).wait_send()
            remote(ref.at[other], ref.at[other], twin_send.at[sem], twin_recv.at[sem], twin).wait_recv()
        sent, came = out.at[0:3, span], out.at[0:3, other]
        remote(sent, sent, twin_send.at[2], twin_recv.at[2], twin).wait_send()
        remote(came, came, twin_send.at[2], twin_recv.at[2], twin).wait_recv()

    for part in (0, 1):
        pl.when(c == part)(partial(run, part))


def shape(*dims, dtype=F32):
    return jax.ShapeDtypeStruct(dims, dtype)


def params(limit=None, **more):
    return pltpu.CompilerParams(vmem_limit_bytes=limit, **more)


DMA = pltpu.SemaphoreType.DMA


def comm(kernel, name, collective_id, outs, scratch, *args, in_spec=ANY, out_spec=ANY):
    return pl.pallas_call(
        kernel,
        name=name,
        out_shape=outs,
        in_specs=[in_spec] * len(args),
        out_specs=jax.tree.map(lambda _: out_spec, outs),
        scratch_shapes=scratch,
        compiler_params=pltpu.CompilerParams(
            collective_id=collective_id, has_side_effects=True, vmem_limit_bytes=4 * 1024 * 1024
        ),
    )(*args)


BIG = 32 * 1024 * 1024
WORK = [
    pltpu.VMEM((512, 512), BF16),
    pltpu.VMEM((512, 512), BF16),
    pltpu.VMEM((512, 512), F32),
]


def suffix_work(count):
    return [
        pltpu.VMEM((2, N, N), F32),
        pltpu.VMEM((2, N, N), F32),
        pltpu.VMEM((2, 8, N), F32),
        pltpu.VMEM((N, N), BF16),
        pltpu.VMEM((N, N), BF16),
        pltpu.VMEM((count - 1, N, N), BF16),
        pltpu.VMEM((count - 1, N, N), BF16),
        pltpu.VMEM((N, N), F32),
    ]


def ring(name, collective_id, mine, axis, own, others):
    packet = shape(ROWS, N)
    return pl.pallas_call(
        partial(ring_kernel, mine, axis),
        name=name,
        out_shape=(packet, shape(4, ROWS, N), packet),
        in_specs=[VM, VM],
        out_specs=(VM, VM, VM),
        scratch_shapes=suffix_work(4) + [DMA((48,)), DMA((48,)), DMA((3,)), DMA((3,))],
        compiler_params=params(RING_LIMIT, collective_id=collective_id, has_side_effects=True),
    )(own, others)


RING_LIMIT = 24 * 1024 * 1024


def on_device(filtered_cov, filtered_mean, noise_var, trans_blocks, pattern):
    z = lax.axis_index("state")
    cov, twin_mean, mean_here, noise_here, blocks_here = comm(
        gather_step_kernel,
        "gather_step",
        0,
        (shape(4, B, N), shape(4, N), shape(4, N), shape(1, N), shape(4, 2, B, B)),
        [pltpu.VMEM((2, B, N), F32), DMA((4,)), DMA((4,)), DMA((2,)), DMA((2,)), DMA, DMA, DMA, DMA((3,))],
        filtered_cov,
        filtered_mean,
        noise_var.reshape(1, N),
        trans_blocks,
        in_spec=pl.BlockSpec(memory_space=pltpu.HBM),
        out_spec=VM,
    )
    own = pl.pallas_call(
        element_kernel,
        name="element",
        out_shape=shape(ROWS, N),
        in_specs=[SM] + [VM] * 5,
        out_specs=VM,
        scratch_shapes=[pltpu.VMEM((N, N), F32)] * 3 + [pltpu.VMEM((8, N), F32), pltpu.VMEM((N, N), F32), pltpu.VMEM((B, B), F32)],
        compiler_params=params(BIG),
    )(pattern, cov, mean_here, twin_mean, noise_here, blocks_here)
    packet, packets = shape(ROWS, N), shape(4, ROWS, N)
    pair, pairs = pl.pallas_call(
        pair_kernel,
        name="pair",
        out_shape=(packet, packets),
        in_specs=[VM],
        out_specs=(VM, VM),
        scratch_shapes=[pltpu.VMEM((ROWS, N), F32)] + suffix_work(2) + [DMA((2,)), DMA((2,)), DMA((48,)), DMA((48,))],
        compiler_params=params(RING_LIMIT, collective_id=2, has_side_effects=True),
    )(own)
    down, columns, column = ring("ring_x", 3, "state", "tm_1", pair, pairs)
    across, rows, row = ring("ring_y", 4, "tm_1", "tm_0", column, columns)
    later = pl.pallas_call(
        scan_kernel,
        name="scan_y",
        out_shape=packet,
        in_specs=[VM, VM],
        out_specs=VM,
        scratch_shapes=suffix_work(4),
        compiler_params=params(BIG),
    )(row, rows)
    slabs, mean = pl.pallas_call(
        apply_kernel,
        name="apply",
        out_shape=(shape(4, B, N), shape(8, N)),
        in_specs=[VM] * 5,
        out_specs=(VM, VM),
        scratch_shapes=[pltpu.VMEM((N, N), F32), pltpu.VMEM((8, N), F32), pltpu.VMEM((8, N), F32), pltpu.VMEM((2, N, N), BF16)]
        + WORK,
        compiler_params=params(BIG),
    )(later, across, down, pair, own)
    smooth_cov, means = comm(
        scatter_step_kernel,
        "scatter_step",
        5,
        (shape(4, B, N), shape(4, 8, N)),
        [pltpu.VMEM((B, N), F32), DMA((4,)), DMA((4,)), DMA((2,)), DMA, DMA((2,)), DMA((4,)), DMA((4,))],
        slabs,
        mean,
        out_spec=VM,
    )
    return lax.dynamic_slice_in_dim(means[:, 0, :], z * B, B, 1), smooth_cov


def solution(mesh):
    torus = Mesh(
        mesh.devices.reshape(4, 4, 2, mesh.shape["state"]), ("tm_0", "tm_1", "tm_2", "state")
    )
    return jax.shard_map(
        on_device,
        mesh=torus,
        in_specs=(P(TM, "state", None), P(TM, None), P(), P(), P()),
        out_specs=(P(TM, "state"), P(TM, "state", None)),
        check_vma=False,
    )
```

```python
from functools import partial

import jax
import jax.numpy as jnp
from jax import lax
from jax.experimental import pallas as pl
from jax.experimental.pallas import tpu as pltpu
from jax.sharding import Mesh
from jax.sharding import PartitionSpec as P

N = 512
B = 128
LROW = 512
GROW = 832
ROWS = 896
MESH = pl.DeviceIdType.MESH
F32 = jnp.float32
BF16 = jnp.bfloat16
ANY = pl.BlockSpec(memory_space=pl.ANY)
VM = pl.BlockSpec(memory_space=pltpu.VMEM)
SM = pl.BlockSpec(memory_space=pltpu.SMEM)
TM = ("tm_0", "tm_1", "tm_2")


def split(x):
    high = x.astype(BF16)
    return high, (x - high.astype(F32)).astype(BF16)


def dg(a, b, cb=0):
    return lax.dot_general(a, b, (((1,), (cb,)), ((), ())), preferred_element_type=F32)


def dot_s(a, b, cb=0):
    return dg(a[0], b[0], cb) + (dg(a[0], b[1], cb) + dg(a[1], b[0], cb))


def dot3(a, b, cb=0):
    return dot_s(split(a), split(b), cb)


def dot6(a, b, cb=0, ca=1):
    return lax.dot_general(
        a, b, (((ca,), (cb,)), ((), ())), precision=lax.Precision.HIGHEST, preferred_element_type=F32
    )


def packed_blocks():
    out = []
    for j in range(4):
        out.append((0, j, LROW, j, 128, 0))
    for lane, (i, j) in enumerate(((1, 1), (1, 2), (1, 3), (2, 2))):
        out.append((i, j, LROW + 128, lane, 128, 0))
    for lane, (i, j, r) in enumerate(((2, 3, 0), (2, 3, 64), (3, 3, 0), (3, 3, 64))):
        out.append((i, j, LROW + 256, lane, 64, r))
    return out


def pack_spread(ref, full):
    for i, j, row, lane, rows, r0 in packed_blocks():
        ref[row : row + rows, lane * B : lane * B + B] = full(i * B + r0, rows, j * B)


def unpack_spread(load, full_ref):
    for i, j, row, lane, rows, r0 in packed_blocks():
        block = load(row, rows, lane * B)
        full_ref[i * B + r0 : i * B + r0 + rows, j * B : j * B + B] = block
    for i in range(4):
        for j in range(i + 1, 4):
            block = full_ref[i * B : i * B + B, j * B : j * B + B]
            full_ref[j * B : j * B + B, i * B : i * B + B] = jnp.transpose(block)


def tree_sum(terms):
    while len(terms) > 1:
        terms = [sum(terms[i + 1 : i + 2], terms[i]) for i in range(0, len(terms), 2)]
    return terms[0]


def small_mul(a, b):
    return [
        [tree_sum([a[i][t] * b[t][j] for t in range(len(b))]) for j in range(len(b[0]))] for i in range(len(a))
    ]


def small_inverse(m):
    n = len(m)
    if n == 2:
        a, b, d = m[0][0], m[0][1], m[1][1]
        inv = 1.0 / (a * d - b * b)
        return [[d * inv, -b * inv], [-b * inv, a * inv]]
    h = n // 2
    upper = [row[h:] for row in m[:h]]
    lower = [[upper[j][i] for j in range(h)] for i in range(h)]
    first = small_inverse([row[:h] for row in m[:h]])
    q = small_mul(lower, first)
    qb = small_mul(q, upper)
    schur = [[m[h + min(i, j)][h + max(i, j)] - qb[min(i, j)][max(i, j)] for j in range(h)] for i in range(h)]
    second = small_inverse(schur)
    sq = small_mul(second, q)
    qsq = small_mul([[q[j][i] for j in range(h)] for i in range(h)], sq)
    out = [[None] * n for _ in range(n)]
    for i in range(h):
        for j in range(h):
            out[i][j] = first[i][j] + qsq[i][j]
            out[h + i][h + j] = second[i][j]
            out[h + i][j] = out[j][h + i] = -sq[i][j]
    return out


PANEL = 64


def inverse128(block):
    groups = PANEL // 8
    row_id = lax.broadcasted_iota(jnp.int32, (8, B), 0)
    lane_id = lax.broadcasted_iota(jnp.int32, (8, B), 1)
    lanes = lax.broadcasted_iota(jnp.int32, (B, B), 1)

    def body(_, x):
        top = x[:PANEL, :]
        vs = [x[8 * k : 8 * k + 8, :] for k in range(groups)]
        for q in range(groups):
            at = 8 * q
            cols = [[jnp.broadcast_to(v[:, at + s : at + s + 1], (8, B)) for v in vs] for s in range(8)]
            rows = [jnp.broadcast_to(vs[q][s : s + 1, :], (8, B)) for s in range(8)]
            m = [[None] * 8 for _ in range(8)]
            for s in range(8):
                for t in range(s, 8):
                    m[s][t] = m[t][s] = jnp.broadcast_to(cols[s][q][t : t + 1, :], (8, B))
            inv = small_inverse(m)
            new_rows = [n[0] for n in small_mul(inv, [[r] for r in rows])]
            for s in range(8):
                for t in range(8):
                    new_rows[s] = jnp.where(lane_id == at + t, -inv[s][t], new_rows[s])
            inside = (lane_id >= at) & (lane_id < at + 8)
            for k in range(groups):
                if k == q:
                    new = new_rows[0]
                    for s in range(1, 8):
                        new = jnp.where(row_id == s, new_rows[s], new)
                else:
                    new = jnp.where(inside, 0.0, vs[k])
                    new -= tree_sum([cols[s][k] * new_rows[s] for s in range(8)])
                vs[k] = new
        done = jnp.concatenate(vs, axis=0)
        rest = jnp.where(lanes < PANEL, 0.0, x) - dot6(top, done, 0, 0)
        return pltpu.roll(jnp.concatenate([rest[PANEL:, :], done], axis=0), B - PANEL, 1)

    return -lax.fori_loop(0, B // PANEL, body, block)


def element_kernel(pattern, cov_in, mean_a, mean_b, noise, blocks, out, left, pred, sol, upd, cov, inv_ref):
    y, x, c, z = (lax.axis_index(a) for a in ("tm_0", "tm_1", "tm_2", "state"))
    for i in range(4):
        for t in range(3):
            lanes = slice((i + t) % 4 * B, (i + t) % 4 * B + B)
            cov[i * B : i * B + B, lanes] = cov_in[i, :, lanes]
        j = (i + 3) % 4
        cov[i * B : i * B + B, j * B : j * B + B] = jnp.transpose(cov_in[j, :, i * B : i * B + B])
    tb = lambda r, j: blocks[r, j]

    def rows_of(ref, block):
        return ref[pl.ds(pl.multiple_of(block * B, B), B), :]

    def lanes_of(ref, row, rows, block):
        return ref[row : row + rows, pl.ds(pl.multiple_of(block * B, B), B)]

    place = lax.rem(2 * z + c, 4)
    mean = jnp.where(z // 2 == c, mean_a[pl.ds(place, 1), :], mean_b[pl.ds(place, 1), :])
    upd[0:8, :] = jnp.broadcast_to(mean, (8, N))
    pushed = []
    for r in range(4):
        t0, t1 = tb(r, 0), tb(r, 1)
        left[r * B : r * B + B, :] = dot6(t0, rows_of(cov, pattern[r, 0])) + dot6(
            t1, rows_of(cov, pattern[r, 1])
        )
        pushed.append(
            dot6(lanes_of(upd, 0, 8, pattern[r, 0]), t0, 1)
            + dot6(lanes_of(upd, 0, 8, pattern[r, 1]), t1, 1)
        )
    pushed = jnp.concatenate(pushed, axis=1)
    eye = lax.broadcasted_iota(jnp.int32, (B, B), 0) == lax.broadcasted_iota(jnp.int32, (B, B), 1)
    for r in range(4):
        rows = (r + 1) * B
        value = dot6(lanes_of(left, 0, rows, pattern[r, 0]), tb(r, 0), 1) + dot6(
            lanes_of(left, 0, rows, pattern[r, 1]), tb(r, 1), 1
        )
        pred[0:rows, r * B : r * B + B] = value
        q = jnp.where(eye, jnp.broadcast_to(noise[0:1, r * B : r * B + B], (B, B)), 0.0)
        pred[r * B : rows, r * B : r * B + B] += q
    sol[...] = left[...]

    def eliminate(k, _):
        at = pl.ds(pl.multiple_of(k * B, B), B)
        inv_ref[...] = inverse128(pred[at, at])
        for kk in range(4):

            @pl.when(k == kk)
            def _():
                k0, k1 = kk * B, kk * B + B
                inv = inv_ref[...]
                ub = dot6(inv, sol[k0:k1, :])
                sol[k0:k1, :] = ub
                if kk < 3:
                    tail = pred[k0:k1, k1:]
                    ut = dot6(inv, tail)
                    st = jnp.transpose(tail)
                    pred[k1:, k1:] -= dot6(st, ut)
                    sol[k1:, :] -= dot6(st, ub)
                    pred[k0:k1, k1:] = ut

        return 0

    lax.fori_loop(0, 4, eliminate, 0)
    for k in (2, 1, 0):
        k0, k1 = k * B, k * B + B
        sol[k0:k1, :] -= dot6(pred[k0:k1, k1:], sol[k1:, :])
    keep = (8 * (4 * y + x) + 2 * z + c != 127).astype(F32)
    for i in range(4):
        for j in range(4):
            out[i * B : i * B + B, j * B : j * B + B] = (
                jnp.transpose(sol[j * B : j * B + B, i * B : i * B + B]) * keep
            )
    out[GROW : GROW + 8, :] = jnp.broadcast_to(mean, (8, N)) - keep * dot6(pushed, sol[...])
    out[GROW + 8 :, :] = jnp.zeros((ROWS - GROW - 8, N), F32)
    pred[...] = cov[...] - dot6(out[0:N, :], left[...])
    pack_spread(out, lambda r, n, c: pred[r : r + n, c : c + B])


def split_into(high, low, value):
    for r in range(4):
        rows = slice(r * B, r * B + B)
        high[rows, :], low[rows, :] = split(value(rows))


def chosen(me, own, other):
    def load(k, row, rows, lane=0, lanes=N):
        return jnp.where(k == me, own[row : row + rows, lane : lane + lanes], other(k, row, rows, lane, lanes))

    return load


def split_gains(count, load, work):
    eh, el = work[5:7]

    def body(k, _):
        split_into(eh.at[k], el.at[k], lambda rows: load(k, rows.start, B))
        return 0

    lax.fori_loop(0, count - 1, body, 0)


def gains(count, me, load, total, rest, work):
    se, _, _, rh, rl, eh, el, _ = work
    last = count - 1
    if rest is not None:

        @pl.when(me == last)
        def _():
            same = lax.broadcasted_iota(jnp.int32, (N, N), 0) == lax.broadcasted_iota(jnp.int32, (N, N), 1)
            rest[0:N, :] = same.astype(F32)

    def step(t, _):
        k = last - 1 - t
        now = lax.rem(t, 2)
        if rest is not None:

            @pl.when(k == me)
            def _():
                rest[0:N, :] = se[now]

        split_into(eh.at[k], el.at[k], lambda rows: load(k, rows.start, B))
        split_into(rh, rl, lambda rows: se[now, rows, :])
        se[1 - now] = dot_s((eh[k], el[k]), (rh[...], rl[...]))
        return 0

    se[0] = load(last, 0, N)
    lax.fori_loop(0, last, step, 0)
    total[0:N, :] = se[last % 2]


def spreads(count, me, load, total, rest, work):
    _, sl, sg, rh, rl, eh, el, lk = work
    last = count - 1
    if rest is not None:

        @pl.when(me == last)
        def _():
            rest[N:, :] = jnp.zeros((ROWS - N, N), F32)

    unpack_spread(lambda r, n, c: load(last, r, n, c, B), sl.at[0])
    sg[0] = load(last, GROW, 8)

    def keep(ref, slot):
        pack_spread(ref, lambda r, n, c: sl[slot, r : r + n, c : c + B])
        ref[GROW : GROW + 8, :] = sg[slot]
        ref[GROW + 8 :, :] = jnp.zeros((ROWS - GROW - 8, N), F32)

    def step(t, _):
        k = last - 1 - t
        now = lax.rem(t, 2)
        if rest is not None:

            @pl.when(k == me)
            def _():
                keep(rest, now)

        split_into(rh, rl, lambda rows: sl[now, rows, :])
        unpack_spread(lambda r, n, c: load(k, r, n, c, B), lk)
        e = (eh[k], el[k])
        sg[1 - now] = dot_s(split(sg[now]), e, 1) + load(k, GROW, 8)
        half = split(dot_s(e, (rh[...], rl[...])))
        sl[1 - now] = dot_s(half, e, 1) + lk[...]
        return 0

    lax.fori_loop(0, last, step, 0)
    if total is not None:
        keep(total, last % 2)


def from_slots(others):
    return lambda k, row, rows, lane, lanes: others[k, row : row + rows, lane : lane + lanes]


def greet(peers):
    barrier = pltpu.get_barrier_semaphore()
    for peer in peers:
        pl.semaphore_signal(barrier, inc=1, device_id=peer, device_id_type=MESH)
    pl.semaphore_wait(barrier, len(peers))


def column_peers(z, c):
    return [
        {"state": lax.rem(z + dz, 4), "tm_2": c if dc == 0 else 1 - c}
        for dz in range(4)
        for dc in range(2)
        if dz or dc
    ]


def remote(src, dst, send, recv, peer):
    return pltpu.make_async_remote_copy(
        src_ref=src, dst_ref=dst, send_sem=send, recv_sem=recv, device_id=peer, device_id_type=MESH
    )


def lanes_of_block(ref, j):
    return ref.at[:, pl.ds(pl.multiple_of(lax.rem(j, 4) * B, B), B)]


def gather_step_kernel(
    cov,
    mean,
    noise,
    blocks,
    out,
    mean_out,
    mean_here,
    noise_here,
    blocks_here,
    relay,
    send,
    recv,
    relay_send,
    relay_recv,
    local,
    msend,
    mrecv,
    small,
):
    z, c = lax.axis_index("state"), lax.axis_index("tm_2")
    greet(column_peers(z, c))
    other = remote(mean, mean_out, msend, mrecv, {"tm_2": 1 - c})
    other.start()
    here = [
        pltpu.make_async_copy(src, dst, small.at[n])
        for n, (src, dst) in enumerate(((mean, mean_here), (noise, noise_here), (blocks, blocks_here)))
    ]
    for copy_here in here:
        copy_here.start()

    def start(src, dst, row, ssem, rsem, peer):
        for t in range(3):
            remote(lanes_of_block(src, row + t), lanes_of_block(dst, row + t), ssem, rsem, peer).start()

    def whole(ref, ssem, rsem):
        part = ref.at[:, 0 : 3 * B]
        return remote(part, part, ssem, rsem, {"state": 0, "tm_2": 0})

    def target(i):
        dz, e = 2 * c + i // 2, i % 2
        mine = (z == dz) & (c == e)
        far = lax.rem(dz + 4 - z, 4) == 2
        return dz, e, mine, far

    for i in range(4):
        dz, e, mine, far = target(i)

        @pl.when(far)
        def _():
            start(cov.at[i], relay.at[e], z, send.at[i], relay_recv.at[e], {"state": lax.rem(z + (3 if e else 1), 4)})

    for i in range(4):
        dz, e, mine, far = target(i)

        @pl.when(mine)
        def _():
            pltpu.make_async_copy(cov.at[i], out.at[z], local).start()

        @pl.when(jnp.logical_not(mine | far))
        def _():
            start(cov.at[i], out.at[z], z, send.at[i], recv.at[z], {"state": dz, "tm_2": e})

    duties = []
    for e in range(2):
        source, dz = lax.rem(z + (1 if e else 3), 4), lax.rem(z + (3 if e else 1), 4)
        duty = source // 2 != c
        duties.append(duty)

        @pl.when(duty)
        def _():
            whole(relay.at[e], send.at[0], relay_recv.at[e]).wait_recv()
            start(relay.at[e], out.at[source], source, relay_send.at[e], recv.at[source], {"state": dz, "tm_2": e})

    for i in range(4):
        dz, e, mine, far = target(i)

        @pl.when(mine)
        def _():
            pltpu.make_async_copy(cov.at[i], out.at[z], local).wait()

        @pl.when(jnp.logical_not(mine))
        def _():
            whole(cov.at[i], send.at[i], recv.at[0]).wait_send()

    for e in range(2):

        @pl.when(duties[e])
        def _():
            whole(relay.at[e], relay_send.at[e], recv.at[0]).wait_send()

    source_core = z // 2
    for s in range(4):

        @pl.when(jnp.logical_not((z == s) & (c == source_core)))
        def _():
            whole(out.at[s], send.at[0], recv.at[s]).wait_recv()

    other.wait()
    for copy_here in here:
        copy_here.wait()


def final_kernel(
    row,
    rows,
    across,
    down,
    pair,
    own,
    out,
    mean_out,
    cov,
    mean,
    add,
    relay,
    sl,
    sg,
    rh,
    rl,
    eh,
    el,
    lk,
    send,
    recv,
    relay_send,
    relay_recv,
    local,
    msend,
    mrecv,
):
    z, c, me = lax.axis_index("state"), lax.axis_index("tm_2"), lax.axis_index("tm_0")
    barrier = pltpu.get_barrier_semaphore()
    peers = column_peers(z, c)
    for peer in peers:
        pl.semaphore_signal(barrier, inc=1, device_id=peer, device_id_type=MESH)
    load = chosen(me, row, from_slots(rows))

    @pl.when(me == 3)
    def _():
        cov[...] = jnp.zeros((N, N), F32)
        mean[...] = jnp.zeros((8, N), F32)

    @pl.when(me == 2)
    def _():
        unpack_spread(lambda r, n, c: load(3, r, n, c, B), cov)
        mean[...] = load(3, GROW, 8)

    @pl.when(me < 2)
    def _():
        unpack_spread(lambda r, n, c: load(3, r, n, c, B), sl)
        sg[...] = load(3, GROW, 8)

    def take(get):
        split_into(eh, el, lambda r: get(r.start, B))
        unpack_spread(lambda r, n, c: get(r, n, c, B), lk)
        add[...] = get(GROW, 8)

    def push(state, offset):
        split_into(rh, rl, lambda r: state[r, :])
        e = (eh[...], el[...])
        offset[...] = dot_s(split(offset[...]), e, 1) + add[...]
        state[...] = dot_s(split(dot_s(e, (rh[...], rl[...]))), e, 1) + lk[...]

    choices = (
        lambda r, n, c=0, m=N: load(2, r, n, c, m),
        lambda r, n, c=0, m=N: load(1, r, n, c, m),
        lambda r, n, c=0, m=N: across[r : r + n, c : c + m],
        lambda r, n, c=0, m=N: down[r : r + n, c : c + m],
        lambda r, n, c=0, m=N: jnp.where(
            lax.axis_index("tm_2") == 0, pair[r : r + n, c : c + m], own[r : r + n, c : c + m]
        ),
    )

    def early(t, _):
        @pl.when(me < 2 - t)
        def _():
            for k in range(2):
                pl.when(t == k)(partial(take, choices[k]))
            push(sl, sg)

        @pl.when(me == 1 - t)
        def _():
            cov[...] = sl[...]
            mean[...] = sg[...]

        return 0

    lax.fori_loop(0, 2, early, 0)

    def late(t, _):
        for k in range(3):
            pl.when(t == k)(partial(take, choices[2 + k]))
        push(cov, mean)
        return 0

    lax.fori_loop(0, 3, late, 0)
    pl.semaphore_wait(barrier, len(peers))

    core = z // 2
    slot = 2 * lax.rem(z, 2) + c
    opposite = lax.rem(z + 2, 4)
    onward = lax.rem(z + 1 + 2 * c, 4)

    def slab(t):
        return cov.at[pl.ds(pl.multiple_of(t * B, B), B), :]

    far = remote(slab(opposite), relay, relay_send.at[0], relay_recv, {"state": onward})
    far.start()

    def copy(t):
        return remote(slab(t), out.at[slot], send.at[t], recv.at[slot], {"state": t, "tm_2": core})

    def mean_copy(t):
        return remote(mean, mean_out.at[slot], msend.at[t], mrecv.at[slot], {"state": t, "tm_2": core})

    def mine(t):
        return (z == t) & (c == core)

    def copies(t):
        return pltpu.make_async_copy(slab(t), out.at[slot], local.at[0]), pltpu.make_async_copy(
            mean, mean_out.at[slot], local.at[1]
        )

    for t in range(4):

        @pl.when(mine(t))
        def _():
            for copy_here in copies(t):
                copy_here.start()

        @pl.when(jnp.logical_not(mine(t)))
        def _():
            mean_copy(t).start()

        @pl.when(jnp.logical_not(mine(t)) & (t != opposite))
        def _():
            copy(t).start()

    source = lax.rem(z + 3 + 2 * c, 4)
    far.wait_recv()
    on = remote(
        relay,
        out.at[2 * lax.rem(source, 2) + c],
        relay_send.at[1],
        recv.at[2 * lax.rem(source, 2) + c],
        {"state": onward, "tm_2": source // 2},
    )
    on.start()
    for t in range(4):

        @pl.when(mine(t))
        def _():
            for copy_here in copies(t):
                copy_here.wait()

        @pl.when(jnp.logical_not(mine(t)))
        def _():
            mean_copy(t).wait_send()

        @pl.when(jnp.logical_not(mine(t)) & (t != opposite))
        def _():
            copy(t).wait_send()

    far.wait_send()
    on.wait_send()
    for i in range(4):

        @pl.when(jnp.logical_not((z == 2 * c + i // 2) & (c == i % 2)))
        def _():
            remote(slab(0), out.at[i], send.at[0], recv.at[i], {"state": 0, "tm_2": 0}).wait_recv()
            remote(mean, mean_out.at[i], msend.at[0], mrecv.at[i], {"state": 0, "tm_2": 0}).wait_recv()


class Copies:
    def __init__(self, out, send, recv):
        self.out, self.send, self.recv, self.used, self.sent = out, send, recv, 0, []

    def put(self, peer, slot, row, rows, src=None):
        n, self.used = self.used, self.used + 1
        place = self.out.at[slot, pl.ds(pl.multiple_of(row, 8), rows), :]
        copy = remote(place if src is None else src, place, self.send.at[n], self.recv.at[n], peer)
        copy.start()
        self.sent.append(copy)
        return n

    def arrived(self, n, slot, row, rows):
        place = self.out.at[slot, pl.ds(pl.multiple_of(row, 8), rows), :]
        remote(place, place, self.send.at[n], self.recv.at[n], {"tm_2": 0}).wait_recv()

    def finish(self):
        for copy in self.sent:
            copy.wait_send()


Z_PIECES = (((0, 64), (64, 64), (128, 64), (192, 64)), ((0, 48), (48, 40), (88, 40), (128, 40)))
Z_HALF = (256, 168)


def pair_kernel(own, total, out, twin_buf, *refs):
    work, (swap_send, swap_recv, send, recv) = refs[:8], refs[8:]
    z, c = lax.axis_index("state"), lax.axis_index("tm_2")
    zu, zd, zo = lax.rem(z + 1, 4), lax.rem(z + 3, 4), lax.rem(z + 2, 4)
    up, down, twin = {"state": zu}, {"state": zd}, {"tm_2": 1 - c}
    greet([up, down, twin])
    swaps = []
    for part, rows in ((0, pl.ds(0, N)), (1, pl.ds(N, ROWS - N))):
        swaps.append(remote(own.at[rows], twin_buf.at[rows], swap_send.at[part], swap_recv.at[part], twin))
        swaps[part].start()
    cp = Copies(out, send, recv)
    ups, downs, tails, twins = [], [], [], []

    def rows_of(part, core, piece):
        return (N if part else 0) + core * Z_HALF[part] + piece[0], piece[1]

    def first_hop(part):
        pieces = Z_PIECES[part]
        for j, (a, b) in enumerate(zip(pieces, pieces[::-1])):
            for into, peer, piece in ((ups, up, a), (downs, down, b)):
                row, rows = rows_of(part, c, piece)
                n = cp.put(peer, z, row, rows, total.at[pl.ds(pl.multiple_of(row, 8), rows), :])
                into.append((n, part, piece, j < len(pieces) // 2))

    load = chosen(c, own, lambda k, row, rows, lane, lanes: twin_buf[row : row + rows, lane : lane + lanes])
    swaps[0].wait()
    gains(2, c, load, total, None, work)
    first_hop(0)
    swaps[1].wait()
    spreads(2, c, load, total, None, work)
    first_hop(1)

    def hand(slot, part, piece):
        row, rows = rows_of(part, c, piece)
        twins.append((cp.put(twin, slot, row, rows), slot, rows_of(part, 1 - c, piece)))

    for pair in zip(ups, downs):
        for (n, part, piece, further), slot, peer in zip(pair, (zd, zu), (up, down)):
            row, rows = rows_of(part, c, piece)
            cp.arrived(n, slot, row, rows)
            if further:
                tails.append((cp.put(peer, slot, row, rows), part, piece))
            hand(slot, part, piece)
    for n, part, piece in tails:
        row, rows = rows_of(part, c, piece)
        cp.arrived(n, zo, row, rows)
        hand(zo, part, piece)
    for n, slot, (row, rows) in twins:
        cp.arrived(n, slot, row, rows)
    cp.finish()


QUARTER = (128, 96)
PIECES = 4


def ring_kernel(mine, axis, own, others, rest, out, total, *refs):
    z, c, a = lax.axis_index("state"), lax.axis_index("tm_2"), lax.axis_index(axis)
    work, (send, recv, twin_send, twin_recv) = refs[:8], refs[8:]
    me = lax.axis_index(mine)
    zu, zd, zo = lax.rem(z + 1, 4), lax.rem(z + 3, 4), lax.rem(z + 2, 4)
    au, ad, ao = lax.rem(a + 1, 4), lax.rem(a + 3, 4), lax.rem(a + 2, 4)
    up, down = {axis: au}, {axis: ad}
    above, below, twin = {"state": zu}, {"state": zd}, {"tm_2": 1 - c}
    peers = [up, down, above, below, twin]
    barrier = pltpu.get_barrier_semaphore()
    for peer in peers:
        pl.semaphore_signal(barrier, inc=1, device_id=peer, device_id_type=MESH)
    quarters = (z, zu)
    coming = (zd, zo)
    load = chosen(me, own, from_slots(others))

    def run(part):
        base, size = N if part else 0, QUARTER[part] // PIECES
        span = pl.ds(base, 4 * QUARTER[part])
        if part:
            split_gains(4, load, work)
            spreads(4, me, load, total, rest, work)
        else:
            gains(4, me, load, total, rest, work)
        pl.semaphore_wait(barrier, len(peers))
        cp = Copies(out, send, recv)

        def hand(src, dst, sem):
            copy = remote(src, dst, twin_send.at[sem], twin_recv.at[sem], twin)
            copy.start()

        def row_of(quarter, j):
            return pl.multiple_of(base + quarter * QUARTER[part] + j * size, 8)

        ups, downs, zs, tails = [], [], [], []
        for j in range(PIECES):
            for k in (0, 1):
                for into, peer, jj in ((ups, up, j), (downs, down, PIECES - 1 - j)):
                    row = row_of(quarters[k], jj)
                    n = cp.put(peer, a, row, size, total.at[pl.ds(row, size), :])
                    into.append((n, k, jj, j < PIECES // 2))
        hand(total.at[span], total.at[span], 0)
        hand(rest.at[span], rest.at[span], 1)

        def pass_on(slot, row):
            place = out.at[slot, pl.ds(row, size), :]
            hand(place, place, 2)

        def spread(slot, k, j):
            row = row_of(quarters[k], j)
            zs.append((cp.put(below if k else above, slot, row, size), slot, k, j))
            pass_on(slot, row)

        def take(count):
            while len(zs) > count:
                n, slot, k, j = zs.pop(0)
                row = row_of(coming[k], j)
                cp.arrived(n, slot, row, size)
                pass_on(slot, row)

        for pair in zip(ups, downs):
            for (n, k, j, further), slot, peer in zip(pair, (ad, au), (up, down)):
                row = row_of(quarters[k], j)
                cp.arrived(n, slot, row, size)
                if further:
                    tails.append((cp.put(peer, slot, row, size), k, j))
                spread(slot, k, j)
        for n, k, j in tails:
            cp.arrived(n, ao, row_of(quarters[k], j), size)
            spread(ao, k, j)
            take(len(zs) - 2)
        take(0)
        cp.finish()
        other = pl.ds(0 if part else N, 4 * QUARTER[1 - part])
        for sem, ref in enumerate((total, rest)):
            remote(ref.at[span], ref.at[span], twin_send.at[sem], twin_recv.at[sem], twin).wait_send()
            remote(ref.at[other], ref.at[other], twin_send.at[sem], twin_recv.at[sem], twin).wait_recv()
        sent, came = out.at[0:3, span], out.at[0:3, other]
        remote(sent, sent, twin_send.at[2], twin_recv.at[2], twin).wait_send()
        remote(came, came, twin_send.at[2], twin_recv.at[2], twin).wait_recv()

    for part in (0, 1):
        pl.when(c == part)(partial(run, part))


def shape(*dims, dtype=F32):
    return jax.ShapeDtypeStruct(dims, dtype)


def params(limit=None, **more):
    return pltpu.CompilerParams(vmem_limit_bytes=limit, **more)


DMA = pltpu.SemaphoreType.DMA


def comm(kernel, name, collective_id, outs, scratch, *args, limit, in_spec=ANY, out_spec=ANY):
    return pl.pallas_call(
        kernel,
        name=name,
        out_shape=outs,
        in_specs=[in_spec] * len(args),
        out_specs=jax.tree.map(lambda _: out_spec, outs),
        scratch_shapes=scratch,
        compiler_params=pltpu.CompilerParams(
            collective_id=collective_id, has_side_effects=True, vmem_limit_bytes=limit
        ),
    )(*args)


BIG = 32 * 1024 * 1024
def suffix_work(count):
    return [
        pltpu.VMEM((2, N, N), F32),
        pltpu.VMEM((2, N, N), F32),
        pltpu.VMEM((2, 8, N), F32),
        pltpu.VMEM((N, N), BF16),
        pltpu.VMEM((N, N), BF16),
        pltpu.VMEM((count - 1, N, N), BF16),
        pltpu.VMEM((count - 1, N, N), BF16),
        pltpu.VMEM((N, N), F32),
    ]


def ring(name, collective_id, mine, axis, own, others):
    packet = shape(ROWS, N)
    return pl.pallas_call(
        partial(ring_kernel, mine, axis),
        name=name,
        out_shape=(packet, shape(4, ROWS, N), packet),
        in_specs=[VM, VM],
        out_specs=(VM, VM, VM),
        scratch_shapes=suffix_work(4) + [DMA((48,)), DMA((48,)), DMA((3,)), DMA((3,))],
        compiler_params=params(RING_LIMIT, collective_id=collective_id, has_side_effects=True),
    )(own, others)


RING_LIMIT = 24 * 1024 * 1024
FIRST_LIMIT = 4 * 1024 * 1024


def on_device(filtered_cov, filtered_mean, noise_var, trans_blocks, pattern):
    z = lax.axis_index("state")
    cov, twin_mean, mean_here, noise_here, blocks_here = comm(
        gather_step_kernel,
        "gather_step",
        0,
        (shape(4, B, N), shape(4, N), shape(4, N), shape(1, N), shape(4, 2, B, B)),
        [pltpu.VMEM((2, B, N), F32), DMA((4,)), DMA((4,)), DMA((2,)), DMA((2,)), DMA, DMA, DMA, DMA((3,))],
        filtered_cov,
        filtered_mean,
        noise_var.reshape(1, N),
        trans_blocks,
        limit=FIRST_LIMIT,
        out_spec=VM,
    )
    own = pl.pallas_call(
        element_kernel,
        name="element",
        out_shape=shape(ROWS, N),
        in_specs=[SM] + [VM] * 5,
        out_specs=VM,
        scratch_shapes=[pltpu.VMEM((N, N), F32)] * 3 + [pltpu.VMEM((8, N), F32), pltpu.VMEM((N, N), F32), pltpu.VMEM((B, B), F32)],
        compiler_params=params(BIG),
    )(pattern, cov, mean_here, twin_mean, noise_here, blocks_here)
    packet, packets = shape(ROWS, N), shape(4, ROWS, N)
    pair, pairs = pl.pallas_call(
        pair_kernel,
        name="pair",
        out_shape=(packet, packets),
        in_specs=[VM],
        out_specs=(VM, VM),
        scratch_shapes=[pltpu.VMEM((ROWS, N), F32)] + suffix_work(2) + [DMA((2,)), DMA((2,)), DMA((48,)), DMA((48,))],
        compiler_params=params(RING_LIMIT, collective_id=2, has_side_effects=True),
    )(own)
    down, columns, column = ring("ring_x", 3, "state", "tm_1", pair, pairs)
    across, rows, row = ring("ring_y", 4, "tm_1", "tm_0", column, columns)
    half = pltpu.VMEM((N, N), BF16)
    smooth_cov, means = pl.pallas_call(
        final_kernel,
        name="final",
        out_shape=(shape(4, B, N), shape(4, 8, N)),
        in_specs=[VM] * 6,
        out_specs=(VM, VM),
        scratch_shapes=[pltpu.VMEM((N, N), F32), pltpu.VMEM((8, N), F32), pltpu.VMEM((8, N), F32), pltpu.VMEM((B, N), F32)]
        + [pltpu.VMEM((N, N), F32), pltpu.VMEM((8, N), F32), half, half, half, half, pltpu.VMEM((N, N), F32)]
        + [DMA((4,)), DMA((4,)), DMA((2,)), DMA, DMA((2,)), DMA((4,)), DMA((4,))],
        compiler_params=params(RING_LIMIT, collective_id=5, has_side_effects=True),
    )(row, rows, across, down, pair, own)
    return lax.dynamic_slice_in_dim(means[:, 0, :], z * B, B, 1), smooth_cov


def solution(mesh):
    torus = Mesh(
        mesh.devices.reshape(4, 4, 2, mesh.shape["state"]), ("tm_0", "tm_1", "tm_2", "state")
    )
    return jax.shard_map(
        on_device,
        mesh=torus,
        in_specs=(P(TM, "state", None), P(TM, None), P(), P(), P()),
        out_specs=(P(TM, "state"), P(TM, "state", None)),
        check_vma=False,
    )
```

```python
from functools import partial

import jax
import jax.numpy as jnp
from jax import lax
from jax.experimental import pallas as pl
from jax.experimental.pallas import tpu as pltpu
from jax.sharding import Mesh
from jax.sharding import PartitionSpec as P

N = 512
B = 128
LROW = 512
GROW = 832
ROWS = 896
MESH = pl.DeviceIdType.MESH
F32 = jnp.float32
BF16 = jnp.bfloat16
ANY = pl.BlockSpec(memory_space=pl.ANY)
VM = pl.BlockSpec(memory_space=pltpu.VMEM)
SM = pl.BlockSpec(memory_space=pltpu.SMEM)
TM = ("tm_0", "tm_1", "tm_2")


def split(x):
    high = x.astype(BF16)
    return high, (x - high.astype(F32)).astype(BF16)


def dg(a, b, cb=0):
    return lax.dot_general(a, b, (((1,), (cb,)), ((), ())), preferred_element_type=F32)


def dot_s(a, b, cb=0):
    return dg(a[0], b[0], cb) + (dg(a[0], b[1], cb) + dg(a[1], b[0], cb))


def dot3(a, b, cb=0):
    return dot_s(split(a), split(b), cb)


def dot6(a, b, cb=0, ca=1):
    return lax.dot_general(
        a, b, (((ca,), (cb,)), ((), ())), precision=lax.Precision.HIGHEST, preferred_element_type=F32
    )


def packed_blocks():
    out = []
    for j in range(4):
        out.append((0, j, LROW, j, 128, 0))
    for lane, (i, j) in enumerate(((1, 1), (1, 2), (1, 3), (2, 2))):
        out.append((i, j, LROW + 128, lane, 128, 0))
    for lane, (i, j, r) in enumerate(((2, 3, 0), (2, 3, 64), (3, 3, 0), (3, 3, 64))):
        out.append((i, j, LROW + 256, lane, 64, r))
    return out


def pack_spread(ref, full):
    for i, j, row, lane, rows, r0 in packed_blocks():
        ref[row : row + rows, lane * B : lane * B + B] = full(i * B + r0, rows, j * B)


def unpack_spread(load, full_ref):
    for i, j, row, lane, rows, r0 in packed_blocks():
        block = load(row, rows, lane * B)
        full_ref[i * B + r0 : i * B + r0 + rows, j * B : j * B + B] = block
    for i in range(4):
        for j in range(i + 1, 4):
            block = full_ref[i * B : i * B + B, j * B : j * B + B]
            full_ref[j * B : j * B + B, i * B : i * B + B] = jnp.transpose(block)


def tree_sum(terms):
    while len(terms) > 1:
        terms = [sum(terms[i + 1 : i + 2], terms[i]) for i in range(0, len(terms), 2)]
    return terms[0]


def small_mul(a, b):
    return [
        [tree_sum([a[i][t] * b[t][j] for t in range(len(b))]) for j in range(len(b[0]))] for i in range(len(a))
    ]


def small_inverse(m):
    n = len(m)
    if n == 2:
        a, b, d = m[0][0], m[0][1], m[1][1]
        inv = 1.0 / (a * d - b * b)
        return [[d * inv, -b * inv], [-b * inv, a * inv]]
    h = n // 2
    upper = [row[h:] for row in m[:h]]
    lower = [[upper[j][i] for j in range(h)] for i in range(h)]
    first = small_inverse([row[:h] for row in m[:h]])
    q = small_mul(lower, first)
    qb = small_mul(q, upper)
    schur = [[m[h + min(i, j)][h + max(i, j)] - qb[min(i, j)][max(i, j)] for j in range(h)] for i in range(h)]
    second = small_inverse(schur)
    sq = small_mul(second, q)
    qsq = small_mul([[q[j][i] for j in range(h)] for i in range(h)], sq)
    out = [[None] * n for _ in range(n)]
    for i in range(h):
        for j in range(h):
            out[i][j] = first[i][j] + qsq[i][j]
            out[h + i][h + j] = second[i][j]
            out[h + i][j] = out[j][h + i] = -sq[i][j]
    return out


PANEL = 64


def inverse128(block):
    groups = PANEL // 8
    row_id = lax.broadcasted_iota(jnp.int32, (8, B), 0)
    lane_id = lax.broadcasted_iota(jnp.int32, (8, B), 1)
    lanes = lax.broadcasted_iota(jnp.int32, (B, B), 1)

    def body(_, x):
        top = x[:PANEL, :]
        vs = [x[8 * k : 8 * k + 8, :] for k in range(groups)]
        for q in range(groups):
            at = 8 * q
            cols = [[jnp.broadcast_to(v[:, at + s : at + s + 1], (8, B)) for v in vs] for s in range(8)]
            rows = [jnp.broadcast_to(vs[q][s : s + 1, :], (8, B)) for s in range(8)]
            m = [[None] * 8 for _ in range(8)]
            for s in range(8):
                for t in range(s, 8):
                    m[s][t] = m[t][s] = jnp.broadcast_to(cols[s][q][t : t + 1, :], (8, B))
            inv = small_inverse(m)
            new_rows = [n[0] for n in small_mul(inv, [[r] for r in rows])]
            for s in range(8):
                for t in range(8):
                    new_rows[s] = jnp.where(lane_id == at + t, -inv[s][t], new_rows[s])
            inside = (lane_id >= at) & (lane_id < at + 8)
            for k in range(groups):
                if k == q:
                    new = new_rows[0]
                    for s in range(1, 8):
                        new = jnp.where(row_id == s, new_rows[s], new)
                else:
                    new = jnp.where(inside, 0.0, vs[k])
                    new -= tree_sum([cols[s][k] * new_rows[s] for s in range(8)])
                vs[k] = new
        done = jnp.concatenate(vs, axis=0)
        rest = jnp.where(lanes < PANEL, 0.0, x) - dot6(top, done, 0, 0)
        return pltpu.roll(jnp.concatenate([rest[PANEL:, :], done], axis=0), B - PANEL, 1)

    return -lax.fori_loop(0, B // PANEL, body, block)


def predict_kernel(pattern, cov_in, mean_a, mean_b, noise, blocks, cov, left, pred, vectors):
    c, z = lax.axis_index("tm_2"), lax.axis_index("state")
    for i in range(4):
        for t in range(3):
            lanes = slice((i + t) % 4 * B, (i + t) % 4 * B + B)
            cov[i * B : i * B + B, lanes] = cov_in[i, :, lanes]
        j = (i + 3) % 4
        cov[i * B : i * B + B, j * B : j * B + B] = jnp.transpose(cov_in[j, :, i * B : i * B + B])
    tb = lambda r, j: blocks[r, j]

    def rows_of(ref, block):
        return ref[pl.ds(pl.multiple_of(block * B, B), B), :]

    def lanes_of(ref, row, rows, block):
        return ref[row : row + rows, pl.ds(pl.multiple_of(block * B, B), B)]

    place = lax.rem(2 * z + c, 4)
    mean = jnp.where(z // 2 == c, mean_a[pl.ds(place, 1), :], mean_b[pl.ds(place, 1), :])
    vectors[0:8, :] = jnp.broadcast_to(mean, (8, N))
    pushed = []
    for r in range(4):
        t0, t1 = tb(r, 0), tb(r, 1)
        left[r * B : r * B + B, :] = dot6(t0, rows_of(cov, pattern[r, 0])) + dot6(
            t1, rows_of(cov, pattern[r, 1])
        )
        pushed.append(
            dot6(lanes_of(vectors, 0, 8, pattern[r, 0]), t0, 1)
            + dot6(lanes_of(vectors, 0, 8, pattern[r, 1]), t1, 1)
        )
    vectors[8:16, :] = jnp.concatenate(pushed, axis=1)
    eye = lax.broadcasted_iota(jnp.int32, (B, B), 0) == lax.broadcasted_iota(jnp.int32, (B, B), 1)
    for r in range(4):
        rows = (r + 1) * B
        value = dot6(lanes_of(left, 0, rows, pattern[r, 0]), tb(r, 0), 1) + dot6(
            lanes_of(left, 0, rows, pattern[r, 1]), tb(r, 1), 1
        )
        pred[0:rows, r * B : r * B + B] = value
        q = jnp.where(eye, jnp.broadcast_to(noise[0:1, r * B : r * B + B], (B, B)), 0.0)
        pred[r * B : rows, r * B : r * B + B] += q


def element(cov, left, pred_in, vectors, out, pred, sol, inv_ref, gain_ready):
    y, x, c, z = (lax.axis_index(a) for a in ("tm_0", "tm_1", "tm_2", "state"))
    pred[...] = pred_in[...]
    sol[...] = left[...]

    def eliminate(k, _):
        at = pl.ds(pl.multiple_of(k * B, B), B)
        inv_ref[...] = inverse128(pred[at, at])
        for kk in range(4):

            @pl.when(k == kk)
            def _():
                k0, k1 = kk * B, kk * B + B
                inv = inv_ref[...]
                ub = dot6(inv, sol[k0:k1, :])
                sol[k0:k1, :] = ub
                if kk < 3:
                    tail = pred[k0:k1, k1:]
                    ut = dot6(inv, tail)
                    st = jnp.transpose(tail)
                    pred[k1:, k1:] -= dot6(st, ut)
                    sol[k1:, :] -= dot6(st, ub)
                    pred[k0:k1, k1:] = ut

        return 0

    lax.fori_loop(0, 4, eliminate, 0)
    for k in (2, 1, 0):
        k0, k1 = k * B, k * B + B
        sol[k0:k1, :] -= dot6(pred[k0:k1, k1:], sol[k1:, :])
    keep = (8 * (4 * y + x) + 2 * z + c != 127).astype(F32)
    for i in range(4):
        for j in range(4):
            out[i * B : i * B + B, j * B : j * B + B] = (
                jnp.transpose(sol[j * B : j * B + B, i * B : i * B + B]) * keep
            )
    gain_ready()
    out[GROW : GROW + 8, :] = vectors[0:8, :] - keep * dot6(vectors[8:16, :], sol[...])
    out[GROW + 8 :, :] = jnp.zeros((ROWS - GROW - 8, N), F32)
    pred[...] = cov[...] - dot6(out[0:N, :], left[...])
    pack_spread(out, lambda r, n, c: pred[r : r + n, c : c + B])


def split_into(high, low, value):
    for r in range(4):
        rows = slice(r * B, r * B + B)
        high[rows, :], low[rows, :] = split(value(rows))


def chosen(me, own, other):
    def load(k, row, rows, lane=0, lanes=N):
        return jnp.where(k == me, own[row : row + rows, lane : lane + lanes], other(k, row, rows, lane, lanes))

    return load


def split_gains(count, load, work):
    eh, el = work[5:7]

    def body(k, _):
        split_into(eh.at[k], el.at[k], lambda rows: load(k, rows.start, B))
        return 0

    lax.fori_loop(0, count - 1, body, 0)


def gains(count, me, load, total, rest, work):
    se, _, _, rh, rl, eh, el, _ = work
    last = count - 1
    if rest is not None:

        @pl.when(me == last)
        def _():
            same = lax.broadcasted_iota(jnp.int32, (N, N), 0) == lax.broadcasted_iota(jnp.int32, (N, N), 1)
            rest[0:N, :] = same.astype(F32)

    def step(t, _):
        k = last - 1 - t
        now = lax.rem(t, 2)
        if rest is not None:

            @pl.when(k == me)
            def _():
                rest[0:N, :] = se[now]

        split_into(eh.at[k], el.at[k], lambda rows: load(k, rows.start, B))
        split_into(rh, rl, lambda rows: se[now, rows, :])
        se[1 - now] = dot_s((eh[k], el[k]), (rh[...], rl[...]))
        return 0

    se[0] = load(last, 0, N)
    lax.fori_loop(0, last, step, 0)
    total[0:N, :] = se[last % 2]


def spreads(count, me, load, total, rest, work):
    _, sl, sg, rh, rl, eh, el, lk = work
    last = count - 1
    if rest is not None:

        @pl.when(me == last)
        def _():
            rest[N:, :] = jnp.zeros((ROWS - N, N), F32)

    unpack_spread(lambda r, n, c: load(last, r, n, c, B), sl.at[0])
    sg[0] = load(last, GROW, 8)

    def keep(ref, slot):
        pack_spread(ref, lambda r, n, c: sl[slot, r : r + n, c : c + B])
        ref[GROW : GROW + 8, :] = sg[slot]
        ref[GROW + 8 :, :] = jnp.zeros((ROWS - GROW - 8, N), F32)

    def step(t, _):
        k = last - 1 - t
        now = lax.rem(t, 2)
        if rest is not None:

            @pl.when(k == me)
            def _():
                keep(rest, now)

        split_into(rh, rl, lambda rows: sl[now, rows, :])
        unpack_spread(lambda r, n, c: load(k, r, n, c, B), lk)
        e = (eh[k], el[k])
        sg[1 - now] = dot_s(split(sg[now]), e, 1) + load(k, GROW, 8)
        half = split(dot_s(e, (rh[...], rl[...])))
        sl[1 - now] = dot_s(half, e, 1) + lk[...]
        return 0

    lax.fori_loop(0, last, step, 0)
    if total is not None:
        keep(total, last % 2)


def from_slots(others):
    return lambda k, row, rows, lane, lanes: others[k, row : row + rows, lane : lane + lanes]


def greet(peers):
    barrier = pltpu.get_barrier_semaphore()
    for peer in peers:
        pl.semaphore_signal(barrier, inc=1, device_id=peer, device_id_type=MESH)
    pl.semaphore_wait(barrier, len(peers))


def column_peers(z, c):
    return [
        {"state": lax.rem(z + dz, 4), "tm_2": c if dc == 0 else 1 - c}
        for dz in range(4)
        for dc in range(2)
        if dz or dc
    ]


def remote(src, dst, send, recv, peer):
    return pltpu.make_async_remote_copy(
        src_ref=src, dst_ref=dst, send_sem=send, recv_sem=recv, device_id=peer, device_id_type=MESH
    )


def lanes_of_block(ref, j):
    return ref.at[:, pl.ds(pl.multiple_of(lax.rem(j, 4) * B, B), B)]


def gather_step_kernel(
    cov,
    mean,
    noise,
    blocks,
    out,
    mean_out,
    mean_here,
    noise_here,
    blocks_here,
    relay,
    send,
    recv,
    relay_send,
    relay_recv,
    local,
    msend,
    mrecv,
    small,
):
    z, c = lax.axis_index("state"), lax.axis_index("tm_2")
    greet(column_peers(z, c))
    other = remote(mean, mean_out, msend, mrecv, {"tm_2": 1 - c})
    other.start()
    here = [
        pltpu.make_async_copy(src, dst, small.at[n])
        for n, (src, dst) in enumerate(((mean, mean_here), (noise, noise_here), (blocks, blocks_here)))
    ]
    for copy_here in here:
        copy_here.start()

    def start(src, dst, row, ssem, rsem, peer):
        for t in range(3):
            remote(lanes_of_block(src, row + t), lanes_of_block(dst, row + t), ssem, rsem, peer).start()

    def whole(ref, ssem, rsem):
        part = ref.at[:, 0 : 3 * B]
        return remote(part, part, ssem, rsem, {"state": 0, "tm_2": 0})

    def target(i):
        dz, e = 2 * c + i // 2, i % 2
        mine = (z == dz) & (c == e)
        far = lax.rem(dz + 4 - z, 4) == 2
        return dz, e, mine, far

    for i in range(4):
        dz, e, mine, far = target(i)

        @pl.when(far)
        def _():
            start(cov.at[i], relay.at[e], z, send.at[i], relay_recv.at[e], {"state": lax.rem(z + (3 if e else 1), 4)})

    for i in range(4):
        dz, e, mine, far = target(i)

        @pl.when(mine)
        def _():
            pltpu.make_async_copy(cov.at[i], out.at[z], local).start()

        @pl.when(jnp.logical_not(mine | far))
        def _():
            start(cov.at[i], out.at[z], z, send.at[i], recv.at[z], {"state": dz, "tm_2": e})

    duties = []
    for e in range(2):
        source, dz = lax.rem(z + (1 if e else 3), 4), lax.rem(z + (3 if e else 1), 4)
        duty = source // 2 != c
        duties.append(duty)

        @pl.when(duty)
        def _():
            whole(relay.at[e], send.at[0], relay_recv.at[e]).wait_recv()
            start(relay.at[e], out.at[source], source, relay_send.at[e], recv.at[source], {"state": dz, "tm_2": e})

    for i in range(4):
        dz, e, mine, far = target(i)

        @pl.when(mine)
        def _():
            pltpu.make_async_copy(cov.at[i], out.at[z], local).wait()

        @pl.when(jnp.logical_not(mine))
        def _():
            whole(cov.at[i], send.at[i], recv.at[0]).wait_send()

    for e in range(2):

        @pl.when(duties[e])
        def _():
            whole(relay.at[e], relay_send.at[e], recv.at[0]).wait_send()

    source_core = z // 2
    for s in range(4):

        @pl.when(jnp.logical_not((z == s) & (c == source_core)))
        def _():
            whole(out.at[s], send.at[0], recv.at[s]).wait_recv()

    other.wait()
    for copy_here in here:
        copy_here.wait()


def final_kernel(
    row,
    rows,
    across,
    down,
    pair,
    own,
    out,
    mean_out,
    cov,
    mean,
    add,
    relay,
    sl,
    sg,
    rh,
    rl,
    eh,
    el,
    lk,
    send,
    recv,
    relay_send,
    relay_recv,
    local,
    msend,
    mrecv,
):
    z, c, me = lax.axis_index("state"), lax.axis_index("tm_2"), lax.axis_index("tm_0")
    barrier = pltpu.get_barrier_semaphore()
    peers = column_peers(z, c)
    for peer in peers:
        pl.semaphore_signal(barrier, inc=1, device_id=peer, device_id_type=MESH)
    load = chosen(me, row, from_slots(rows))

    @pl.when(me == 3)
    def _():
        cov[...] = jnp.zeros((N, N), F32)
        mean[...] = jnp.zeros((8, N), F32)

    @pl.when(me == 2)
    def _():
        unpack_spread(lambda r, n, c: load(3, r, n, c, B), cov)
        mean[...] = load(3, GROW, 8)

    @pl.when(me < 2)
    def _():
        unpack_spread(lambda r, n, c: load(3, r, n, c, B), sl)
        sg[...] = load(3, GROW, 8)

    def take(get):
        split_into(eh, el, lambda r: get(r.start, B))
        unpack_spread(lambda r, n, c: get(r, n, c, B), lk)
        add[...] = get(GROW, 8)

    def push(state, offset):
        split_into(rh, rl, lambda r: state[r, :])
        e = (eh[...], el[...])
        offset[...] = dot_s(split(offset[...]), e, 1) + add[...]
        state[...] = dot_s(split(dot_s(e, (rh[...], rl[...]))), e, 1) + lk[...]

    choices = (
        lambda r, n, c=0, m=N: load(2, r, n, c, m),
        lambda r, n, c=0, m=N: load(1, r, n, c, m),
        lambda r, n, c=0, m=N: across[r : r + n, c : c + m],
        lambda r, n, c=0, m=N: down[r : r + n, c : c + m],
        lambda r, n, c=0, m=N: jnp.where(
            lax.axis_index("tm_2") == 0, pair[r : r + n, c : c + m], own[r : r + n, c : c + m]
        ),
    )

    def early(t, _):
        @pl.when(me < 2 - t)
        def _():
            for k in range(2):
                pl.when(t == k)(partial(take, choices[k]))
            push(sl, sg)

        @pl.when(me == 1 - t)
        def _():
            cov[...] = sl[...]
            mean[...] = sg[...]

        return 0

    lax.fori_loop(0, 2, early, 0)

    def late(t, _):
        for k in range(3):
            pl.when(t == k)(partial(take, choices[2 + k]))
        push(cov, mean)
        return 0

    lax.fori_loop(0, 3, late, 0)
    pl.semaphore_wait(barrier, len(peers))

    core = z // 2
    slot = 2 * lax.rem(z, 2) + c
    opposite = lax.rem(z + 2, 4)
    onward = lax.rem(z + 1 + 2 * c, 4)

    def slab(t):
        return cov.at[pl.ds(pl.multiple_of(t * B, B), B), :]

    far = remote(slab(opposite), relay, relay_send.at[0], relay_recv, {"state": onward})
    far.start()

    def copy(t):
        return remote(slab(t), out.at[slot], send.at[t], recv.at[slot], {"state": t, "tm_2": core})

    def mean_copy(t):
        return remote(mean, mean_out.at[slot], msend.at[t], mrecv.at[slot], {"state": t, "tm_2": core})

    def mine(t):
        return (z == t) & (c == core)

    def copies(t):
        return pltpu.make_async_copy(slab(t), out.at[slot], local.at[0]), pltpu.make_async_copy(
            mean, mean_out.at[slot], local.at[1]
        )

    for t in range(4):

        @pl.when(mine(t))
        def _():
            for copy_here in copies(t):
                copy_here.start()

        @pl.when(jnp.logical_not(mine(t)))
        def _():
            mean_copy(t).start()

        @pl.when(jnp.logical_not(mine(t)) & (t != opposite))
        def _():
            copy(t).start()

    source = lax.rem(z + 3 + 2 * c, 4)
    far.wait_recv()
    on = remote(
        relay,
        out.at[2 * lax.rem(source, 2) + c],
        relay_send.at[1],
        recv.at[2 * lax.rem(source, 2) + c],
        {"state": onward, "tm_2": source // 2},
    )
    on.start()
    for t in range(4):

        @pl.when(mine(t))
        def _():
            for copy_here in copies(t):
                copy_here.wait()

        @pl.when(jnp.logical_not(mine(t)))
        def _():
            mean_copy(t).wait_send()

        @pl.when(jnp.logical_not(mine(t)) & (t != opposite))
        def _():
            copy(t).wait_send()

    far.wait_send()
    on.wait_send()
    for i in range(4):

        @pl.when(jnp.logical_not((z == 2 * c + i // 2) & (c == i % 2)))
        def _():
            remote(slab(0), out.at[i], send.at[0], recv.at[i], {"state": 0, "tm_2": 0}).wait_recv()
            remote(mean, mean_out.at[i], msend.at[0], mrecv.at[i], {"state": 0, "tm_2": 0}).wait_recv()


class Copies:
    def __init__(self, out, send, recv):
        self.out, self.send, self.recv, self.used, self.sent = out, send, recv, 0, []

    def put(self, peer, slot, row, rows, src=None):
        n, self.used = self.used, self.used + 1
        place = self.out.at[slot, pl.ds(pl.multiple_of(row, 8), rows), :]
        copy = remote(place if src is None else src, place, self.send.at[n], self.recv.at[n], peer)
        copy.start()
        self.sent.append(copy)
        return n

    def arrived(self, n, slot, row, rows):
        place = self.out.at[slot, pl.ds(pl.multiple_of(row, 8), rows), :]
        remote(place, place, self.send.at[n], self.recv.at[n], {"tm_2": 0}).wait_recv()

    def finish(self):
        for copy in self.sent:
            copy.wait_send()


Z_PIECES = (((0, 64), (64, 64), (128, 64), (192, 64)), ((0, 48), (48, 40), (88, 40), (128, 40)))
Z_HALF = (256, 168)


def pair_kernel(cov, left, pred, vectors, own, total, out, twin_buf, *refs):
    scratch, work, (swap_send, swap_recv, send, recv) = refs[:3], refs[3:11], refs[11:]
    z, c = lax.axis_index("state"), lax.axis_index("tm_2")
    zu, zd, zo = lax.rem(z + 1, 4), lax.rem(z + 3, 4), lax.rem(z + 2, 4)
    up, down, twin = {"state": zu}, {"state": zd}, {"tm_2": 1 - c}
    barrier = pltpu.get_barrier_semaphore()
    for peer in (up, down, twin):
        pl.semaphore_signal(barrier, inc=1, device_id=peer, device_id_type=MESH)
    swaps = [
        remote(own.at[rows], twin_buf.at[rows], swap_send.at[part], swap_recv.at[part], twin)
        for part, rows in ((0, pl.ds(0, N)), (1, pl.ds(N, ROWS - N)))
    ]

    def gain_ready():
        pl.semaphore_wait(barrier, 3)
        swaps[0].start()

    element(cov, left, pred, vectors, own, *scratch, gain_ready)
    swaps[1].start()
    cp = Copies(out, send, recv)
    ups, downs, tails, twins = [], [], [], []

    def rows_of(part, core, piece):
        return (N if part else 0) + core * Z_HALF[part] + piece[0], piece[1]

    def first_hop(part):
        pieces = Z_PIECES[part]
        for j, (a, b) in enumerate(zip(pieces, pieces[::-1])):
            for into, peer, piece in ((ups, up, a), (downs, down, b)):
                row, rows = rows_of(part, c, piece)
                n = cp.put(peer, z, row, rows, total.at[pl.ds(pl.multiple_of(row, 8), rows), :])
                into.append((n, part, piece, j < len(pieces) // 2))

    load = chosen(c, own, lambda k, row, rows, lane, lanes: twin_buf[row : row + rows, lane : lane + lanes])
    swaps[0].wait()
    gains(2, c, load, total, None, work)
    first_hop(0)
    swaps[1].wait()
    spreads(2, c, load, total, None, work)
    first_hop(1)

    def hand(slot, part, piece):
        row, rows = rows_of(part, c, piece)
        twins.append((cp.put(twin, slot, row, rows), slot, rows_of(part, 1 - c, piece)))

    for pair in zip(ups, downs):
        for (n, part, piece, further), slot, peer in zip(pair, (zd, zu), (up, down)):
            row, rows = rows_of(part, c, piece)
            cp.arrived(n, slot, row, rows)
            if further:
                tails.append((cp.put(peer, slot, row, rows), part, piece))
            hand(slot, part, piece)
    for n, part, piece in tails:
        row, rows = rows_of(part, c, piece)
        cp.arrived(n, zo, row, rows)
        hand(zo, part, piece)
    for n, slot, (row, rows) in twins:
        cp.arrived(n, slot, row, rows)
    cp.finish()


QUARTER = (128, 88)
PIECES = (((0, 32), (32, 32), (64, 32), (96, 32)), ((0, 24), (24, 24), (48, 24), (72, 16)))


def ring_kernel(mine, axis, own, others, rest, out, total, *refs):
    z, c, a = lax.axis_index("state"), lax.axis_index("tm_2"), lax.axis_index(axis)
    work, (send, recv, twin_send, twin_recv) = refs[:8], refs[8:]
    me = lax.axis_index(mine)
    zu, zd, zo = lax.rem(z + 1, 4), lax.rem(z + 3, 4), lax.rem(z + 2, 4)
    au, ad, ao = lax.rem(a + 1, 4), lax.rem(a + 3, 4), lax.rem(a + 2, 4)
    up, down = {axis: au}, {axis: ad}
    above, below, twin = {"state": zu}, {"state": zd}, {"tm_2": 1 - c}
    peers = [up, down, above, below, twin]
    barrier = pltpu.get_barrier_semaphore()
    for peer in peers:
        pl.semaphore_signal(barrier, inc=1, device_id=peer, device_id_type=MESH)
    quarters = (z, zu)
    coming = (zd, zo)
    load = chosen(me, own, from_slots(others))

    def run(part):
        base, pieces = N if part else 0, PIECES[part]
        span = pl.ds(base, 4 * QUARTER[part])
        if part:
            split_gains(4, load, work)
            spreads(4, me, load, total, rest, work)
        else:
            gains(4, me, load, total, rest, work)
        pl.semaphore_wait(barrier, len(peers))
        cp = Copies(out, send, recv)

        def hand(src, dst, sem):
            copy = remote(src, dst, twin_send.at[sem], twin_recv.at[sem], twin)
            copy.start()

        def row_of(quarter, j):
            return pl.multiple_of(base + quarter * QUARTER[part] + pieces[j][0], 8)

        count = len(pieces)
        ups, downs, zs, tails = [], [], [], []
        for j in range(count):
            for k in (0, 1):
                for into, peer, jj in ((ups, up, j), (downs, down, count - 1 - j)):
                    row = row_of(quarters[k], jj)
                    n = cp.put(peer, a, row, pieces[jj][1], total.at[pl.ds(row, pieces[jj][1]), :])
                    into.append((n, k, jj, j < count // 2))
        hand(total.at[span], total.at[span], 0)
        hand(rest.at[span], rest.at[span], 1)

        def pass_on(slot, row, j):
            place = out.at[slot, pl.ds(row, pieces[j][1]), :]
            hand(place, place, 2)

        def spread(slot, k, j):
            row = row_of(quarters[k], j)
            zs.append((cp.put(below if k else above, slot, row, pieces[j][1]), slot, k, j))
            pass_on(slot, row, j)

        def take(keep):
            while len(zs) > keep:
                n, slot, k, j = zs.pop(0)
                row = row_of(coming[k], j)
                cp.arrived(n, slot, row, pieces[j][1])
                pass_on(slot, row, j)

        for pair in zip(ups, downs):
            for (n, k, j, further), slot, peer in zip(pair, (ad, au), (up, down)):
                row = row_of(quarters[k], j)
                cp.arrived(n, slot, row, pieces[j][1])
                if further:
                    tails.append((cp.put(peer, slot, row, pieces[j][1]), k, j))
                spread(slot, k, j)
        for n, k, j in tails:
            cp.arrived(n, ao, row_of(quarters[k], j), pieces[j][1])
            spread(ao, k, j)
            take(len(zs) - 2)
        take(0)
        cp.finish()
        other = pl.ds(0 if part else N, 4 * QUARTER[1 - part])
        for sem, ref in enumerate((total, rest)):
            remote(ref.at[span], ref.at[span], twin_send.at[sem], twin_recv.at[sem], twin).wait_send()
            remote(ref.at[other], ref.at[other], twin_send.at[sem], twin_recv.at[sem], twin).wait_recv()
        sent, came = out.at[0:3, span], out.at[0:3, other]
        remote(sent, sent, twin_send.at[2], twin_recv.at[2], twin).wait_send()
        remote(came, came, twin_send.at[2], twin_recv.at[2], twin).wait_recv()

    for part in (0, 1):
        pl.when(c == part)(partial(run, part))


def shape(*dims, dtype=F32):
    return jax.ShapeDtypeStruct(dims, dtype)


def params(limit=None, **more):
    return pltpu.CompilerParams(vmem_limit_bytes=limit, **more)


DMA = pltpu.SemaphoreType.DMA


def comm(kernel, name, collective_id, outs, scratch, *args, limit, in_spec=ANY, out_spec=ANY):
    return pl.pallas_call(
        kernel,
        name=name,
        out_shape=outs,
        in_specs=[in_spec] * len(args),
        out_specs=jax.tree.map(lambda _: out_spec, outs),
        scratch_shapes=scratch,
        compiler_params=pltpu.CompilerParams(
            collective_id=collective_id, has_side_effects=True, vmem_limit_bytes=limit
        ),
    )(*args)


def suffix_work(count):
    return [
        pltpu.VMEM((2, N, N), F32),
        pltpu.VMEM((2, N, N), F32),
        pltpu.VMEM((2, 8, N), F32),
        pltpu.VMEM((N, N), BF16),
        pltpu.VMEM((N, N), BF16),
        pltpu.VMEM((count - 1, N, N), BF16),
        pltpu.VMEM((count - 1, N, N), BF16),
        pltpu.VMEM((N, N), F32),
    ]


def ring(name, collective_id, mine, axis, own, others):
    packet = shape(ROWS, N)
    return pl.pallas_call(
        partial(ring_kernel, mine, axis),
        name=name,
        out_shape=(packet, shape(4, ROWS, N), packet),
        in_specs=[VM, VM],
        out_specs=(VM, VM, VM),
        scratch_shapes=suffix_work(4) + [DMA((48,)), DMA((48,)), DMA((3,)), DMA((3,))],
        compiler_params=params(RING_LIMIT, collective_id=collective_id, has_side_effects=True),
    )(own, others)


RING_LIMIT = 24 * 1024 * 1024
FIRST_LIMIT = 4 * 1024 * 1024


def on_device(filtered_cov, filtered_mean, noise_var, trans_blocks, pattern):
    z = lax.axis_index("state")
    cov, twin_mean, mean_here, noise_here, blocks_here = comm(
        gather_step_kernel,
        "gather_step",
        0,
        (shape(4, B, N), shape(4, N), shape(4, N), shape(1, N), shape(4, 2, B, B)),
        [pltpu.VMEM((2, B, N), F32), DMA((4,)), DMA((4,)), DMA((2,)), DMA((2,)), DMA, DMA, DMA, DMA((3,))],
        filtered_cov,
        filtered_mean,
        noise_var.reshape(1, N),
        trans_blocks,
        limit=FIRST_LIMIT,
        out_spec=VM,
    )
    packet, packets = shape(ROWS, N), shape(4, ROWS, N)
    square = shape(N, N)
    predicted = pl.pallas_call(
        predict_kernel,
        name="predict",
        out_shape=(square, square, square, shape(16, N)),
        in_specs=[SM] + [VM] * 5,
        out_specs=(VM, VM, VM, VM),
        compiler_params=params(RING_LIMIT),
    )(pattern, cov, mean_here, twin_mean, noise_here, blocks_here)
    own, pair, pairs = pl.pallas_call(
        pair_kernel,
        name="pair",
        out_shape=(packet, packet, packets),
        in_specs=[VM] * 4,
        out_specs=(VM, VM, VM),
        scratch_shapes=[pltpu.VMEM((ROWS, N), F32)]
        + [pltpu.VMEM((N, N), F32)] * 2
        + [pltpu.VMEM((B, B), F32)]
        + suffix_work(2)
        + [DMA((2,)), DMA((2,)), DMA((48,)), DMA((48,))],
        compiler_params=params(RING_LIMIT, collective_id=2, has_side_effects=True),
    )(*predicted)
    down, columns, column = ring("ring_x", 3, "state", "tm_1", pair, pairs)
    across, rows, row = ring("ring_y", 4, "tm_1", "tm_0", column, columns)
    half = pltpu.VMEM((N, N), BF16)
    smooth_cov, means = pl.pallas_call(
        final_kernel,
        name="final",
        out_shape=(shape(4, B, N), shape(4, 8, N)),
        in_specs=[VM] * 6,
        out_specs=(VM, VM),
        scratch_shapes=[pltpu.VMEM((N, N), F32), pltpu.VMEM((8, N), F32), pltpu.VMEM((8, N), F32), pltpu.VMEM((B, N), F32)]
        + [pltpu.VMEM((N, N), F32), pltpu.VMEM((8, N), F32), half, half, half, half, pltpu.VMEM((N, N), F32)]
        + [DMA((4,)), DMA((4,)), DMA((2,)), DMA, DMA((2,)), DMA((4,)), DMA((4,))],
        compiler_params=params(RING_LIMIT, collective_id=5, has_side_effects=True),
    )(row, rows, across, down, pair, own)
    return lax.dynamic_slice_in_dim(means[:, 0, :], z * B, B, 1), smooth_cov


def solution(mesh):
    torus = Mesh(
        mesh.devices.reshape(4, 4, 2, mesh.shape["state"]), ("tm_0", "tm_1", "tm_2", "state")
    )
    return jax.shard_map(
        on_device,
        mesh=torus,
        in_specs=(P(TM, "state", None), P(TM, None), P(), P(), P()),
        out_specs=(P(TM, "state"), P(TM, "state", None)),
        check_vma=False,
    )
```

```python
from functools import partial

import jax
import jax.numpy as jnp
from jax import lax
from jax.experimental import pallas as pl
from jax.experimental.pallas import tpu as pltpu
from jax.sharding import Mesh
from jax.sharding import PartitionSpec as P

N = 512
B = 128
LROW = 512
GROW = 832
ROWS = 896
MESH = pl.DeviceIdType.MESH
F32 = jnp.float32
BF16 = jnp.bfloat16
ANY = pl.BlockSpec(memory_space=pl.ANY)
VM = pl.BlockSpec(memory_space=pltpu.VMEM)
SM = pl.BlockSpec(memory_space=pltpu.SMEM)
TM = ("tm_0", "tm_1", "tm_2")


def split(x):
    high = x.astype(BF16)
    return high, (x - high.astype(F32)).astype(BF16)


def dg(a, b, cb=0):
    return lax.dot_general(a, b, (((1,), (cb,)), ((), ())), preferred_element_type=F32)


def dot_s(a, b, cb=0):
    return dg(a[0], b[0], cb) + (dg(a[0], b[1], cb) + dg(a[1], b[0], cb))


def dot3(a, b, cb=0):
    return dot_s(split(a), split(b), cb)


def dot6(a, b, cb=0, ca=1):
    return lax.dot_general(
        a, b, (((ca,), (cb,)), ((), ())), precision=lax.Precision.HIGHEST, preferred_element_type=F32
    )


def packed_blocks():
    out = []
    for j in range(4):
        out.append((0, j, LROW, j, 128, 0))
    for lane, (i, j) in enumerate(((1, 1), (1, 2), (1, 3), (2, 2))):
        out.append((i, j, LROW + 128, lane, 128, 0))
    for lane, (i, j, r) in enumerate(((2, 3, 0), (2, 3, 64), (3, 3, 0), (3, 3, 64))):
        out.append((i, j, LROW + 256, lane, 64, r))
    return out


def pack_spread(ref, full):
    for i, j, row, lane, rows, r0 in packed_blocks():
        ref[row : row + rows, lane * B : lane * B + B] = full(i * B + r0, rows, j * B)


def unpack_spread(load, full_ref):
    for i, j, row, lane, rows, r0 in packed_blocks():
        block = load(row, rows, lane * B)
        full_ref[i * B + r0 : i * B + r0 + rows, j * B : j * B + B] = block
    for i in range(4):
        for j in range(i + 1, 4):
            block = full_ref[i * B : i * B + B, j * B : j * B + B]
            full_ref[j * B : j * B + B, i * B : i * B + B] = jnp.transpose(block)


def tree_sum(terms):
    while len(terms) > 1:
        terms = [sum(terms[i + 1 : i + 2], terms[i]) for i in range(0, len(terms), 2)]
    return terms[0]


def small_mul(a, b):
    return [
        [tree_sum([a[i][t] * b[t][j] for t in range(len(b))]) for j in range(len(b[0]))] for i in range(len(a))
    ]


def small_inverse(m):
    n = len(m)
    if n == 2:
        a, b, d = m[0][0], m[0][1], m[1][1]
        inv = 1.0 / (a * d - b * b)
        return [[d * inv, -b * inv], [-b * inv, a * inv]]
    h = n // 2
    upper = [row[h:] for row in m[:h]]
    lower = [[upper[j][i] for j in range(h)] for i in range(h)]
    first = small_inverse([row[:h] for row in m[:h]])
    q = small_mul(lower, first)
    qb = small_mul(q, upper)
    schur = [[m[h + min(i, j)][h + max(i, j)] - qb[min(i, j)][max(i, j)] for j in range(h)] for i in range(h)]
    second = small_inverse(schur)
    sq = small_mul(second, q)
    qsq = small_mul([[q[j][i] for j in range(h)] for i in range(h)], sq)
    out = [[None] * n for _ in range(n)]
    for i in range(h):
        for j in range(h):
            out[i][j] = first[i][j] + qsq[i][j]
            out[h + i][h + j] = second[i][j]
            out[h + i][j] = out[j][h + i] = -sq[i][j]
    return out


PANEL = 64


def inverse128(block):
    groups = PANEL // 8
    row_id = lax.broadcasted_iota(jnp.int32, (8, B), 0)
    lane_id = lax.broadcasted_iota(jnp.int32, (8, B), 1)
    lanes = lax.broadcasted_iota(jnp.int32, (B, B), 1)

    def body(_, x):
        top = x[:PANEL, :]
        vs = [x[8 * k : 8 * k + 8, :] for k in range(groups)]
        for q in range(groups):
            at = 8 * q
            cols = [[jnp.broadcast_to(v[:, at + s : at + s + 1], (8, B)) for v in vs] for s in range(8)]
            rows = [jnp.broadcast_to(vs[q][s : s + 1, :], (8, B)) for s in range(8)]
            m = [[None] * 8 for _ in range(8)]
            for s in range(8):
                for t in range(s, 8):
                    m[s][t] = m[t][s] = jnp.broadcast_to(cols[s][q][t : t + 1, :], (8, B))
            inv = small_inverse(m)
            new_rows = [n[0] for n in small_mul(inv, [[r] for r in rows])]
            for s in range(8):
                for t in range(8):
                    new_rows[s] = jnp.where(lane_id == at + t, -inv[s][t], new_rows[s])
            inside = (lane_id >= at) & (lane_id < at + 8)
            for k in range(groups):
                if k == q:
                    new = new_rows[0]
                    for s in range(1, 8):
                        new = jnp.where(row_id == s, new_rows[s], new)
                else:
                    new = jnp.where(inside, 0.0, vs[k])
                    new -= tree_sum([cols[s][k] * new_rows[s] for s in range(8)])
                vs[k] = new
        done = jnp.concatenate(vs, axis=0)
        rest = jnp.where(lanes < PANEL, 0.0, x) - dot6(top, done, 0, 0)
        return pltpu.roll(jnp.concatenate([rest[PANEL:, :], done], axis=0), B - PANEL, 1)

    return -lax.fori_loop(0, B // PANEL, body, block)


def predict_kernel(pattern, cov_in, mean_a, mean_b, noise, blocks, cov, left, pred, vectors):
    c, z = lax.axis_index("tm_2"), lax.axis_index("state")
    for i in range(4):
        for t in range(3):
            lanes = slice((i + t) % 4 * B, (i + t) % 4 * B + B)
            cov[i * B : i * B + B, lanes] = cov_in[i, :, lanes]
        j = (i + 3) % 4
        cov[i * B : i * B + B, j * B : j * B + B] = jnp.transpose(cov_in[j, :, i * B : i * B + B])
    tb = lambda r, j: blocks[r, j]

    def rows_of(ref, block):
        return ref[pl.ds(pl.multiple_of(block * B, B), B), :]

    def lanes_of(ref, row, rows, block):
        return ref[row : row + rows, pl.ds(pl.multiple_of(block * B, B), B)]

    place = lax.rem(2 * z + c, 4)
    mean = jnp.where(z // 2 == c, mean_a[pl.ds(place, 1), :], mean_b[pl.ds(place, 1), :])
    vectors[0:8, :] = jnp.broadcast_to(mean, (8, N))
    pushed = []
    for r in range(4):
        t0, t1 = tb(r, 0), tb(r, 1)
        left[r * B : r * B + B, :] = dot6(t0, rows_of(cov, pattern[r, 0])) + dot6(
            t1, rows_of(cov, pattern[r, 1])
        )
        pushed.append(
            dot6(lanes_of(vectors, 0, 8, pattern[r, 0]), t0, 1)
            + dot6(lanes_of(vectors, 0, 8, pattern[r, 1]), t1, 1)
        )
    vectors[8:16, :] = jnp.concatenate(pushed, axis=1)
    eye = lax.broadcasted_iota(jnp.int32, (B, B), 0) == lax.broadcasted_iota(jnp.int32, (B, B), 1)
    for r in range(4):
        rows = (r + 1) * B
        value = dot6(lanes_of(left, 0, rows, pattern[r, 0]), tb(r, 0), 1) + dot6(
            lanes_of(left, 0, rows, pattern[r, 1]), tb(r, 1), 1
        )
        pred[0:rows, r * B : r * B + B] = value
        q = jnp.where(eye, jnp.broadcast_to(noise[0:1, r * B : r * B + B], (B, B)), 0.0)
        pred[r * B : rows, r * B : r * B + B] += q


def element(cov, left, pred_in, vectors, out, pred, sol, inv_ref, gain_ready):
    y, x, c, z = (lax.axis_index(a) for a in ("tm_0", "tm_1", "tm_2", "state"))
    pred[...] = pred_in[...]
    sol[...] = left[...]

    def eliminate(k, _):
        at = pl.ds(pl.multiple_of(k * B, B), B)
        inv_ref[...] = inverse128(pred[at, at])
        for kk in range(4):

            @pl.when(k == kk)
            def _():
                k0, k1 = kk * B, kk * B + B
                inv = inv_ref[...]
                ub = dot6(inv, sol[k0:k1, :])
                sol[k0:k1, :] = ub
                if kk < 3:
                    tail = pred[k0:k1, k1:]
                    ut = dot6(inv, tail)
                    st = jnp.transpose(tail)
                    pred[k1:, k1:] -= dot6(st, ut)
                    sol[k1:, :] -= dot6(st, ub)
                    pred[k0:k1, k1:] = ut

        return 0

    lax.fori_loop(0, 4, eliminate, 0)
    for k in (2, 1, 0):
        k0, k1 = k * B, k * B + B
        sol[k0:k1, :] -= dot6(pred[k0:k1, k1:], sol[k1:, :])
    keep = (8 * (4 * y + x) + 2 * z + c != 127).astype(F32)
    for i in range(4):
        for j in range(4):
            out[i * B : i * B + B, j * B : j * B + B] = (
                jnp.transpose(sol[j * B : j * B + B, i * B : i * B + B]) * keep
            )
    gain_ready()
    out[GROW : GROW + 8, :] = vectors[0:8, :] - keep * dot6(vectors[8:16, :], sol[...])
    out[GROW + 8 :, :] = jnp.zeros((ROWS - GROW - 8, N), F32)
    pred[...] = cov[...] - dot6(out[0:N, :], left[...])
    pack_spread(out, lambda r, n, c: pred[r : r + n, c : c + B])


def split_into(high, low, value):
    for r in range(4):
        rows = slice(r * B, r * B + B)
        high[rows, :], low[rows, :] = split(value(rows))


def chosen(me, own, other):
    def load(k, row, rows, lane=0, lanes=N):
        return jnp.where(k == me, own[row : row + rows, lane : lane + lanes], other(k, row, rows, lane, lanes))

    return load


def split_gains(count, load, work):
    eh, el = work[5:7]

    def body(k, _):
        split_into(eh.at[k], el.at[k], lambda rows: load(k, rows.start, B))
        return 0

    lax.fori_loop(0, count - 1, body, 0)


def gains(count, me, load, total, rest, work):
    se, _, _, rh, rl, eh, el, _ = work
    last = count - 1
    if rest is not None:

        @pl.when(me == last)
        def _():
            same = lax.broadcasted_iota(jnp.int32, (N, N), 0) == lax.broadcasted_iota(jnp.int32, (N, N), 1)
            rest[0:N, :] = same.astype(F32)

    def step(t, _):
        k = last - 1 - t
        now = lax.rem(t, 2)
        if rest is not None:

            @pl.when(k == me)
            def _():
                rest[0:N, :] = se[now]

        split_into(eh.at[k], el.at[k], lambda rows: load(k, rows.start, B))
        split_into(rh, rl, lambda rows: se[now, rows, :])
        se[1 - now] = dot_s((eh[k], el[k]), (rh[...], rl[...]))
        return 0

    se[0] = load(last, 0, N)
    lax.fori_loop(0, last, step, 0)
    total[0:N, :] = se[last % 2]


def spreads(count, me, load, total, rest, work):
    _, sl, sg, rh, rl, eh, el, lk = work
    last = count - 1
    if rest is not None:

        @pl.when(me == last)
        def _():
            rest[N:, :] = jnp.zeros((ROWS - N, N), F32)

    unpack_spread(lambda r, n, c: load(last, r, n, c, B), sl.at[0])
    sg[0] = load(last, GROW, 8)

    def keep(ref, slot):
        pack_spread(ref, lambda r, n, c: sl[slot, r : r + n, c : c + B])
        ref[GROW : GROW + 8, :] = sg[slot]
        ref[GROW + 8 :, :] = jnp.zeros((ROWS - GROW - 8, N), F32)

    def step(t, _):
        k = last - 1 - t
        now = lax.rem(t, 2)
        if rest is not None:

            @pl.when(k == me)
            def _():
                keep(rest, now)

        split_into(rh, rl, lambda rows: sl[now, rows, :])
        unpack_spread(lambda r, n, c: load(k, r, n, c, B), lk)
        e = (eh[k], el[k])
        sg[1 - now] = dot_s(split(sg[now]), e, 1) + load(k, GROW, 8)
        half = split(dot_s(e, (rh[...], rl[...])))
        sl[1 - now] = dot_s(half, e, 1) + lk[...]
        return 0

    lax.fori_loop(0, last, step, 0)
    if total is not None:
        keep(total, last % 2)


def from_slots(others):
    return lambda k, row, rows, lane, lanes: others[k, row : row + rows, lane : lane + lanes]


def greet(peers):
    barrier = pltpu.get_barrier_semaphore()
    for peer in peers:
        pl.semaphore_signal(barrier, inc=1, device_id=peer, device_id_type=MESH)
    pl.semaphore_wait(barrier, len(peers))


def column_peers(z, c):
    return [
        {"state": lax.rem(z + dz, 4), "tm_2": c if dc == 0 else 1 - c}
        for dz in range(4)
        for dc in range(2)
        if dz or dc
    ]


def remote(src, dst, send, recv, peer):
    return pltpu.make_async_remote_copy(
        src_ref=src, dst_ref=dst, send_sem=send, recv_sem=recv, device_id=peer, device_id_type=MESH
    )


def lanes_of_block(ref, j):
    return ref.at[:, pl.ds(pl.multiple_of(lax.rem(j, 4) * B, B), B)]


def gather_step_kernel(
    cov,
    mean,
    noise,
    blocks,
    out,
    mean_out,
    mean_here,
    noise_here,
    blocks_here,
    relay,
    send,
    recv,
    relay_send,
    relay_recv,
    local,
    msend,
    mrecv,
    small,
):
    z, c = lax.axis_index("state"), lax.axis_index("tm_2")
    greet(column_peers(z, c))
    other = remote(mean, mean_out, msend, mrecv, {"tm_2": 1 - c})
    other.start()
    here = [
        pltpu.make_async_copy(src, dst, small.at[n])
        for n, (src, dst) in enumerate(((mean, mean_here), (noise, noise_here), (blocks, blocks_here)))
    ]
    for copy_here in here:
        copy_here.start()

    def start(src, dst, row, ssem, rsem, peer):
        for t in range(3):
            remote(lanes_of_block(src, row + t), lanes_of_block(dst, row + t), ssem, rsem, peer).start()

    def whole(ref, ssem, rsem):
        part = ref.at[:, 0 : 3 * B]
        return remote(part, part, ssem, rsem, {"state": 0, "tm_2": 0})

    def target(i):
        dz, e = 2 * c + i // 2, i % 2
        mine = (z == dz) & (c == e)
        far = lax.rem(dz + 4 - z, 4) == 2
        return dz, e, mine, far

    for i in range(4):
        dz, e, mine, far = target(i)

        @pl.when(far)
        def _():
            for t in range(3):
                remote(
                    lanes_of_block(cov.at[i], z + t),
                    lanes_of_block(relay.at[e], z + t),
                    send.at[i],
                    relay_recv.at[e, t],
                    {"state": lax.rem(z + (3 if e else 1), 4)},
                ).start()

    for i in range(4):
        dz, e, mine, far = target(i)

        @pl.when(mine)
        def _():
            pltpu.make_async_copy(cov.at[i], out.at[z], local).start()

        @pl.when(jnp.logical_not(mine | far))
        def _():
            start(cov.at[i], out.at[z], z, send.at[i], recv.at[z], {"state": dz, "tm_2": e})

    sources = [lax.rem(z + (1 if e else 3), 4) for e in range(2)]
    duties = [source // 2 != c for source in sources]
    for t in range(3):
        for e in range(2):

            @pl.when(duties[e])
            def _():
                here = lanes_of_block(relay.at[e], sources[e] + t)
                remote(here, here, send.at[0], relay_recv.at[e, t], {"state": 0, "tm_2": 0}).wait_recv()
                remote(
                    here,
                    lanes_of_block(out.at[sources[e]], sources[e] + t),
                    relay_send.at[e],
                    recv.at[sources[e]],
                    {"state": lax.rem(z + (3 if e else 1), 4), "tm_2": e},
                ).start()

    for i in range(4):
        dz, e, mine, far = target(i)

        @pl.when(mine)
        def _():
            pltpu.make_async_copy(cov.at[i], out.at[z], local).wait()

        @pl.when(jnp.logical_not(mine))
        def _():
            whole(cov.at[i], send.at[i], recv.at[0]).wait_send()

    for e in range(2):

        @pl.when(duties[e])
        def _():
            whole(relay.at[e], relay_send.at[e], recv.at[0]).wait_send()

    source_core = z // 2
    for s in range(4):

        @pl.when(jnp.logical_not((z == s) & (c == source_core)))
        def _():
            whole(out.at[s], send.at[0], recv.at[s]).wait_recv()

    other.wait()
    for copy_here in here:
        copy_here.wait()


def final_kernel(
    row,
    rows,
    across,
    down,
    pair,
    own,
    out,
    mean_out,
    cov,
    mean,
    add,
    relay,
    sl,
    sg,
    rh,
    rl,
    eh,
    el,
    lk,
    send,
    recv,
    relay_send,
    relay_recv,
    local,
    msend,
    mrecv,
):
    z, c, me = lax.axis_index("state"), lax.axis_index("tm_2"), lax.axis_index("tm_0")
    barrier = pltpu.get_barrier_semaphore()
    peers = column_peers(z, c)
    for peer in peers:
        pl.semaphore_signal(barrier, inc=1, device_id=peer, device_id_type=MESH)
    load = chosen(me, row, from_slots(rows))

    @pl.when(me == 3)
    def _():
        cov[...] = jnp.zeros((N, N), F32)
        mean[...] = jnp.zeros((8, N), F32)

    @pl.when(me == 2)
    def _():
        unpack_spread(lambda r, n, c: load(3, r, n, c, B), cov)
        mean[...] = load(3, GROW, 8)

    @pl.when(me < 2)
    def _():
        unpack_spread(lambda r, n, c: load(3, r, n, c, B), sl)
        sg[...] = load(3, GROW, 8)

    def take(get):
        split_into(eh, el, lambda r: get(r.start, B))
        unpack_spread(lambda r, n, c: get(r, n, c, B), lk)
        add[...] = get(GROW, 8)

    def push(state, offset):
        split_into(rh, rl, lambda r: state[r, :])
        e = (eh[...], el[...])
        offset[...] = dot_s(split(offset[...]), e, 1) + add[...]
        state[...] = dot_s(split(dot_s(e, (rh[...], rl[...]))), e, 1) + lk[...]

    choices = (
        lambda r, n, c=0, m=N: load(2, r, n, c, m),
        lambda r, n, c=0, m=N: load(1, r, n, c, m),
        lambda r, n, c=0, m=N: across[r : r + n, c : c + m],
        lambda r, n, c=0, m=N: down[r : r + n, c : c + m],
        lambda r, n, c=0, m=N: jnp.where(
            lax.axis_index("tm_2") == 0, pair[r : r + n, c : c + m], own[r : r + n, c : c + m]
        ),
    )

    def early(t, _):
        @pl.when(me < 2 - t)
        def _():
            for k in range(2):
                pl.when(t == k)(partial(take, choices[k]))
            push(sl, sg)

        @pl.when(me == 1 - t)
        def _():
            cov[...] = sl[...]
            mean[...] = sg[...]

        return 0

    lax.fori_loop(0, 2, early, 0)

    def late(t, _):
        for k in range(3):
            pl.when(t == k)(partial(take, choices[2 + k]))
        push(cov, mean)
        return 0

    lax.fori_loop(0, 3, late, 0)
    pl.semaphore_wait(barrier, len(peers))

    core = z // 2
    slot = 2 * lax.rem(z, 2) + c
    opposite = lax.rem(z + 2, 4)
    onward = lax.rem(z + 1 + 2 * c, 4)

    def slab(t):
        return cov.at[pl.ds(pl.multiple_of(t * B, B), B), :]

    parts = [pl.ds(B // 4 * p, B // 4) for p in range(4)]
    far = remote(slab(opposite), relay, relay_send.at[0], relay_recv.at[0], {"state": onward})
    for p, part in enumerate(parts):
        remote(
            cov.at[pl.ds(pl.multiple_of(opposite * B + B // 4 * p, 8), B // 4), :],
            relay.at[part],
            relay_send.at[0],
            relay_recv.at[p],
            {"state": onward},
        ).start()

    def copy(t):
        return remote(slab(t), out.at[slot], send.at[t], recv.at[slot], {"state": t, "tm_2": core})

    def mean_copy(t):
        return remote(mean, mean_out.at[slot], msend.at[t], mrecv.at[slot], {"state": t, "tm_2": core})

    def mine(t):
        return (z == t) & (c == core)

    def copies(t):
        return pltpu.make_async_copy(slab(t), out.at[slot], local.at[0]), pltpu.make_async_copy(
            mean, mean_out.at[slot], local.at[1]
        )

    for t in range(4):

        @pl.when(mine(t))
        def _():
            for copy_here in copies(t):
                copy_here.start()

        @pl.when(jnp.logical_not(mine(t)))
        def _():
            mean_copy(t).start()

        @pl.when(jnp.logical_not(mine(t)) & (t != opposite))
        def _():
            copy(t).start()

    source = lax.rem(z + 3 + 2 * c, 4)
    there = out.at[2 * lax.rem(source, 2) + c]

    def onto(part):
        return remote(
            relay.at[part],
            there.at[part],
            relay_send.at[1],
            recv.at[2 * lax.rem(source, 2) + c],
            {"state": onward, "tm_2": source // 2},
        )

    for p, part in enumerate(parts):
        here = relay.at[part]
        remote(here, here, relay_send.at[0], relay_recv.at[p], {"state": onward}).wait_recv()
        onto(part).start()
    for t in range(4):

        @pl.when(mine(t))
        def _():
            for copy_here in copies(t):
                copy_here.wait()

        @pl.when(jnp.logical_not(mine(t)))
        def _():
            mean_copy(t).wait_send()

        @pl.when(jnp.logical_not(mine(t)) & (t != opposite))
        def _():
            copy(t).wait_send()

    far.wait_send()
    onto(pl.ds(0, B)).wait_send()
    for i in range(4):

        @pl.when(jnp.logical_not((z == 2 * c + i // 2) & (c == i % 2)))
        def _():
            remote(slab(0), out.at[i], send.at[0], recv.at[i], {"state": 0, "tm_2": 0}).wait_recv()
            remote(mean, mean_out.at[i], msend.at[0], mrecv.at[i], {"state": 0, "tm_2": 0}).wait_recv()


class Copies:
    def __init__(self, out, send, recv):
        self.out, self.send, self.recv, self.used, self.sent = out, send, recv, 0, []

    def put(self, peer, slot, row, rows, src=None):
        n, self.used = self.used, self.used + 1
        place = self.out.at[slot, pl.ds(pl.multiple_of(row, 8), rows), :]
        copy = remote(place if src is None else src, place, self.send.at[n], self.recv.at[n], peer)
        copy.start()
        self.sent.append(copy)
        return n

    def arrived(self, n, slot, row, rows):
        place = self.out.at[slot, pl.ds(pl.multiple_of(row, 8), rows), :]
        remote(place, place, self.send.at[n], self.recv.at[n], {"tm_2": 0}).wait_recv()

    def finish(self):
        for copy in self.sent:
            copy.wait_send()


Z_PIECES = (((0, 64), (64, 64), (128, 64), (192, 64)), ((0, 48), (48, 40), (88, 40), (128, 40)))
Z_HALF = (256, 168)


def pair_kernel(cov, left, pred, vectors, own, total, out, twin_buf, *refs):
    scratch, work, (swap_send, swap_recv, send, recv) = refs[:3], refs[3:11], refs[11:]
    z, c = lax.axis_index("state"), lax.axis_index("tm_2")
    zu, zd, zo = lax.rem(z + 1, 4), lax.rem(z + 3, 4), lax.rem(z + 2, 4)
    up, down, twin = {"state": zu}, {"state": zd}, {"tm_2": 1 - c}
    barrier = pltpu.get_barrier_semaphore()
    for peer in (up, down, twin):
        pl.semaphore_signal(barrier, inc=1, device_id=peer, device_id_type=MESH)
    swaps = [
        remote(own.at[rows], twin_buf.at[rows], swap_send.at[part], swap_recv.at[part], twin)
        for part, rows in ((0, pl.ds(0, N)), (1, pl.ds(N, ROWS - N)))
    ]

    def gain_ready():
        pl.semaphore_wait(barrier, 3)
        swaps[0].start()

    element(cov, left, pred, vectors, own, *scratch, gain_ready)
    swaps[1].start()
    cp = Copies(out, send, recv)
    ups, downs, tails, twins = [], [], [], []

    def rows_of(part, core, piece):
        return (N if part else 0) + core * Z_HALF[part] + piece[0], piece[1]

    def first_hop(part):
        pieces = Z_PIECES[part]
        for j, (a, b) in enumerate(zip(pieces, pieces[::-1])):
            for into, peer, piece in ((ups, up, a), (downs, down, b)):
                row, rows = rows_of(part, c, piece)
                n = cp.put(peer, z, row, rows, total.at[pl.ds(pl.multiple_of(row, 8), rows), :])
                into.append((n, part, piece, j < len(pieces) // 2))

    load = chosen(c, own, lambda k, row, rows, lane, lanes: twin_buf[row : row + rows, lane : lane + lanes])
    swaps[0].wait()
    gains(2, c, load, total, None, work)
    first_hop(0)
    swaps[1].wait()
    spreads(2, c, load, total, None, work)
    first_hop(1)

    def hand(slot, part, piece):
        row, rows = rows_of(part, c, piece)
        twins.append((cp.put(twin, slot, row, rows), slot, rows_of(part, 1 - c, piece)))

    for pair in zip(ups, downs):
        for (n, part, piece, further), slot, peer in zip(pair, (zd, zu), (up, down)):
            row, rows = rows_of(part, c, piece)
            cp.arrived(n, slot, row, rows)
            if further:
                tails.append((cp.put(peer, slot, row, rows), part, piece))
            hand(slot, part, piece)
    for n, part, piece in tails:
        row, rows = rows_of(part, c, piece)
        cp.arrived(n, zo, row, rows)
        hand(zo, part, piece)
    for n, slot, (row, rows) in twins:
        cp.arrived(n, slot, row, rows)
    cp.finish()


QUARTER = (128, 88)
PIECES = (((0, 32), (32, 32), (64, 32), (96, 32)), ((0, 24), (24, 24), (48, 24), (72, 16)))


def ring_kernel(mine, axis, coarse, own, others, rest, out, total, *refs):
    z, c, a = lax.axis_index("state"), lax.axis_index("tm_2"), lax.axis_index(axis)
    work, (send, recv, twin_send, twin_recv) = refs[:8], refs[8:]
    me = lax.axis_index(mine)
    zu, zd, zo = lax.rem(z + 1, 4), lax.rem(z + 3, 4), lax.rem(z + 2, 4)
    au, ad, ao = lax.rem(a + 1, 4), lax.rem(a + 3, 4), lax.rem(a + 2, 4)
    up, down = {axis: au}, {axis: ad}
    above, below, twin = {"state": zu}, {"state": zd}, {"tm_2": 1 - c}
    peers = [up, down, above, below, twin]
    barrier = pltpu.get_barrier_semaphore()
    for peer in peers:
        pl.semaphore_signal(barrier, inc=1, device_id=peer, device_id_type=MESH)
    quarters = (z, zu)
    coming = (zd, zo)
    load = chosen(me, own, from_slots(others))

    def run(part):
        base, pieces = N if part else 0, PIECES[part]
        span = pl.ds(base, 4 * QUARTER[part])
        if part:
            split_gains(4, load, work)
            spreads(4, me, load, total, rest, work)
        else:
            gains(4, me, load, total, rest, work)
        pl.semaphore_wait(barrier, len(peers))
        cp = Copies(out, send, recv)

        def hand(src, dst, sem):
            copy = remote(src, dst, twin_send.at[sem], twin_recv.at[sem], twin)
            copy.start()

        def row_of(quarter, j):
            return pl.multiple_of(base + quarter * QUARTER[part] + pieces[j][0], 8)

        count = len(pieces)
        ups, downs, zs, tails = [], [], [], []
        for j in range(count):
            for k in (0, 1):
                for into, peer, jj in ((ups, up, j), (downs, down, count - 1 - j)):
                    row = row_of(quarters[k], jj)
                    n = cp.put(peer, a, row, pieces[jj][1], total.at[pl.ds(row, pieces[jj][1]), :])
                    into.append((n, k, jj, j < count // 2))
        hand(total.at[span], total.at[span], 0)
        hand(rest.at[span], rest.at[span], 1)

        came_in = {}

        def pass_on(slot, quarter, j, key):
            came_in.setdefault(key, []).append(j)
            if len(came_in[key]) * coarse == count:
                row, rows = row_of(quarter, 0), QUARTER[part]
            elif not coarse:
                row, rows = row_of(quarter, j), pieces[j][1]
            else:
                return
            place = out.at[slot, pl.ds(row, rows), :]
            hand(place, place, 2)

        def spread(slot, k, j, name):
            row = row_of(quarters[k], j)
            zs.append((cp.put(below if k else above, slot, row, pieces[j][1]), slot, k, j, name))
            pass_on(slot, quarters[k], j, (name, k))

        def take(keep):
            while len(zs) > keep:
                n, slot, k, j, name = zs.pop(0)
                row = row_of(coming[k], j)
                cp.arrived(n, slot, row, pieces[j][1])
                pass_on(slot, coming[k], j, (name, k + 2))

        for pair in zip(ups, downs):
            for (n, k, j, further), slot, peer, name in zip(pair, (ad, au), (up, down), ("below", "above")):
                row = row_of(quarters[k], j)
                cp.arrived(n, slot, row, pieces[j][1])
                if further:
                    tails.append((cp.put(peer, slot, row, pieces[j][1]), k, j))
                spread(slot, k, j, name)
        for n, k, j in tails:
            cp.arrived(n, ao, row_of(quarters[k], j), pieces[j][1])
            spread(ao, k, j, "opposite")
            take(len(zs) - 2)
        take(0)
        cp.finish()
        other = pl.ds(0 if part else N, 4 * QUARTER[1 - part])
        for sem, ref in enumerate((total, rest)):
            remote(ref.at[span], ref.at[span], twin_send.at[sem], twin_recv.at[sem], twin).wait_send()
            remote(ref.at[other], ref.at[other], twin_send.at[sem], twin_recv.at[sem], twin).wait_recv()
        sent, came = out.at[0:3, span], out.at[0:3, other]
        remote(sent, sent, twin_send.at[2], twin_recv.at[2], twin).wait_send()
        remote(came, came, twin_send.at[2], twin_recv.at[2], twin).wait_recv()

    for part in (0, 1):
        pl.when(c == part)(partial(run, part))


def shape(*dims, dtype=F32):
    return jax.ShapeDtypeStruct(dims, dtype)


def params(limit=None, **more):
    return pltpu.CompilerParams(vmem_limit_bytes=limit, **more)


DMA = pltpu.SemaphoreType.DMA


def comm(kernel, name, collective_id, outs, scratch, *args, limit, in_spec=ANY, out_spec=ANY):
    return pl.pallas_call(
        kernel,
        name=name,
        out_shape=outs,
        in_specs=[in_spec] * len(args),
        out_specs=jax.tree.map(lambda _: out_spec, outs),
        scratch_shapes=scratch,
        compiler_params=pltpu.CompilerParams(
            collective_id=collective_id, has_side_effects=True, vmem_limit_bytes=limit
        ),
    )(*args)


def suffix_work(count):
    return [
        pltpu.VMEM((2, N, N), F32),
        pltpu.VMEM((2, N, N), F32),
        pltpu.VMEM((2, 8, N), F32),
        pltpu.VMEM((N, N), BF16),
        pltpu.VMEM((N, N), BF16),
        pltpu.VMEM((count - 1, N, N), BF16),
        pltpu.VMEM((count - 1, N, N), BF16),
        pltpu.VMEM((N, N), F32),
    ]


def ring(name, collective_id, mine, axis, own, others, coarse=1):
    packet = shape(ROWS, N)
    return pl.pallas_call(
        partial(ring_kernel, mine, axis, coarse),
        name=name,
        out_shape=(packet, shape(4, ROWS, N), packet),
        in_specs=[VM, VM],
        out_specs=(VM, VM, VM),
        scratch_shapes=suffix_work(4) + [DMA((48,)), DMA((48,)), DMA((3,)), DMA((3,))],
        compiler_params=params(RING_LIMIT, collective_id=collective_id, has_side_effects=True),
    )(own, others)


RING_LIMIT = 24 * 1024 * 1024
FIRST_LIMIT = 4 * 1024 * 1024


def on_device(filtered_cov, filtered_mean, noise_var, trans_blocks, pattern):
    z = lax.axis_index("state")
    cov, twin_mean, mean_here, noise_here, blocks_here = comm(
        gather_step_kernel,
        "gather_step",
        0,
        (shape(4, B, N), shape(4, N), shape(4, N), shape(1, N), shape(4, 2, B, B)),
        [pltpu.VMEM((2, B, N), F32), DMA((4,)), DMA((4,)), DMA((2,)), DMA((2, 3)), DMA, DMA, DMA, DMA((3,))],
        filtered_cov,
        filtered_mean,
        noise_var.reshape(1, N),
        trans_blocks,
        limit=FIRST_LIMIT,
        out_spec=VM,
    )
    packet, packets = shape(ROWS, N), shape(4, ROWS, N)
    square = shape(N, N)
    predicted = pl.pallas_call(
        predict_kernel,
        name="predict",
        out_shape=(square, square, square, shape(16, N)),
        in_specs=[SM] + [VM] * 5,
        out_specs=(VM, VM, VM, VM),
        compiler_params=params(RING_LIMIT),
    )(pattern, cov, mean_here, twin_mean, noise_here, blocks_here)
    own, pair, pairs = pl.pallas_call(
        pair_kernel,
        name="pair",
        out_shape=(packet, packet, packets),
        in_specs=[VM] * 4,
        out_specs=(VM, VM, VM),
        scratch_shapes=[pltpu.VMEM((ROWS, N), F32)]
        + [pltpu.VMEM((N, N), F32)] * 2
        + [pltpu.VMEM((B, B), F32)]
        + suffix_work(2)
        + [DMA((2,)), DMA((2,)), DMA((48,)), DMA((48,))],
        compiler_params=params(RING_LIMIT, collective_id=2, has_side_effects=True),
    )(*predicted)
    down, columns, column = ring("ring_x", 3, "state", "tm_1", pair, pairs)
    across, rows, row = ring("ring_y", 4, "tm_1", "tm_0", column, columns)
    half = pltpu.VMEM((N, N), BF16)
    smooth_cov, means = pl.pallas_call(
        final_kernel,
        name="final",
        out_shape=(shape(4, B, N), shape(4, 8, N)),
        in_specs=[VM] * 6,
        out_specs=(VM, VM),
        scratch_shapes=[pltpu.VMEM((N, N), F32), pltpu.VMEM((8, N), F32), pltpu.VMEM((8, N), F32), pltpu.VMEM((B, N), F32)]
        + [pltpu.VMEM((N, N), F32), pltpu.VMEM((8, N), F32), half, half, half, half, pltpu.VMEM((N, N), F32)]
        + [DMA((4,)), DMA((4,)), DMA((2,)), DMA((4,)), DMA((2,)), DMA((4,)), DMA((4,))],
        compiler_params=params(RING_LIMIT, collective_id=5, has_side_effects=True),
    )(row, rows, across, down, pair, own)
    return lax.dynamic_slice_in_dim(means[:, 0, :], z * B, B, 1), smooth_cov


def solution(mesh):
    torus = Mesh(
        mesh.devices.reshape(4, 4, 2, mesh.shape["state"]), ("tm_0", "tm_1", "tm_2", "state")
    )
    return jax.shard_map(
        on_device,
        mesh=torus,
        in_specs=(P(TM, "state", None), P(TM, None), P(), P(), P()),
        out_specs=(P(TM, "state"), P(TM, "state", None)),
        check_vma=False,
    )
```

```python
from functools import partial

import jax
import jax.numpy as jnp
from jax import lax
from jax.experimental import pallas as pl
from jax.experimental.pallas import tpu as pltpu
from jax.sharding import Mesh
from jax.sharding import PartitionSpec as P

N = 512
B = 128
LROW = 512
GROW = 832
ROWS = 896
MESH = pl.DeviceIdType.MESH
F32 = jnp.float32
BF16 = jnp.bfloat16
ANY = pl.BlockSpec(memory_space=pl.ANY)
VM = pl.BlockSpec(memory_space=pltpu.VMEM)
SM = pl.BlockSpec(memory_space=pltpu.SMEM)
TM = ("tm_0", "tm_1", "tm_2")


def split(x):
    high = x.astype(BF16)
    return high, (x - high.astype(F32)).astype(BF16)


def dg(a, b, cb=0):
    return lax.dot_general(a, b, (((1,), (cb,)), ((), ())), preferred_element_type=F32)


def dot_s(a, b, cb=0):
    return dg(a[0], b[0], cb) + (dg(a[0], b[1], cb) + dg(a[1], b[0], cb))


def dot3(a, b, cb=0):
    return dot_s(split(a), split(b), cb)


def dot6(a, b, cb=0, ca=1):
    return lax.dot_general(
        a, b, (((ca,), (cb,)), ((), ())), precision=lax.Precision.HIGHEST, preferred_element_type=F32
    )


def packed_blocks():
    out = []
    for j in range(4):
        out.append((0, j, LROW, j, 128, 0))
    for lane, (i, j) in enumerate(((1, 1), (1, 2), (1, 3), (2, 2))):
        out.append((i, j, LROW + 128, lane, 128, 0))
    for lane, (i, j, r) in enumerate(((2, 3, 0), (2, 3, 64), (3, 3, 0), (3, 3, 64))):
        out.append((i, j, LROW + 256, lane, 64, r))
    return out


def pack_spread(ref, full):
    for i, j, row, lane, rows, r0 in packed_blocks():
        ref[row : row + rows, lane * B : lane * B + B] = full(i * B + r0, rows, j * B)


def unpack_spread(load, full_ref):
    for i, j, row, lane, rows, r0 in packed_blocks():
        block = load(row, rows, lane * B)
        full_ref[i * B + r0 : i * B + r0 + rows, j * B : j * B + B] = block
    for i in range(4):
        for j in range(i + 1, 4):
            block = full_ref[i * B : i * B + B, j * B : j * B + B]
            full_ref[j * B : j * B + B, i * B : i * B + B] = jnp.transpose(block)


def tree_sum(terms):
    while len(terms) > 1:
        terms = [sum(terms[i + 1 : i + 2], terms[i]) for i in range(0, len(terms), 2)]
    return terms[0]


def small_mul(a, b):
    return [
        [tree_sum([a[i][t] * b[t][j] for t in range(len(b))]) for j in range(len(b[0]))] for i in range(len(a))
    ]


def small_inverse(m):
    n = len(m)
    if n == 2:
        a, b, d = m[0][0], m[0][1], m[1][1]
        inv = 1.0 / (a * d - b * b)
        return [[d * inv, -b * inv], [-b * inv, a * inv]]
    h = n // 2
    upper = [row[h:] for row in m[:h]]
    lower = [[upper[j][i] for j in range(h)] for i in range(h)]
    first = small_inverse([row[:h] for row in m[:h]])
    q = small_mul(lower, first)
    qb = small_mul(q, upper)
    schur = [[m[h + min(i, j)][h + max(i, j)] - qb[min(i, j)][max(i, j)] for j in range(h)] for i in range(h)]
    second = small_inverse(schur)
    sq = small_mul(second, q)
    qsq = small_mul([[q[j][i] for j in range(h)] for i in range(h)], sq)
    out = [[None] * n for _ in range(n)]
    for i in range(h):
        for j in range(h):
            out[i][j] = first[i][j] + qsq[i][j]
            out[h + i][h + j] = second[i][j]
            out[h + i][j] = out[j][h + i] = -sq[i][j]
    return out


PANEL = 64


def inverse128(block):
    groups = PANEL // 8
    row_id = lax.broadcasted_iota(jnp.int32, (8, B), 0)
    lane_id = lax.broadcasted_iota(jnp.int32, (8, B), 1)
    lanes = lax.broadcasted_iota(jnp.int32, (B, B), 1)

    def body(_, x):
        top = x[:PANEL, :]
        vs = [x[8 * k : 8 * k + 8, :] for k in range(groups)]
        for q in range(groups):
            at = 8 * q
            cols = [[jnp.broadcast_to(v[:, at + s : at + s + 1], (8, B)) for v in vs] for s in range(8)]
            rows = [jnp.broadcast_to(vs[q][s : s + 1, :], (8, B)) for s in range(8)]
            m = [[None] * 8 for _ in range(8)]
            for s in range(8):
                for t in range(s, 8):
                    m[s][t] = m[t][s] = jnp.broadcast_to(cols[s][q][t : t + 1, :], (8, B))
            inv = small_inverse(m)
            new_rows = [n[0] for n in small_mul(inv, [[r] for r in rows])]
            for s in range(8):
                for t in range(8):
                    new_rows[s] = jnp.where(lane_id == at + t, -inv[s][t], new_rows[s])
            inside = (lane_id >= at) & (lane_id < at + 8)
            for k in range(groups):
                if k == q:
                    new = new_rows[0]
                    for s in range(1, 8):
                        new = jnp.where(row_id == s, new_rows[s], new)
                else:
                    new = jnp.where(inside, 0.0, vs[k])
                    new -= tree_sum([cols[s][k] * new_rows[s] for s in range(8)])
                vs[k] = new
        done = jnp.concatenate(vs, axis=0)
        rest = jnp.where(lanes < PANEL, 0.0, x) - dot6(top, done, 0, 0)
        return pltpu.roll(jnp.concatenate([rest[PANEL:, :], done], axis=0), B - PANEL, 1)

    return -lax.fori_loop(0, B // PANEL, body, block)


def predict_kernel(pattern, cov_in, mean_a, mean_b, noise, blocks, cov, left, pred, vectors):
    c, z = lax.axis_index("tm_2"), lax.axis_index("state")
    for i in range(4):
        for t in range(3):
            lanes = slice((i + t) % 4 * B, (i + t) % 4 * B + B)
            cov[i * B : i * B + B, lanes] = cov_in[i, :, lanes]
        j = (i + 3) % 4
        cov[i * B : i * B + B, j * B : j * B + B] = jnp.transpose(cov_in[j, :, i * B : i * B + B])
    both = [jnp.concatenate([blocks[r, 0], blocks[r, 1]], axis=1) for r in range(4)]

    def rows_of(ref, r):
        return jnp.concatenate(
            [ref[pl.ds(pl.multiple_of(pattern[r, j] * B, B), B), :] for j in range(2)], axis=0
        )

    def lanes_of(ref, rows, r):
        return jnp.concatenate(
            [ref[0:rows, pl.ds(pl.multiple_of(pattern[r, j] * B, B), B)] for j in range(2)], axis=1
        )

    place = lax.rem(2 * z + c, 4)
    mean = jnp.where(z // 2 == c, mean_a[pl.ds(place, 1), :], mean_b[pl.ds(place, 1), :])
    vectors[0:8, :] = jnp.broadcast_to(mean, (8, N))
    pushed = []
    for r in range(4):
        left[r * B : r * B + B, :] = dot6(both[r], rows_of(cov, r))
        pushed.append(dot6(lanes_of(vectors, 8, r), both[r], 1))
    vectors[8:16, :] = jnp.concatenate(pushed, axis=1)
    eye = lax.broadcasted_iota(jnp.int32, (B, B), 0) == lax.broadcasted_iota(jnp.int32, (B, B), 1)
    for r in range(4):
        rows = (r + 1) * B
        value = dot6(lanes_of(left, rows, r), both[r], 1)
        pred[0:rows, r * B : r * B + B] = value
        q = jnp.where(eye, jnp.broadcast_to(noise[0:1, r * B : r * B + B], (B, B)), 0.0)
        pred[r * B : rows, r * B : r * B + B] += q


def element(cov, left, pred_in, vectors, out, pred, sol, inv_ref, gain_ready):
    y, x, c, z = (lax.axis_index(a) for a in ("tm_0", "tm_1", "tm_2", "state"))
    pred[...] = pred_in[...]
    sol[...] = left[...]

    def eliminate(k, _):
        at = pl.ds(pl.multiple_of(k * B, B), B)
        inv_ref[...] = inverse128(pred[at, at])
        for kk in range(4):

            @pl.when(k == kk)
            def _():
                k0, k1 = kk * B, kk * B + B
                inv = inv_ref[...]
                ub = dot6(inv, sol[k0:k1, :])
                sol[k0:k1, :] = ub
                if kk < 3:
                    tail = pred[k0:k1, k1:]
                    ut = dot6(inv, tail)
                    st = jnp.transpose(tail)
                    pred[k1:, k1:] -= dot6(st, ut)
                    sol[k1:, :] -= dot6(st, ub)
                    pred[k0:k1, k1:] = ut

        return 0

    lax.fori_loop(0, 4, eliminate, 0)
    for k in (2, 1, 0):
        k0, k1 = k * B, k * B + B
        sol[k0:k1, :] -= dot6(pred[k0:k1, k1:], sol[k1:, :])
    keep = (8 * (4 * y + x) + 2 * z + c != 127).astype(F32)
    for i in range(4):
        for j in range(4):
            out[i * B : i * B + B, j * B : j * B + B] = (
                jnp.transpose(sol[j * B : j * B + B, i * B : i * B + B]) * keep
            )
    gain_ready()
    out[GROW : GROW + 8, :] = vectors[0:8, :] - keep * dot6(vectors[8:16, :], sol[...])
    out[GROW + 8 :, :] = jnp.zeros((ROWS - GROW - 8, N), F32)
    pred[...] = cov[...] - dot6(out[0:N, :], left[...])
    pack_spread(out, lambda r, n, c: pred[r : r + n, c : c + B])


def split_into(high, low, value):
    for r in range(4):
        rows = slice(r * B, r * B + B)
        high[rows, :], low[rows, :] = split(value(rows))


def chosen(me, own, other):
    def load(k, row, rows, lane=0, lanes=N):
        return jnp.where(k == me, own[row : row + rows, lane : lane + lanes], other(k, row, rows, lane, lanes))

    return load


def split_gains(count, load, work):
    eh, el = work[5:7]

    def body(k, _):
        split_into(eh.at[k], el.at[k], lambda rows: load(k, rows.start, B))
        return 0

    lax.fori_loop(0, count - 1, body, 0)


def gains(count, me, load, total, rest, work):
    se, _, _, rh, rl, eh, el, _ = work
    last = count - 1
    if rest is not None:

        @pl.when(me == last)
        def _():
            same = lax.broadcasted_iota(jnp.int32, (N, N), 0) == lax.broadcasted_iota(jnp.int32, (N, N), 1)
            rest[0:N, :] = same.astype(F32)

    def step(t, _):
        k = last - 1 - t
        now = lax.rem(t, 2)
        if rest is not None:

            @pl.when(k == me)
            def _():
                rest[0:N, :] = se[now]

        split_into(eh.at[k], el.at[k], lambda rows: load(k, rows.start, B))
        split_into(rh, rl, lambda rows: se[now, rows, :])
        se[1 - now] = dot_s((eh[k], el[k]), (rh[...], rl[...]))
        return 0

    se[0] = load(last, 0, N)
    lax.fori_loop(0, last, step, 0)
    total[0:N, :] = se[last % 2]


def spreads(count, me, load, total, rest, work):
    _, sl, sg, rh, rl, eh, el, lk = work
    last = count - 1
    if rest is not None:

        @pl.when(me == last)
        def _():
            rest[N:, :] = jnp.zeros((ROWS - N, N), F32)

    unpack_spread(lambda r, n, c: load(last, r, n, c, B), sl.at[0])
    sg[0] = load(last, GROW, 8)

    def keep(ref, slot):
        pack_spread(ref, lambda r, n, c: sl[slot, r : r + n, c : c + B])
        ref[GROW : GROW + 8, :] = sg[slot]
        ref[GROW + 8 :, :] = jnp.zeros((ROWS - GROW - 8, N), F32)

    def step(t, _):
        k = last - 1 - t
        now = lax.rem(t, 2)
        if rest is not None:

            @pl.when(k == me)
            def _():
                keep(rest, now)

        split_into(rh, rl, lambda rows: sl[now, rows, :])
        unpack_spread(lambda r, n, c: load(k, r, n, c, B), lk)
        e = (eh[k], el[k])
        sg[1 - now] = dot_s(split(sg[now]), e, 1) + load(k, GROW, 8)
        half = split(dot_s(e, (rh[...], rl[...])))
        sl[1 - now] = dot_s(half, e, 1) + lk[...]
        return 0

    lax.fori_loop(0, last, step, 0)
    if total is not None:
        keep(total, last % 2)


def from_slots(others):
    return lambda k, row, rows, lane, lanes: others[k, row : row + rows, lane : lane + lanes]


def greet(peers):
    barrier = pltpu.get_barrier_semaphore()
    for peer in peers:
        pl.semaphore_signal(barrier, inc=1, device_id=peer, device_id_type=MESH)
    pl.semaphore_wait(barrier, len(peers))


def column_peers(z, c):
    return [
        {"state": lax.rem(z + dz, 4), "tm_2": c if dc == 0 else 1 - c}
        for dz in range(4)
        for dc in range(2)
        if dz or dc
    ]


def remote(src, dst, send, recv, peer):
    return pltpu.make_async_remote_copy(
        src_ref=src, dst_ref=dst, send_sem=send, recv_sem=recv, device_id=peer, device_id_type=MESH
    )


def lanes_of_block(ref, j):
    return ref.at[:, pl.ds(pl.multiple_of(lax.rem(j, 4) * B, B), B)]


def gather_step_kernel(
    cov,
    mean,
    noise,
    blocks,
    out,
    mean_out,
    mean_here,
    noise_here,
    blocks_here,
    relay,
    send,
    recv,
    relay_send,
    relay_recv,
    local,
    msend,
    mrecv,
    small,
):
    z, c = lax.axis_index("state"), lax.axis_index("tm_2")
    greet(column_peers(z, c))
    other = remote(mean, mean_out, msend, mrecv, {"tm_2": 1 - c})
    other.start()
    here = [
        pltpu.make_async_copy(src, dst, small.at[n])
        for n, (src, dst) in enumerate(((mean, mean_here), (noise, noise_here), (blocks, blocks_here)))
    ]
    for copy_here in here:
        copy_here.start()

    def start(src, dst, row, ssem, rsem, peer):
        for t in range(3):
            remote(lanes_of_block(src, row + t), lanes_of_block(dst, row + t), ssem, rsem, peer).start()

    def whole(ref, ssem, rsem):
        part = ref.at[:, 0 : 3 * B]
        return remote(part, part, ssem, rsem, {"state": 0, "tm_2": 0})

    def target(i):
        dz, e = 2 * c + i // 2, i % 2
        mine = (z == dz) & (c == e)
        far = lax.rem(dz + 4 - z, 4) == 2
        return dz, e, mine, far

    for i in range(4):
        dz, e, mine, far = target(i)

        @pl.when(far)
        def _():
            start(cov.at[i], relay.at[e], z, send.at[i], relay_recv.at[e], {"state": lax.rem(z + (3 if e else 1), 4)})

    for i in range(4):
        dz, e, mine, far = target(i)

        @pl.when(mine)
        def _():
            pltpu.make_async_copy(cov.at[i], out.at[z], local).start()

        @pl.when(jnp.logical_not(mine | far))
        def _():
            start(cov.at[i], out.at[z], z, send.at[i], recv.at[z], {"state": dz, "tm_2": e})

    duties = []
    for e in range(2):
        source, dz = lax.rem(z + (1 if e else 3), 4), lax.rem(z + (3 if e else 1), 4)
        duty = source // 2 != c
        duties.append(duty)

        @pl.when(duty)
        def _():
            whole(relay.at[e], send.at[0], relay_recv.at[e]).wait_recv()
            start(relay.at[e], out.at[source], source, relay_send.at[e], recv.at[source], {"state": dz, "tm_2": e})

    for i in range(4):
        dz, e, mine, far = target(i)

        @pl.when(mine)
        def _():
            pltpu.make_async_copy(cov.at[i], out.at[z], local).wait()

        @pl.when(jnp.logical_not(mine))
        def _():
            whole(cov.at[i], send.at[i], recv.at[0]).wait_send()

    for e in range(2):

        @pl.when(duties[e])
        def _():
            whole(relay.at[e], relay_send.at[e], recv.at[0]).wait_send()

    source_core = z // 2
    for s in range(4):

        @pl.when(jnp.logical_not((z == s) & (c == source_core)))
        def _():
            whole(out.at[s], send.at[0], recv.at[s]).wait_recv()

    other.wait()
    for copy_here in here:
        copy_here.wait()


def final_kernel(
    row,
    rows,
    across,
    down,
    pair,
    own,
    out,
    mean_out,
    cov,
    mean,
    add,
    relay,
    sl,
    sg,
    rh,
    rl,
    eh,
    el,
    lk,
    send,
    recv,
    relay_send,
    relay_recv,
    local,
    msend,
    mrecv,
):
    z, c, me = lax.axis_index("state"), lax.axis_index("tm_2"), lax.axis_index("tm_0")
    barrier = pltpu.get_barrier_semaphore()
    peers = column_peers(z, c)
    for peer in peers:
        pl.semaphore_signal(barrier, inc=1, device_id=peer, device_id_type=MESH)
    load = chosen(me, row, from_slots(rows))

    @pl.when(me == 3)
    def _():
        cov[...] = jnp.zeros((N, N), F32)
        mean[...] = jnp.zeros((8, N), F32)

    @pl.when(me == 2)
    def _():
        unpack_spread(lambda r, n, c: load(3, r, n, c, B), cov)
        mean[...] = load(3, GROW, 8)

    @pl.when(me < 2)
    def _():
        unpack_spread(lambda r, n, c: load(3, r, n, c, B), sl)
        sg[...] = load(3, GROW, 8)

    def take(get):
        split_into(eh, el, lambda r: get(r.start, B))
        unpack_spread(lambda r, n, c: get(r, n, c, B), lk)
        add[...] = get(GROW, 8)

    def push(state, offset):
        split_into(rh, rl, lambda r: state[r, :])
        e = (eh[...], el[...])
        offset[...] = dot_s(split(offset[...]), e, 1) + add[...]
        state[...] = dot_s(split(dot_s(e, (rh[...], rl[...]))), e, 1) + lk[...]

    choices = (
        lambda r, n, c=0, m=N: load(2, r, n, c, m),
        lambda r, n, c=0, m=N: load(1, r, n, c, m),
        lambda r, n, c=0, m=N: across[r : r + n, c : c + m],
        lambda r, n, c=0, m=N: down[r : r + n, c : c + m],
        lambda r, n, c=0, m=N: jnp.where(
            lax.axis_index("tm_2") == 0, pair[r : r + n, c : c + m], own[r : r + n, c : c + m]
        ),
    )

    def early(t, _):
        @pl.when(me < 2 - t)
        def _():
            for k in range(2):
                pl.when(t == k)(partial(take, choices[k]))
            push(sl, sg)

        @pl.when(me == 1 - t)
        def _():
            cov[...] = sl[...]
            mean[...] = sg[...]

        return 0

    lax.fori_loop(0, 2, early, 0)

    def late(t, _):
        for k in range(3):
            pl.when(t == k)(partial(take, choices[2 + k]))
        push(cov, mean)
        return 0

    lax.fori_loop(0, 3, late, 0)
    pl.semaphore_wait(barrier, len(peers))

    core = z // 2
    slot = 2 * lax.rem(z, 2) + c
    opposite = lax.rem(z + 2, 4)
    onward = lax.rem(z + 1 + 2 * c, 4)

    def slab(t):
        return cov.at[pl.ds(pl.multiple_of(t * B, B), B), :]

    far = remote(slab(opposite), relay, relay_send.at[0], relay_recv, {"state": onward})
    far.start()

    def copy(t):
        return remote(slab(t), out.at[slot], send.at[t], recv.at[slot], {"state": t, "tm_2": core})

    def mean_copy(t):
        return remote(mean, mean_out.at[slot], msend.at[t], mrecv.at[slot], {"state": t, "tm_2": core})

    def mine(t):
        return (z == t) & (c == core)

    def copies(t):
        return pltpu.make_async_copy(slab(t), out.at[slot], local.at[0]), pltpu.make_async_copy(
            mean, mean_out.at[slot], local.at[1]
        )

    for t in range(4):

        @pl.when(mine(t))
        def _():
            for copy_here in copies(t):
                copy_here.start()

        @pl.when(jnp.logical_not(mine(t)))
        def _():
            mean_copy(t).start()

        @pl.when(jnp.logical_not(mine(t)) & (t != opposite))
        def _():
            copy(t).start()

    source = lax.rem(z + 3 + 2 * c, 4)
    far.wait_recv()
    on = remote(
        relay,
        out.at[2 * lax.rem(source, 2) + c],
        relay_send.at[1],
        recv.at[2 * lax.rem(source, 2) + c],
        {"state": onward, "tm_2": source // 2},
    )
    on.start()
    for t in range(4):

        @pl.when(mine(t))
        def _():
            for copy_here in copies(t):
                copy_here.wait()

        @pl.when(jnp.logical_not(mine(t)))
        def _():
            mean_copy(t).wait_send()

        @pl.when(jnp.logical_not(mine(t)) & (t != opposite))
        def _():
            copy(t).wait_send()

    far.wait_send()
    on.wait_send()
    for i in range(4):

        @pl.when(jnp.logical_not((z == 2 * c + i // 2) & (c == i % 2)))
        def _():
            remote(slab(0), out.at[i], send.at[0], recv.at[i], {"state": 0, "tm_2": 0}).wait_recv()
            remote(mean, mean_out.at[i], msend.at[0], mrecv.at[i], {"state": 0, "tm_2": 0}).wait_recv()


class Copies:
    def __init__(self, out, send, recv):
        self.out, self.send, self.recv, self.used, self.sent = out, send, recv, 0, []

    def put(self, peer, slot, row, rows, src=None):
        n, self.used = self.used, self.used + 1
        place = self.out.at[slot, pl.ds(pl.multiple_of(row, 8), rows), :]
        copy = remote(place if src is None else src, place, self.send.at[n], self.recv.at[n], peer)
        copy.start()
        self.sent.append(copy)
        return n

    def arrived(self, n, slot, row, rows):
        place = self.out.at[slot, pl.ds(pl.multiple_of(row, 8), rows), :]
        remote(place, place, self.send.at[n], self.recv.at[n], {"tm_2": 0}).wait_recv()

    def finish(self):
        for copy in self.sent:
            copy.wait_send()


Z_PIECES = (((0, 64), (64, 64), (128, 64), (192, 64)), ((0, 48), (48, 40), (88, 40), (128, 40)))
Z_HALF = (256, 168)


def pair_kernel(cov, left, pred, vectors, own, total, out, twin_buf, *refs):
    scratch, work, (swap_send, swap_recv, send, recv) = refs[:3], refs[3:11], refs[11:]
    z, c = lax.axis_index("state"), lax.axis_index("tm_2")
    zu, zd, zo = lax.rem(z + 1, 4), lax.rem(z + 3, 4), lax.rem(z + 2, 4)
    up, down, twin = {"state": zu}, {"state": zd}, {"tm_2": 1 - c}
    barrier = pltpu.get_barrier_semaphore()
    for peer in (up, down, twin):
        pl.semaphore_signal(barrier, inc=1, device_id=peer, device_id_type=MESH)
    swaps = [
        remote(own.at[rows], twin_buf.at[rows], swap_send.at[part], swap_recv.at[part], twin)
        for part, rows in ((0, pl.ds(0, N)), (1, pl.ds(N, ROWS - N)))
    ]

    def gain_ready():
        pl.semaphore_wait(barrier, 3)
        swaps[0].start()

    element(cov, left, pred, vectors, own, *scratch, gain_ready)
    swaps[1].start()
    cp = Copies(out, send, recv)
    ups, downs, tails, twins = [], [], [], []

    def rows_of(part, core, piece):
        return (N if part else 0) + core * Z_HALF[part] + piece[0], piece[1]

    def first_hop(part):
        pieces = Z_PIECES[part]
        for j, (a, b) in enumerate(zip(pieces, pieces[::-1])):
            for into, peer, piece in ((ups, up, a), (downs, down, b)):
                row, rows = rows_of(part, c, piece)
                n = cp.put(peer, z, row, rows, total.at[pl.ds(pl.multiple_of(row, 8), rows), :])
                into.append((n, part, piece, j < len(pieces) // 2))

    load = chosen(c, own, lambda k, row, rows, lane, lanes: twin_buf[row : row + rows, lane : lane + lanes])
    swaps[0].wait()
    gains(2, c, load, total, None, work)
    first_hop(0)
    swaps[1].wait()
    spreads(2, c, load, total, None, work)
    first_hop(1)

    def hand(slot, part, piece):
        row, rows = rows_of(part, c, piece)
        twins.append((cp.put(twin, slot, row, rows), slot, rows_of(part, 1 - c, piece)))

    for pair in zip(ups, downs):
        for (n, part, piece, further), slot, peer in zip(pair, (zd, zu), (up, down)):
            row, rows = rows_of(part, c, piece)
            cp.arrived(n, slot, row, rows)
            if further:
                tails.append((cp.put(peer, slot, row, rows), part, piece))
            hand(slot, part, piece)
    for n, part, piece in tails:
        row, rows = rows_of(part, c, piece)
        cp.arrived(n, zo, row, rows)
        hand(zo, part, piece)
    for n, slot, (row, rows) in twins:
        cp.arrived(n, slot, row, rows)
    cp.finish()


QUARTER = (128, 88)
PIECES = (((0, 32), (32, 32), (64, 32), (96, 32)), ((0, 24), (24, 24), (48, 24), (72, 16)))


def ring_kernel(mine, axis, own, others, rest, out, total, *refs):
    z, c, a = lax.axis_index("state"), lax.axis_index("tm_2"), lax.axis_index(axis)
    work, (send, recv, twin_send, twin_recv) = refs[:8], refs[8:]
    me = lax.axis_index(mine)
    zu, zd, zo = lax.rem(z + 1, 4), lax.rem(z + 3, 4), lax.rem(z + 2, 4)
    au, ad, ao = lax.rem(a + 1, 4), lax.rem(a + 3, 4), lax.rem(a + 2, 4)
    up, down = {axis: au}, {axis: ad}
    above, below, twin = {"state": zu}, {"state": zd}, {"tm_2": 1 - c}
    peers = [up, down, above, below, twin]
    barrier = pltpu.get_barrier_semaphore()
    for peer in peers:
        pl.semaphore_signal(barrier, inc=1, device_id=peer, device_id_type=MESH)
    quarters = (z, zu)
    coming = (zd, zo)
    load = chosen(me, own, from_slots(others))

    def run(part):
        base, pieces = N if part else 0, PIECES[part]
        span = pl.ds(base, 4 * QUARTER[part])
        if part:
            split_gains(4, load, work)
            spreads(4, me, load, total, rest, work)
        else:
            gains(4, me, load, total, rest, work)
        pl.semaphore_wait(barrier, len(peers))
        cp = Copies(out, send, recv)

        def hand(src, dst, sem):
            copy = remote(src, dst, twin_send.at[sem], twin_recv.at[sem], twin)
            copy.start()

        def row_of(quarter, j):
            return pl.multiple_of(base + quarter * QUARTER[part] + pieces[j][0], 8)

        count = len(pieces)
        ups, downs, zs, tails = [], [], [], []
        for j in range(count):
            for k in (0, 1):
                for into, peer, jj in ((ups, up, j), (downs, down, count - 1 - j)):
                    row = row_of(quarters[k], jj)
                    n = cp.put(peer, a, row, pieces[jj][1], total.at[pl.ds(row, pieces[jj][1]), :])
                    into.append((n, k, jj, j < count // 2))
        hand(total.at[span], total.at[span], 0)
        hand(rest.at[span], rest.at[span], 1)

        def pass_on(slot, row, j):
            place = out.at[slot, pl.ds(row, pieces[j][1]), :]
            hand(place, place, 2)

        def spread(slot, k, j):
            row = row_of(quarters[k], j)
            zs.append((cp.put(below if k else above, slot, row, pieces[j][1]), slot, k, j))
            pass_on(slot, row, j)

        def take(keep):
            while len(zs) > keep:
                n, slot, k, j = zs.pop(0)
                row = row_of(coming[k], j)
                cp.arrived(n, slot, row, pieces[j][1])
                pass_on(slot, row, j)

        for pair in zip(ups, downs):
            for (n, k, j, further), slot, peer in zip(pair, (ad, au), (up, down)):
                row = row_of(quarters[k], j)
                cp.arrived(n, slot, row, pieces[j][1])
                if further:
                    tails.append((cp.put(peer, slot, row, pieces[j][1]), k, j))
                spread(slot, k, j)
        for n, k, j in tails:
            cp.arrived(n, ao, row_of(quarters[k], j), pieces[j][1])
            spread(ao, k, j)
            take(len(zs) - 2)
        take(0)
        cp.finish()
        other = pl.ds(0 if part else N, 4 * QUARTER[1 - part])
        for sem, ref in enumerate((total, rest)):
            remote(ref.at[span], ref.at[span], twin_send.at[sem], twin_recv.at[sem], twin).wait_send()
            remote(ref.at[other], ref.at[other], twin_send.at[sem], twin_recv.at[sem], twin).wait_recv()
        sent, came = out.at[0:3, span], out.at[0:3, other]
        remote(sent, sent, twin_send.at[2], twin_recv.at[2], twin).wait_send()
        remote(came, came, twin_send.at[2], twin_recv.at[2], twin).wait_recv()

    for part in (0, 1):
        pl.when(c == part)(partial(run, part))


def shape(*dims, dtype=F32):
    return jax.ShapeDtypeStruct(dims, dtype)


def params(limit=None, **more):
    return pltpu.CompilerParams(vmem_limit_bytes=limit, **more)


DMA = pltpu.SemaphoreType.DMA


def comm(kernel, name, collective_id, outs, scratch, *args, limit, in_spec=ANY, out_spec=ANY):
    return pl.pallas_call(
        kernel,
        name=name,
        out_shape=outs,
        in_specs=[in_spec] * len(args),
        out_specs=jax.tree.map(lambda _: out_spec, outs),
        scratch_shapes=scratch,
        compiler_params=pltpu.CompilerParams(
            collective_id=collective_id, has_side_effects=True, vmem_limit_bytes=limit
        ),
    )(*args)


def suffix_work(count):
    return [
        pltpu.VMEM((2, N, N), F32),
        pltpu.VMEM((2, N, N), F32),
        pltpu.VMEM((2, 8, N), F32),
        pltpu.VMEM((N, N), BF16),
        pltpu.VMEM((N, N), BF16),
        pltpu.VMEM((count - 1, N, N), BF16),
        pltpu.VMEM((count - 1, N, N), BF16),
        pltpu.VMEM((N, N), F32),
    ]


def ring(name, collective_id, mine, axis, own, others):
    packet = shape(ROWS, N)
    return pl.pallas_call(
        partial(ring_kernel, mine, axis),
        name=name,
        out_shape=(packet, shape(4, ROWS, N), packet),
        in_specs=[VM, VM],
        out_specs=(VM, VM, VM),
        scratch_shapes=suffix_work(4) + [DMA((48,)), DMA((48,)), DMA((3,)), DMA((3,))],
        compiler_params=params(RING_LIMIT, collective_id=collective_id, has_side_effects=True),
    )(own, others)


RING_LIMIT = 24 * 1024 * 1024
FIRST_LIMIT = 4 * 1024 * 1024


def on_device(filtered_cov, filtered_mean, noise_var, trans_blocks, pattern):
    z = lax.axis_index("state")
    cov, twin_mean, mean_here, noise_here, blocks_here = comm(
        gather_step_kernel,
        "gather_step",
        0,
        (shape(4, B, N), shape(4, N), shape(4, N), shape(1, N), shape(4, 2, B, B)),
        [pltpu.VMEM((2, B, N), F32), DMA((4,)), DMA((4,)), DMA((2,)), DMA((2,)), DMA, DMA, DMA, DMA((3,))],
        filtered_cov,
        filtered_mean,
        noise_var.reshape(1, N),
        trans_blocks,
        limit=FIRST_LIMIT,
        out_spec=VM,
    )
    packet, packets = shape(ROWS, N), shape(4, ROWS, N)
    square = shape(N, N)
    predicted = pl.pallas_call(
        predict_kernel,
        name="predict",
        out_shape=(square, square, square, shape(16, N)),
        in_specs=[SM] + [VM] * 5,
        out_specs=(VM, VM, VM, VM),
        compiler_params=params(RING_LIMIT),
    )(pattern, cov, mean_here, twin_mean, noise_here, blocks_here)
    own, pair, pairs = pl.pallas_call(
        pair_kernel,
        name="pair",
        out_shape=(packet, packet, packets),
        in_specs=[VM] * 4,
        out_specs=(VM, VM, VM),
        scratch_shapes=[pltpu.VMEM((ROWS, N), F32)]
        + [pltpu.VMEM((N, N), F32)] * 2
        + [pltpu.VMEM((B, B), F32)]
        + suffix_work(2)
        + [DMA((2,)), DMA((2,)), DMA((48,)), DMA((48,))],
        compiler_params=params(RING_LIMIT, collective_id=2, has_side_effects=True),
    )(*predicted)
    down, columns, column = ring("ring_x", 3, "state", "tm_1", pair, pairs)
    across, rows, row = ring("ring_y", 4, "tm_1", "tm_0", column, columns)
    half = pltpu.VMEM((N, N), BF16)
    smooth_cov, means = pl.pallas_call(
        final_kernel,
        name="final",
        out_shape=(shape(4, B, N), shape(4, 8, N)),
        in_specs=[VM] * 6,
        out_specs=(VM, VM),
        scratch_shapes=[pltpu.VMEM((N, N), F32), pltpu.VMEM((8, N), F32), pltpu.VMEM((8, N), F32), pltpu.VMEM((B, N), F32)]
        + [pltpu.VMEM((N, N), F32), pltpu.VMEM((8, N), F32), half, half, half, half, pltpu.VMEM((N, N), F32)]
        + [DMA((4,)), DMA((4,)), DMA((2,)), DMA, DMA((2,)), DMA((4,)), DMA((4,))],
        compiler_params=params(RING_LIMIT, collective_id=5, has_side_effects=True),
    )(row, rows, across, down, pair, own)
    return lax.dynamic_slice_in_dim(means[:, 0, :], z * B, B, 1), smooth_cov


def solution(mesh):
    torus = Mesh(
        mesh.devices.reshape(4, 4, 2, mesh.shape["state"]), ("tm_0", "tm_1", "tm_2", "state")
    )
    return jax.shard_map(
        on_device,
        mesh=torus,
        in_specs=(P(TM, "state", None), P(TM, None), P(), P(), P()),
        out_specs=(P(TM, "state"), P(TM, "state", None)),
        check_vma=False,
    )
```
